128 devices in a mesh: req: 16 (over y, z), head: 8 (over x, core).
Axes of the slice: x: 4, y: 4, z: 4, core: 2. Of those that a mesh axis runs over, the one named last changes fastest.
Arguments:
- queries: bfloat16 [1536, 128, 576], P('req', 'head'), may hold values from -16 to 16
- out_grad: bfloat16 [1536, 128, 512], P('req', 'head'), may hold values from -96 to 96
- latents: bfloat16 [256, 128, 576], P('req', 'head'), may hold values from -4 to 4
- list_blocks: int32 [16, 16], replicated, may hold values from 0 to 255, as said below
- list_counts: int32 [16], replicated, may hold values from 8 to 16
- valid_tokens: int32 [256], replicated, may hold values from 32 to 128
Outputs:
- attended: bfloat16 [1536, 128, 512], P('req', 'head')
- query_grad: bfloat16 [1536, 128, 576], P('req', 'head')
- latent_grad: float32 [256, 128, 576], P('req', 'head')
The draws below stay inside these ranges and needn't reach their ends.
Inputs may be any that keep to these rules, and one draw needn't show every extreme that they name: `list_blocks`: each row holds 16 distinct block numbers. Group g reads its first list_counts[g] entries, and among them at most 2 are owned by one req index, the owner of block b being b // 16; some group reaches 2 in every draw.
All inputs are finite; a program needn't handle non-finite values.
Results may differ from the reference program's by a relative error of at most 0.017.
Values may be sent and summed in bfloat16 or wider, within the bound.
No kernel may reach another device: no remote copies, remote signals or barrier semaphores. Data moves between devices by JAX's collectives and lax.ppermute only.
A program may use at most 64 MiB of HBM per device.

```python
import jax
import jax.numpy as jnp
from jax import lax

HEADS = 128
LAT = 512
ROPE = 64
WIDE = 576
BLOCK = 128
MAXL = 16
CAP = 2
Q_GRP = 96
BLK_DEV = 16
GROUPS = 16
NBLK = 256


def make_lists(key):
    base_key = jax.random.fold_in(key, 7001)
    owner_key, local_key, order_key = jax.random.split(base_key, 3)
    pair_count = MAXL // CAP
    owner_perm = jax.vmap(lambda subkey: jax.random.permutation(subkey, GROUPS))(jax.random.split(owner_key, GROUPS))
    row_ids = jnp.arange(GROUPS)[:, None]
    owner_target = jnp.where(row_ids == 1, GROUPS - 1, 0)
    owner_shift = jnp.where(row_ids < 2, owner_target - owner_perm[:, :1], 0)
    owner_perm = (owner_perm + owner_shift + GROUPS) % GROUPS
    owners = owner_perm[:, :pair_count]
    local_perm = jax.vmap(lambda subkey: jax.random.permutation(subkey, BLK_DEV))(jax.random.split(local_key, GROUPS * pair_count))
    pair_ids = jnp.arange(GROUPS * pair_count)[:, None]
    local_target = jnp.where(pair_ids == pair_count, BLK_DEV - 1, 0)
    fixed_pair = (pair_ids == 0) | (pair_ids == pair_count)
    local_shift = jnp.where(fixed_pair, local_target - local_perm[:, :1], 0)
    local_perm = (local_perm + local_shift + BLK_DEV) % BLK_DEV
    local_pick = local_perm[:, :CAP].reshape(GROUPS, MAXL)
    owner_repeat = jnp.repeat(owners, CAP, axis=1)
    block_ids = owner_repeat * BLK_DEV + local_pick
    entry_order = jax.vmap(lambda subkey: jax.random.permutation(subkey, MAXL))(jax.random.split(order_key, GROUPS))
    return jnp.take_along_axis(block_ids, entry_order, axis=1).astype(jnp.int32)


def make_latents(key):
    base_key = jax.random.fold_in(key, 7004)
    value_key = jax.random.fold_in(base_key, 0)
    shape = (NBLK, BLOCK, WIDE)
    latent_vals = jnp.clip(jax.random.normal(value_key, shape, jnp.float32), -4.0, 4.0)
    return latent_vals


def draw_list_blocks(key, part):
    return make_lists(key)


def draw_list_counts(key, part):
    base_key = jax.random.fold_in(key, 7002)
    first_key, pick_key = jax.random.split(base_key)
    counts = jax.random.randint(first_key, (GROUPS,), MAXL // 2, MAXL + 1)
    longest = jax.random.randint(pick_key, (), 0, GROUPS)
    return jnp.where(jnp.arange(GROUPS) == longest, MAXL, counts).astype(jnp.int32)


def draw_valid_tokens(key, part):
    base_key = jax.random.fold_in(key, 7003)
    first_key, full_key, short_key = jax.random.split(base_key, 3)
    counts = jax.random.randint(first_key, (NBLK,), BLOCK // 4, BLOCK + 1)
    full_at = jax.random.randint(full_key, (), 0, NBLK)
    short_at = (full_at + jax.random.randint(short_key, (), 1, NBLK)) % NBLK
    positions = jnp.arange(NBLK)
    counts = jnp.where(positions == full_at, BLOCK, counts)
    counts = jnp.where(positions == short_at, BLOCK // 4, counts)
    return counts.astype(jnp.int32)


def draw_latents(key, part):
    return make_latents(key).astype(jnp.bfloat16)


def draw_queries(key, part):
    base_key = jax.random.fold_in(key, 7005)
    value_key = jax.random.fold_in(base_key, 0)
    shape = (GROUPS * Q_GRP, HEADS, WIDE)
    query_vals = jnp.clip(jax.random.normal(value_key, shape, jnp.float32), -8.0, 8.0)
    return query_vals.astype(jnp.bfloat16)


def block_levels(stream_key, shape, cuts, least, high):
    level, own = 1.0, jax.random.fold_in(stream_key, 6)
    for position, blocks in cuts:
        steps = jnp.exp(jax.random.uniform(jax.random.fold_in(own, position), (blocks,), jnp.float32, least / len(cuts), high / len(cuts)))
        level = level * jnp.repeat(steps, shape[position] // blocks).reshape([-1 if axis == position else 1 for axis in range(len(shape))])
    return level


def scatter_about(key, shape, scale, bound, cuts=(), kind=jnp.bfloat16):
    factor_of = block_levels(key, shape, cuts, -0.22, 0.18) if cuts else 1.0
    values = jax.random.normal(key, shape, jnp.float32) * scale * factor_of
    return jnp.minimum(jnp.maximum(values, -bound), bound).astype(kind)


def setup_inputs(seed: int = 0) -> dict:
    keys = jax.random.split(jax.random.key(seed), 7)
    queries = draw_queries(jax.random.fold_in(keys[6], 71), 0)
    out_grad = scatter_about(keys[1], (GROUPS * Q_GRP, HEADS, LAT), 16.0, 96.0, ((0, 16), (1, 8)))
    latents = draw_latents(jax.random.fold_in(keys[6], 71), 0)
    list_blocks = draw_list_blocks(jax.random.fold_in(keys[6], 71), 0)
    list_counts = draw_list_counts(jax.random.fold_in(keys[6], 71), 0)
    valid_tokens = draw_valid_tokens(jax.random.fold_in(keys[6], 71), 0)
    return dict(queries=queries, out_grad=out_grad, latents=latents, list_blocks=list_blocks, list_counts=list_counts, valid_tokens=valid_tokens)


softmax_scale = 192.0 ** -0.5


def attend(query_rows, cotangent, key_rows, live_keys):
    scores = jnp.dot(query_rows, key_rows.T, preferred_element_type=jnp.float32) * softmax_scale
    scores = jnp.where(live_keys[None, :], scores, -jnp.inf)
    row_max = jnp.max(scores, axis=1, keepdims=True)
    exponent = jnp.exp(scores - row_max)
    row_sum = jnp.sum(exponent, axis=1, keepdims=True)
    weights = (exponent / row_sum).astype(jnp.bfloat16)
    values = key_rows[:, :LAT]
    output = jnp.dot(weights, values, preferred_element_type=jnp.float32).astype(jnp.bfloat16)
    weight_grads = jnp.dot(cotangent, values.T, preferred_element_type=jnp.float32)
    row_dot = jnp.sum(cotangent.astype(jnp.float32) * output.astype(jnp.float32), axis=1, keepdims=True)
    score_grads = (weights.astype(jnp.float32) * (weight_grads - row_dot) * softmax_scale).astype(jnp.bfloat16)
    query_grad = jnp.dot(score_grads, key_rows, preferred_element_type=jnp.float32).astype(jnp.bfloat16)
    key_grads = jnp.dot(score_grads.T, query_rows, preferred_element_type=jnp.float32)
    value_grads = jnp.dot(weights.T, cotangent, preferred_element_type=jnp.float32)
    key_grads = key_grads + jnp.pad(value_grads, ((0, 0), (0, ROPE)))
    return output, query_grad, key_grads


def reference(queries, out_grad, latents, list_blocks, list_counts, valid_tokens):
    query_groups = queries.reshape(GROUPS, Q_GRP, HEADS, WIDE)
    cotangent_groups = out_grad.reshape(GROUPS, Q_GRP, HEADS, LAT)
    token_pos = jnp.arange(BLOCK, dtype=jnp.int32)
    slot_pos = jnp.arange(MAXL, dtype=jnp.int32)

    def one_group(grad_sum, inputs):
        group_query, cotangent, blocks, listed_count = inputs
        key_rows = latents[blocks].reshape(MAXL * BLOCK, WIDE)
        filled = valid_tokens[blocks]
        live_keys = ((slot_pos < listed_count)[:, None] & (token_pos[None, :] < filled[:, None])).reshape(-1)
        output, query_grad, key_grads = attend(group_query.reshape(-1, WIDE), cotangent.reshape(-1, LAT), key_rows, live_keys)
        grad_sum = grad_sum.at[blocks].add(key_grads.reshape(MAXL, BLOCK, WIDE))
        return grad_sum, (output.reshape(Q_GRP, HEADS, LAT), query_grad.reshape(Q_GRP, HEADS, WIDE))

    zero_grads = jnp.zeros((NBLK, BLOCK, WIDE), jnp.float32)
    latent_grad, (outputs, query_grads) = lax.scan(one_group, zero_grads, (query_groups, cotangent_groups, list_blocks, list_counts))
    attended = outputs.reshape(GROUPS * Q_GRP, HEADS, LAT)
    query_grad = query_grads.reshape(GROUPS * Q_GRP, HEADS, WIDE)
    return attended, query_grad, latent_grad
```

```python
import functools
import math

import jax
import jax.numpy as jnp
from jax import lax
from jax.experimental import pallas as pl
from jax.experimental.pallas import tpu as pltpu
from jax.sharding import PartitionSpec as P

LAT = 512
WIDE = 576
BLOCK = 128
MAXL = 16
CAP = 2
BIG = -1e30
SCALE = 192.0 ** (-0.5)
EXPC = SCALE * math.log2(math.e)
NT = (((1,), (1,)), ((), ()))
NN = (((1,), (0,)), ((), ()))
f32 = jnp.float32
bf16 = jnp.bfloat16


def dot(a, b, dims=NN):
    return lax.dot_general(a, b, dims, preferred_element_type=f32)


def whole(shape):
    rank = len(shape)
    return pl.BlockSpec(shape, lambda *_: (0,) * rank)


def pick_body(lists, counts, me, lat_ref, out_ref):
    own = me[0]

    def group(g, carry):
        def entry(j, rank):
            block = lists[g, j]
            mine = (block // MAXL) == own

            @pl.when(mine)
            def _():
                out_ref[g * CAP + jnp.minimum(rank, CAP - 1)] = lat_ref[lax.rem(block, MAXL)]

            return rank + mine.astype(jnp.int32)

        lax.fori_loop(0, counts[g], entry, jnp.int32(0))
        return carry

    lax.fori_loop(0, 16, group, 0)


def slots_of(lists, counts, me, seen, visit):
    own = me[0]

    def clear(o, carry):
        seen[o] = 0
        return carry

    lax.fori_loop(0, 16, clear, 0)

    def entry(j, carry):
        owner = lists[own, j] // MAXL
        rank = seen[owner]
        seen[owner] = rank + 1
        visit(j, owner * CAP + jnp.minimum(rank, CAP - 1))
        return carry

    lax.fori_loop(0, counts[own], entry, 0)


def take_body(lists, counts, me, arrived_ref, out_ref, seen):
    def visit(j, slot):
        out_ref[j] = arrived_ref[slot]

    slots_of(lists, counts, me, seen, visit)

    def blank(j, carry):
        out_ref[j] = jnp.zeros(out_ref.shape[1:], out_ref.dtype)
        return carry

    lax.fori_loop(counts[me[0]], MAXL, blank, 0)


def put_body(lists, counts, me, a_ref, b_ref, c_ref, d_ref, out_ref, seen):
    def visit(j, slot):
        total = a_ref[j].astype(f32) + b_ref[j].astype(f32)
        total = total + c_ref[j].astype(f32) + d_ref[j].astype(f32)
        out_ref[slot] = total.astype(out_ref.dtype)

    slots_of(lists, counts, me, seen, visit)


def gather_body(lists, counts, me, arrived_ref, out_ref):
    own = me[0]
    out_ref[...] = jnp.zeros(out_ref.shape, out_ref.dtype)

    def group(g, carry):
        def entry(j, rank):
            block = lists[g, j]
            mine = (block // MAXL) == own

            @pl.when(mine)
            def _():
                at = lax.rem(block, MAXL)
                out_ref[at] = out_ref[at] + arrived_ref[g * CAP + jnp.minimum(rank, CAP - 1)].astype(f32)

            return rank + mine.astype(jnp.int32)

        lax.fori_loop(0, counts[g], entry, jnp.int32(0))
        return carry

    lax.fori_loop(0, 16, group, 0)


def listed_call(body, out_shape, scalars, *arrays, scratch=()):
    return pl.pallas_call(
        body,
        grid_spec=pltpu.PrefetchScalarGridSpec(
            num_scalar_prefetch=3,
            grid=(1,),
            in_specs=[whole(a.shape) for a in arrays],
            out_specs=whole(out_shape.shape),
            scratch_shapes=list(scratch),
        ),
        out_shape=out_shape,
    )(*scalars, *arrays)


def forward_body(nkeys, first, last, *refs):
    refs = list(refs)
    key_refs = [refs.pop(0) for _ in range(nkeys)]
    bias, q_ref, g_ref = refs[:3]
    refs = refs[3:]
    if not first:
        m_in, l_in, r_in, o_in = refs[:4]
        refs = refs[4:]
    e_out, p_out, m_out, l_out, r_out, o_out, keys = refs

    @pl.when(pl.program_id(0) == 0)
    def _():
        at = 0
        for ref in key_refs:
            keys[at : at + ref.shape[0]] = ref[...]
            at += ref.shape[0]

    rows = q_ref.shape[0]
    scores = dot(q_ref[...], keys[...], NT) + bias[...]
    top = jnp.max(scores, axis=1, keepdims=True)
    if not first:
        m_old = m_in[:, :1]
        top = jnp.maximum(top, m_old)
    expo = jnp.exp2((scores - top) * EXPC)
    values = keys[:, :LAT]
    grads = dot(g_ref[...], values, NT)
    total = jnp.sum(expo, axis=1, keepdims=True)
    rdot = jnp.sum(expo * grads, axis=1, keepdims=True)
    expo = expo.astype(bf16)
    e_out[...] = expo
    p_out[...] = grads.astype(bf16)
    attended = dot(expo, values)
    if not first:
        fade = jnp.exp2((m_old - top) * EXPC)
        total = total + fade * l_in[:, :1]
        rdot = rdot + fade * r_in[:, :1]
        attended = attended + fade * o_in[...]
    if last:
        total = 1.0 / total
        rdot = rdot * total
        attended = attended * total
    m_out[...] = jnp.broadcast_to(top, (rows, 128))
    l_out[...] = jnp.broadcast_to(total, (rows, 128))
    r_out[...] = jnp.broadcast_to(rdot, (rows, 128))
    o_out[...] = attended.astype(o_out.dtype)


def forward(key_parts, bias, q, g, state, last, block=256):
    n = bias.shape[1]
    rows = q.shape[0]
    first = state is None
    by_row = lambda width: pl.BlockSpec((block, width), lambda i: (i, 0))
    in_specs = [whole(k.shape) for k in key_parts] + [whole((1, n)), by_row(WIDE), by_row(LAT)]
    args = [*key_parts, bias, q, g]
    if not first:
        in_specs += [by_row(128)] * 3 + [by_row(LAT)]
        args += list(state)
    stat = jax.ShapeDtypeStruct((rows, 128), f32)
    side = jax.ShapeDtypeStruct((rows, n), bf16)
    out_shape = (side, side, stat, stat, stat, jax.ShapeDtypeStruct((rows, LAT), bf16 if last else f32))
    return pl.pallas_call(
        functools.partial(forward_body, len(key_parts), first, last),
        grid=(rows // block,),
        in_specs=in_specs,
        out_specs=(by_row(n), by_row(n), by_row(128), by_row(128), by_row(128), by_row(LAT)),
        out_shape=out_shape,
        scratch_shapes=[pltpu.VMEM((n, WIDE), bf16)],
        cost_estimate=pl.CostEstimate(
            flops=2 * rows * n * (WIDE + 2 * LAT), transcendentals=rows * n, bytes_accessed=8 * rows * n
        ),
    )(*args)


def backward_body(half, step, qt_ref, gt_ref, e_ref, p_ref, mc_ref, m_ref, l_ref, r_ref, far_out, near_out, s_out, a_sc, r_sc):
    i = pl.program_id(0)
    rows = qt_ref.shape[1]

    @pl.when(i == 0)
    def _():
        a_sc[...] = jnp.exp2((mc_ref[...] - m_ref[...]) * EXPC) * l_ref[...]
        r_sc[...] = r_ref[...]

    width = e_ref.shape[1]
    acc = None
    for at in range(0, rows, step):
        here = slice(at, at + step)
        a = jnp.tile(a_sc[here], (1, width // 128))
        r = jnp.tile(r_sc[here], (1, width // 128))
        weights = (e_ref[here].astype(f32) * a).astype(bf16)
        sg = (weights.astype(f32) * (p_ref[here].astype(f32) - r) * SCALE).astype(bf16)
        s_out[here] = sg
        key_part = dot(qt_ref[:, here], sg)
        value_part = dot(gt_ref[:, here], weights)
        if acc is None:
            acc = [key_part[:LAT] + value_part, key_part[LAT:]]
        else:
            acc = [acc[0] + (key_part[:LAT] + value_part), acc[1] + key_part[LAT:]]
    top = acc[0].T.astype(bf16)
    low = jnp.concatenate([acc[1], jnp.zeros_like(acc[1])], axis=0).T[:, : WIDE - LAT].astype(bf16)

    def write(ref):
        ref[:, :LAT] = top
        ref[:, LAT:] = low

    @pl.when(i < half)
    def _():
        write(far_out)

    @pl.when(i >= half)
    def _():
        write(near_out)


def backward(qt, gt, e, p, mc, m, linv, r, tile=256):
    rows, n = e.shape
    steps = n // tile
    half = steps // 2
    where = lambda i: lax.rem(i + half, steps)
    part = jax.ShapeDtypeStruct((n // 2, WIDE), bf16)
    by_key = pl.BlockSpec((rows, tile), lambda i: (0, where(i)))
    stat = whole((rows, 128))
    return pl.pallas_call(
        functools.partial(backward_body, half, 256),
        grid=(steps,),
        in_specs=[whole(qt.shape), whole(gt.shape), by_key, by_key, stat, stat, stat, stat],
        out_specs=(
            pl.BlockSpec((tile, WIDE), lambda i: (jnp.minimum(i, half - 1), 0)),
            pl.BlockSpec((tile, WIDE), lambda i: (jnp.maximum(i - half, 0), 0)),
            by_key,
        ),
        out_shape=(part, part, jax.ShapeDtypeStruct((rows, n), bf16)),
        scratch_shapes=[pltpu.VMEM((rows, 128), f32)] * 2,
        cost_estimate=pl.CostEstimate(
            flops=2 * rows * n * (WIDE + LAT), transcendentals=0, bytes_accessed=6 * rows * n
        ),
    )(qt, gt, e, p, mc, m, linv, r)


def query_body(counts, *refs):
    refs = list(refs)
    chunks = len(counts)
    s_refs = [refs.pop(0) for _ in range(chunks)]
    k_refs = [[refs.pop(0) for _ in range(c)] for c in counts]
    out_ref, keys = refs

    @pl.when(pl.program_id(0) == 0)
    def _():
        at = 0
        for ref in sum(k_refs, []):
            keys[at : at + ref.shape[0]] = ref[...]
            at += ref.shape[0]

    total = None
    at = 0
    for ref in s_refs:
        n = ref.shape[1]
        piece = dot(ref[...], keys[at : at + n])
        total = piece if total is None else total + piece
        at += n
    out_ref[...] = total.astype(out_ref.dtype)


def query_side(sgs, parts, block=256):
    rows = sgs[0].shape[0]
    n = sum(s.shape[1] for s in sgs)
    flat = sum(parts, [])
    return pl.pallas_call(
        functools.partial(query_body, [len(p) for p in parts]),
        grid=(rows // block,),
        in_specs=[pl.BlockSpec((block, s.shape[1]), lambda i: (i, 0)) for s in sgs] + [whole(k.shape) for k in flat],
        out_specs=pl.BlockSpec((block, WIDE), lambda i: (i, 0)),
        out_shape=jax.ShapeDtypeStruct((rows, WIDE), bf16),
        scratch_shapes=[pltpu.VMEM((n, WIDE), bf16)],
        cost_estimate=pl.CostEstimate(flops=2 * rows * n * WIDE, transcendentals=0, bytes_accessed=2 * rows * n),
    )(*sgs, *flat)


def per_device(queries, out_grad, latents, list_blocks, list_counts, valid_tokens):
    me = lax.axis_index("req")
    head = lax.axis_index("head")
    chip, core = head // 2, head % 2
    tokens = latents.shape[1]
    shift = lambda d: [(x * 2 + c, ((x + d) % 4) * 2 + c) for x in range(4) for c in range(2)]
    right, left, sibling = shift(1), shift(-1), [(h, h ^ 1) for h in range(8)]
    send = lambda a, perm: lax.ppermute(a, "head", perm)
    scalars = (list_blocks, list_counts, me.reshape(1).astype(jnp.int32))

    slots = jax.ShapeDtypeStruct((16 * CAP, tokens, WIDE), bf16)
    outgoing = listed_call(pick_body, slots, scalars, latents)
    arrived = lax.all_to_all(outgoing.reshape(16, CAP, tokens, WIDE), "req", 0, 0, tiled=True)
    share = listed_call(
        take_body,
        jax.ShapeDtypeStruct((MAXL, tokens, WIDE), bf16),
        scalars,
        arrived.reshape(slots.shape),
        scratch=[pltpu.SMEM((16,), jnp.int32)],
    ).reshape(MAXL * tokens, WIDE)

    my_blocks = lax.dynamic_index_in_dim(list_blocks, me, 0, keepdims=False)
    my_count = lax.dynamic_index_in_dim(list_counts, me, 0, keepdims=False)
    ids = jnp.arange(valid_tokens.shape[0], dtype=jnp.int32)
    filled = jnp.sum(jnp.where(my_blocks[:, None] == ids[None, :], valid_tokens[None, :], 0), axis=1)
    filled = jnp.where(jnp.arange(MAXL, dtype=jnp.int32) < my_count, filled, 0)
    filled = jnp.repeat(filled, tokens)
    offset = jnp.tile(jnp.arange(tokens, dtype=jnp.int32), MAXL)

    def bias_of(places):
        rows = [jnp.where(place * tokens + offset < filled, 0.0, BIG) for place in places]
        return jnp.concatenate(rows).astype(f32)[None, :]

    at = lambda d, c: ((chip + d) % 4) * 2 + c
    other = 1 - core
    bias0 = bias_of([at(0, core), at(0, other)])
    bias1 = bias_of([at(3, core), at(1, core), at(3, other), at(1, other)])
    bias2 = bias_of([at(2, core), at(2, other)])

    q = queries.reshape(-1, WIDE)
    g = out_grad.reshape(-1, LAT)
    qt = q.T
    gt = g.T

    keep = MAXL * tokens // 2
    r1 = send(share, right)
    l1 = send(share, left)
    s0 = send(share, sibling)
    r2 = send(r1[:keep], right)
    l2 = send(l1[keep:], left)
    s1 = send(r1, sibling)
    s2 = send(l1, sibling)
    s3 = send(r2, sibling)
    s4 = send(l2, sibling)
    parts0, parts1, parts2 = [share, s0], [r1, l1, s1, s2], [r2, l2, s3, s4]

    e0, p0, m0, *rest = forward(parts0, bias0, q, g, None, False)
    e1, p1, m1, *rest = forward(parts1, bias1, q, g, (m0, *rest), False)
    e2, p2, m2, linv, rdot, attended = forward(parts2, bias2, q, g, (m1, *rest), True)

    back = functools.partial(backward, qt, gt)
    add = lambda a, b: (a.astype(f32) + b.astype(f32)).astype(bf16)
    far, near, sg2 = back(e2, p2, m2, m2, linv, rdot)
    two = add(near, send(far, sibling))
    from_left = send(two[:keep], right)
    from_right = send(two[keep:], left)
    far, near, sg1 = back(e1, p1, m1, m2, linv, rdot)
    one = add(near, send(far, sibling))
    size = 2 * keep
    to_left = jnp.concatenate([one[:keep], add(one[keep:size], from_right)])
    to_right = jnp.concatenate([add(one[size : size + keep], from_left), one[size + keep :]])
    got_left = send(to_right, right)
    got_right = send(to_left, left)
    far, near, sg0 = back(e0, p0, m0, m2, linv, rdot)
    mate = send(far, sibling)
    fold = lambda a: a.reshape(MAXL, tokens, WIDE)
    slot_grads = listed_call(
        put_body,
        slots,
        scalars,
        fold(near),
        fold(mate),
        fold(got_left),
        fold(got_right),
        scratch=[pltpu.SMEM((16,), jnp.int32)],
    )
    returned = lax.all_to_all(slot_grads.reshape(16, CAP, tokens, WIDE), "req", 0, 0, tiled=True)
    query_grad = query_side([sg2, sg1, sg0], [parts2, parts1, parts0])
    latent_grad = listed_call(
        gather_body, jax.ShapeDtypeStruct((16, tokens, WIDE), f32), scalars, returned.reshape(slots.shape)
    )
    return (attended.reshape(out_grad.shape), query_grad.reshape(queries.shape), latent_grad)


def solution(mesh):
    in_specs = (
        P("req", "head", None),
        P("req", "head", None),
        P("req", "head", None),
        P(),
        P(),
        P(),
    )
    out_specs = (P("req", "head", None), P("req", "head", None), P("req", "head", None))
    return jax.shard_map(
        per_device, mesh=mesh, in_specs=in_specs, out_specs=out_specs, check_vma=False
    )
```

```python
import functools
import math

import jax
import jax.numpy as jnp
from jax import lax
from jax.experimental import pallas as pl
from jax.experimental.pallas import tpu as pltpu
from jax.sharding import PartitionSpec as P

LAT = 512
WIDE = 576
BLOCK = 128
MAXL = 16
CAP = 2
BIG = -1e30
SCALE = 192.0 ** (-0.5)
EXPC = SCALE * math.log2(math.e)
NT = (((1,), (1,)), ((), ()))
NN = (((1,), (0,)), ((), ()))
f32 = jnp.float32
bf16 = jnp.bfloat16


def dot(a, b, dims=NN):
    return lax.dot_general(a, b, dims, preferred_element_type=f32)


def whole(shape):
    rank = len(shape)
    return pl.BlockSpec(shape, lambda *_: (0,) * rank)


def pick_body(lists, counts, me, lat_ref, out_ref):
    own = me[0]

    def group(g, carry):
        def entry(j, rank):
            block = lists[g, j]
            mine = (block // MAXL) == own

            @pl.when(mine)
            def _():
                out_ref[g * CAP + jnp.minimum(rank, CAP - 1)] = lat_ref[lax.rem(block, MAXL)]

            return rank + mine.astype(jnp.int32)

        lax.fori_loop(0, counts[g], entry, jnp.int32(0))
        return carry

    lax.fori_loop(0, 16, group, 0)


def slots_of(lists, counts, me, seen, visit):
    own = me[0]

    def clear(o, carry):
        seen[o] = 0
        return carry

    lax.fori_loop(0, 16, clear, 0)

    def entry(j, carry):
        owner = lists[own, j] // MAXL
        rank = seen[owner]
        seen[owner] = rank + 1
        visit(j, owner * CAP + jnp.minimum(rank, CAP - 1))
        return carry

    lax.fori_loop(0, counts[own], entry, 0)


def take_body(lists, counts, me, arrived_ref, out_ref, seen):
    def visit(j, slot):
        out_ref[j] = arrived_ref[slot]

    slots_of(lists, counts, me, seen, visit)

    def blank(j, carry):
        out_ref[j] = jnp.zeros(out_ref.shape[1:], out_ref.dtype)
        return carry

    lax.fori_loop(counts[me[0]], MAXL, blank, 0)


def put_body(lists, counts, me, a_ref, b_ref, c_ref, d_ref, out_ref, seen):
    def visit(j, slot):
        total = a_ref[j].astype(f32) + b_ref[j].astype(f32)
        total = total + c_ref[j].astype(f32) + d_ref[j].astype(f32)
        out_ref[slot] = total.astype(out_ref.dtype)

    slots_of(lists, counts, me, seen, visit)


def gather_body(lists, counts, me, arrived_ref, out_ref):
    own = me[0]
    out_ref[...] = jnp.zeros(out_ref.shape, out_ref.dtype)

    def group(g, carry):
        def entry(j, rank):
            block = lists[g, j]
            mine = (block // MAXL) == own

            @pl.when(mine)
            def _():
                at = lax.rem(block, MAXL)
                out_ref[at] = out_ref[at] + arrived_ref[g * CAP + jnp.minimum(rank, CAP - 1)].astype(f32)

            return rank + mine.astype(jnp.int32)

        lax.fori_loop(0, counts[g], entry, jnp.int32(0))
        return carry

    lax.fori_loop(0, 16, group, 0)


def on_chip(*arrays):
    return [pltpu.with_memory_space_constraint(a, pltpu.VMEM) for a in arrays]


def call(body, out_shape, scalars, *arrays, scratch=(), limit=24, cost=None):
    single = not isinstance(out_shape, tuple)
    outs = [pltpu.VMEM(o.shape, o.dtype) for o in ((out_shape,) if single else out_shape)]
    vmem = pl.BlockSpec(memory_space=pltpu.VMEM)
    return pl.pallas_call(
        body,
        in_specs=[pl.BlockSpec(memory_space=pltpu.SMEM)] * len(scalars) + [vmem] * len(arrays),
        out_specs=vmem if single else tuple(vmem for _ in outs),
        out_shape=outs[0] if single else tuple(outs),
        scratch_shapes=list(scratch),
        cost_estimate=cost,
        compiler_params=pltpu.CompilerParams(vmem_limit_bytes=limit * 1024 * 1024),
    )(*scalars, *on_chip(*arrays))


def load_keys(key_refs, keys):
    at = 0
    for ref in key_refs:
        keys[at : at + ref.shape[0]] = ref[...]
        at += ref.shape[0]


def forward_body(nkeys, first, last, block, *refs):
    refs = list(refs)
    key_refs = [refs.pop(0) for _ in range(nkeys)]
    bias, q_ref, g_ref = refs[:3]
    refs = refs[3:]
    if not first:
        m_in, l_in, r_in, o_in = refs[:4]
        refs = refs[4:]
    e_out, p_out, m_out, l_out, r_out, o_out, keys = refs
    load_keys(key_refs, keys)

    def rows(i, carry):
        here = pl.ds(pl.multiple_of(i * block, block), block)
        scores = dot(q_ref[here], keys[...], NT) + bias[...]
        top = jnp.max(scores, axis=1, keepdims=True)
        if not first:
            m_old = m_in[here, :1]
            top = jnp.maximum(top, m_old)
        expo = jnp.exp2((scores - top) * EXPC)
        values = keys[:, :LAT]
        grads = dot(g_ref[here], values, NT)
        total = jnp.sum(expo, axis=1, keepdims=True)
        rdot = jnp.sum(expo * grads, axis=1, keepdims=True)
        expo = expo.astype(bf16)
        e_out[here] = expo
        p_out[here] = grads.astype(bf16)
        attended = dot(expo, values)
        if not first:
            fade = jnp.exp2((m_old - top) * EXPC)
            total = total + fade * l_in[here, :1]
            rdot = rdot + fade * r_in[here, :1]
            attended = attended + fade * o_in[here]
        if last:
            total = 1.0 / total
            rdot = rdot * total
            attended = attended * total
        m_out[here] = jnp.broadcast_to(top, (block, 128))
        l_out[here] = jnp.broadcast_to(total, (block, 128))
        r_out[here] = jnp.broadcast_to(rdot, (block, 128))
        o_out[here] = attended.astype(o_out.dtype)
        return carry

    lax.fori_loop(0, q_ref.shape[0] // block, rows, 0)


def forward(key_parts, bias, q, g, state, last, block=256):
    n = bias.shape[1]
    rows = q.shape[0]
    first = state is None
    stat = jax.ShapeDtypeStruct((rows, 128), f32)
    side = jax.ShapeDtypeStruct((rows, n), bf16)
    return call(
        functools.partial(forward_body, len(key_parts), first, last, block),
        (side, side, stat, stat, stat, jax.ShapeDtypeStruct((rows, LAT), bf16 if last else f32)),
        (),
        *key_parts,
        bias,
        q,
        g,
        *(() if first else state),
        scratch=[pltpu.VMEM((n, WIDE), bf16)],
        cost=pl.CostEstimate(
            flops=2 * rows * n * (WIDE + 2 * LAT), transcendentals=rows * n, bytes_accessed=8 * rows * n
        ),
    )


def backward_body(step, tile, qt_ref, gt_ref, e_ref, p_ref, mc_ref, m_ref, l_ref, r_ref, far_out, near_out, s_out, a_sc):
    rows = qt_ref.shape[1]
    n = e_ref.shape[1]
    half = n // 2
    a_sc[...] = jnp.exp2((mc_ref[...] - m_ref[...]) * EXPC) * l_ref[...]
    for start in range(0, n, tile):
        cols = slice((start + half) % n, (start + half) % n + tile)
        acc = None
        for at in range(0, rows, step):
            here = slice(at, at + step)
            a = jnp.tile(a_sc[here], (1, tile // 128))
            r = jnp.tile(r_ref[here], (1, tile // 128))
            weights = (e_ref[here, cols].astype(f32) * a).astype(bf16)
            sg = (weights.astype(f32) * (p_ref[here, cols].astype(f32) - r) * SCALE).astype(bf16)
            s_out[here, cols] = sg
            key_part = dot(qt_ref[:, here], sg)
            value_part = dot(gt_ref[:, here], weights)
            if acc is None:
                acc = [key_part[:LAT] + value_part, key_part[LAT:]]
            else:
                acc = [acc[0] + (key_part[:LAT] + value_part), acc[1] + key_part[LAT:]]
        top = acc[0].T.astype(bf16)
        low = jnp.concatenate([acc[1], jnp.zeros_like(acc[1])], axis=0).T[:, : WIDE - LAT].astype(bf16)
        ref = far_out if start < half else near_out
        put = slice(start % half, start % half + tile)
        ref[put, :LAT] = top
        ref[put, LAT:] = low


def backward(qt, gt, e, p, mc, m, linv, r, tile=256, step=256):
    rows, n = e.shape
    part = jax.ShapeDtypeStruct((n // 2, WIDE), bf16)
    return call(
        functools.partial(backward_body, step, tile),
        (part, part, jax.ShapeDtypeStruct((rows, n), bf16)),
        (),
        qt,
        gt,
        e,
        p,
        mc,
        m,
        linv,
        r,
        scratch=[pltpu.VMEM((rows, 128), f32)],
        cost=pl.CostEstimate(flops=2 * rows * n * (WIDE + LAT), transcendentals=0, bytes_accessed=6 * rows * n),
    )


def query_body(counts, block, *refs):
    refs = list(refs)
    chunks = len(counts)
    s_refs = [refs.pop(0) for _ in range(chunks)]
    k_refs = [refs.pop(0) for _ in range(sum(counts))]
    out_ref, keys = refs
    load_keys(k_refs, keys)

    def rows(i, carry):
        here = pl.ds(pl.multiple_of(i * block, block), block)
        total = None
        at = 0
        for ref in s_refs:
            n = ref.shape[1]
            piece = dot(ref[here], keys[at : at + n])
            total = piece if total is None else total + piece
            at += n
        out_ref[here] = total.astype(out_ref.dtype)
        return carry

    lax.fori_loop(0, out_ref.shape[0] // block, rows, 0)


def query_side(sgs, parts, block=256):
    rows = sgs[0].shape[0]
    n = sum(s.shape[1] for s in sgs)
    return call(
        functools.partial(query_body, [len(p) for p in parts], block),
        jax.ShapeDtypeStruct((rows, WIDE), bf16),
        (),
        *sgs,
        *sum(parts, []),
        scratch=[pltpu.VMEM((n, WIDE), bf16)],
        cost=pl.CostEstimate(flops=2 * rows * n * WIDE, transcendentals=0, bytes_accessed=2 * rows * n),
    )


def per_device(queries, out_grad, latents, list_blocks, list_counts, valid_tokens):
    me = lax.axis_index("req")
    head = lax.axis_index("head")
    chip, core = head // 2, head % 2
    tokens = latents.shape[1]
    shift = lambda d: [(x * 2 + c, ((x + d) % 4) * 2 + c) for x in range(4) for c in range(2)]
    right, left, sibling = shift(1), shift(-1), [(h, h ^ 1) for h in range(8)]
    send = lambda a, perm: lax.ppermute(a, "head", perm)
    scalars = (list_blocks, list_counts, me.reshape(1).astype(jnp.int32))

    slots = jax.ShapeDtypeStruct((16 * CAP, tokens, WIDE), bf16)
    outgoing = call(pick_body, slots, scalars, latents)
    arrived = lax.all_to_all(outgoing.reshape(16, CAP, tokens, WIDE), "req", 0, 0, tiled=True)
    share = call(
        take_body,
        jax.ShapeDtypeStruct((MAXL, tokens, WIDE), bf16),
        scalars,
        arrived.reshape(slots.shape),
        scratch=[pltpu.SMEM((16,), jnp.int32)],
    ).reshape(MAXL * tokens, WIDE)

    my_blocks = lax.dynamic_index_in_dim(list_blocks, me, 0, keepdims=False)
    my_count = lax.dynamic_index_in_dim(list_counts, me, 0, keepdims=False)
    ids = jnp.arange(valid_tokens.shape[0], dtype=jnp.int32)
    filled = jnp.sum(jnp.where(my_blocks[:, None] == ids[None, :], valid_tokens[None, :], 0), axis=1)
    filled = jnp.where(jnp.arange(MAXL, dtype=jnp.int32) < my_count, filled, 0)
    filled = jnp.repeat(filled, tokens)
    offset = jnp.tile(jnp.arange(tokens, dtype=jnp.int32), MAXL)

    def bias_of(places):
        rows = [jnp.where(place * tokens + offset < filled, 0.0, BIG) for place in places]
        return jnp.concatenate(rows).astype(f32)[None, :]

    at = lambda d, c: ((chip + d) % 4) * 2 + c
    other = 1 - core
    bias0 = bias_of([at(0, core), at(0, other)])
    bias1 = bias_of([at(3, core), at(1, core), at(3, other), at(1, other)])
    bias2 = bias_of([at(2, core), at(2, other)])

    q = queries.reshape(-1, WIDE)
    g = out_grad.reshape(-1, LAT)
    qt = q.T
    gt = g.T

    keep = MAXL * tokens // 2
    r1 = send(share, right)
    l1 = send(share, left)
    s0 = send(share, sibling)
    r2 = send(r1[:keep], right)
    l2 = send(l1[keep:], left)
    s1 = send(r1, sibling)
    s2 = send(l1, sibling)
    s3 = send(r2, sibling)
    s4 = send(l2, sibling)
    parts0, parts1, parts2 = [share, s0], [r1, l1, s1, s2], [r2, l2, s3, s4]

    e0, p0, m0, *rest = forward(parts0, bias0, q, g, None, False)
    e1, p1, m1, *rest = forward(parts1, bias1, q, g, (m0, *rest), False)
    e2, p2, m2, linv, rdot, attended = forward(parts2, bias2, q, g, (m1, *rest), True)

    back = functools.partial(backward, qt, gt)
    add = lambda a, b: (a.astype(f32) + b.astype(f32)).astype(bf16)
    far, near, sg2 = back(e2, p2, m2, m2, linv, rdot)
    two = add(near, send(far, sibling))
    from_left = send(two[:keep], right)
    from_right = send(two[keep:], left)
    far, near, sg1 = back(e1, p1, m1, m2, linv, rdot)
    one = add(near, send(far, sibling))
    size = 2 * keep
    to_left = jnp.concatenate([one[:keep], add(one[keep:size], from_right)])
    to_right = jnp.concatenate([add(one[size : size + keep], from_left), one[size + keep :]])
    got_left = send(to_right, right)
    got_right = send(to_left, left)
    far, near, sg0 = back(e0, p0, m0, m2, linv, rdot)
    mate = send(far, sibling)
    fold = lambda a: a.reshape(MAXL, tokens, WIDE)
    slot_grads = call(
        put_body,
        slots,
        scalars,
        fold(near),
        fold(mate),
        fold(got_left),
        fold(got_right),
        scratch=[pltpu.SMEM((16,), jnp.int32)],
    )
    returned = lax.all_to_all(slot_grads.reshape(16, CAP, tokens, WIDE), "req", 0, 0, tiled=True)
    query_grad = query_side([sg2, sg1, sg0], [parts2, parts1, parts0])
    latent_grad = call(
        gather_body, jax.ShapeDtypeStruct((16, tokens, WIDE), f32), scalars, returned.reshape(slots.shape)
    )
    return (attended.reshape(out_grad.shape), query_grad.reshape(queries.shape), latent_grad)


def solution(mesh):
    in_specs = (
        P("req", "head", None),
        P("req", "head", None),
        P("req", "head", None),
        P(),
        P(),
        P(),
    )
    out_specs = (P("req", "head", None), P("req", "head", None), P("req", "head", None))
    return jax.shard_map(
        per_device, mesh=mesh, in_specs=in_specs, out_specs=out_specs, check_vma=False
    )
```

```python
import functools
import math

import jax
import jax.numpy as jnp
from jax import lax
from jax.experimental import pallas as pl
from jax.experimental.pallas import tpu as pltpu
from jax.sharding import PartitionSpec as P

LAT = 512
WIDE = 576
BLOCK = 128
MAXL = 16
CAP = 2
BIG = -1e30
SLOTS = 16 * CAP
SCALE = 192.0 ** (-0.5)
EXPC = SCALE * math.log2(math.e)
NT = (((1,), (1,)), ((), ()))
NN = (((1,), (0,)), ((), ()))
f32 = jnp.float32
bf16 = jnp.bfloat16


def dot(a, b, dims=NN):
    return lax.dot_general(a, b, dims, preferred_element_type=f32)


def owner_table(lists, counts, own, table, empty):
    def group(g, carry):
        table[g * CAP] = empty
        table[g * CAP + 1] = empty
        rank = jnp.int32(0)
        for j in range(MAXL):
            block = lists[g, j]
            mine = ((block >> 4) == own) & (j < counts[g])
            table[jnp.where(mine, g * CAP + rank, SLOTS)] = block & 15
            rank = jnp.where(mine, jnp.minimum(rank + 1, CAP - 1), rank)
        return carry

    lax.fori_loop(0, 16, group, 0)


def slot_table(lists, counts, own, table, seen):
    for o in range(16):
        seen[o] = 0
    for j in range(MAXL):
        owner = lists[own, j] >> 4
        rank = seen[owner]
        seen[owner] = jnp.minimum(rank + 1, CAP - 1)
        table[j] = owner * CAP + rank


def pick_body(lists, counts, me, lat_ref, out_ref, table, sems):
    owner_table(lists, counts, me[0], table, 0)
    copies = [pltpu.make_async_copy(lat_ref.at[table[s]], out_ref.at[s], sems.at[s]) for s in range(SLOTS)]
    for copy in copies:
        copy.start()
    for copy in copies:
        copy.wait()


def gather_body(lists, counts, me, arrived_ref, out_ref, table, held, total, sems, sems_out):
    step = SLOTS // 4
    parts = [slice(i * step, i * step + step) for i in range(4)]
    copies = [pltpu.make_async_copy(arrived_ref.at[p], held.at[p], sems.at[i]) for i, p in enumerate(parts)]
    for copy in copies:
        copy.start()
    owner_table(lists, counts, me[0], table, 16)
    total[...] = jnp.zeros(total.shape, total.dtype)
    for s in range(SLOTS):
        if s % step == 0:
            copies[s // step].wait()
        total[table[s]] = total[table[s]] + held[s].astype(f32)
    copies = [pltpu.make_async_copy(total.at[4 * i : 4 * i + 4], out_ref.at[4 * i : 4 * i + 4], sems_out.at[i]) for i in range(4)]
    for copy in copies:
        copy.start()
    for copy in copies:
        copy.wait()


def take_body(lists, counts, me, arrived_ref, out_ref, table, seen, sems):
    slot_table(lists, counts, me[0], table, seen)
    count = counts[me[0]]

    def copy(j):
        return pltpu.make_async_copy(arrived_ref.at[table[j]], out_ref.at[j * 16 : j * 16 + 16], sems.at[j])

    for j in range(MAXL):
        live = j < count

        @pl.when(live)
        def _():
            copy(j).start()

        @pl.when(jnp.logical_not(live))
        def _():
            out_ref[j * 16 : j * 16 + 16] = jnp.zeros((16, WIDE), bf16)

    for j in range(MAXL):

        @pl.when(j < count)
        def _():
            copy(j).wait()


def put_body(lists, counts, me, a_ref, b_ref, c_ref, d_ref, out_ref, table, seen, held, sems):
    slot_table(lists, counts, me[0], table, seen)
    count = counts[me[0]]

    def copy(j):
        return pltpu.make_async_copy(held.at[j * 16 : j * 16 + 16], out_ref.at[table[j]], sems.at[j])

    for j in range(MAXL):
        here = slice(j * 16, j * 16 + 16)
        total = a_ref[here].astype(f32) + b_ref[here].astype(f32)
        total = total + (c_ref[here].astype(f32) + d_ref[here].astype(f32))
        held[here] = total.astype(bf16)

        @pl.when(j < count)
        def _():
            copy(j).start()

    for j in range(MAXL):

        @pl.when(j < count)
        def _():
            copy(j).wait()


def turn_body(q_ref, g_ref, qt_ref, gt_ref):
    rows = qt_ref.shape[1]
    for at in range(0, rows, 256):
        here = slice(at, at + 256)
        part = slice(at // 16, at // 16 + 16)
        q = q_ref[part].reshape(256, WIDE)
        qt_ref[:LAT, here] = q[:, :LAT].T
        rope = jnp.concatenate([q[:, LAT:], q[:, LAT:]], axis=1)
        qt_ref[LAT:, here] = rope.T[: WIDE - LAT]
        gt_ref[:, here] = g_ref[part].reshape(256, LAT).T


def two_body(near_ref, far_ref, low_ref, high_ref):
    half = low_ref.shape[0]
    total = near_ref[...].astype(f32) + far_ref[...].astype(f32)
    low_ref[...] = total[:half].astype(bf16)
    high_ref[...] = total[half:].astype(bf16)


def one_body(near_ref, far_ref, low_ref, high_ref, left_ref, right_ref):
    size = left_ref.shape[0]
    half = size // 2
    total = near_ref[...].astype(f32) + far_ref[...].astype(f32)
    left_ref[:half] = total[:half].astype(bf16)
    left_ref[half:] = (total[half:size] + high_ref[...].astype(f32)).astype(bf16)
    right_ref[:half] = (total[size : size + half] + low_ref[...].astype(f32)).astype(bf16)
    right_ref[half:] = total[size + half :].astype(bf16)


ONCHIP = pl.BlockSpec(memory_space=pltpu.VMEM)
INPLACE = pl.BlockSpec(memory_space=pltpu.HBM)


def call(body, outs, scalars, arrays, scratch=(), direct_in=(), direct=(), alias=None):
    args = [
        pltpu.with_memory_space_constraint(a, pltpu.HBM if i in direct_in else pltpu.VMEM)
        for i, a in enumerate(arrays)
    ]
    scalars = [pltpu.with_memory_space_constraint(a, pltpu.HBM) for a in scalars]
    shapes = [(pltpu.HBM if i in direct else pltpu.VMEM)(o.shape, o.dtype) for i, o in enumerate(outs)]
    return pl.pallas_call(
        body,
        in_specs=[pl.BlockSpec(memory_space=pltpu.SMEM)] * len(scalars)
        + [INPLACE if i in direct_in else ONCHIP for i in range(len(arrays))],
        out_specs=tuple(INPLACE if i in direct else ONCHIP for i in range(len(outs))),
        out_shape=tuple(shapes),
        scratch_shapes=list(scratch),
        input_output_aliases=alias or {},
        compiler_params=pltpu.CompilerParams(vmem_limit_bytes=16 * 1024 * 1024),
    )(*scalars, *args)


M_COL, L_COL, R_COL = (0, 1, 2), 3, 4


def forward_body(nkeys, chunk, off, n, block, *refs):
    refs = list(refs)
    first, last = chunk == 0, chunk == 2
    key_refs = [refs.pop(0) for _ in range(nkeys)]
    bias, q_ref, g_ref = refs[:3]
    refs = refs[3:]
    if not first:
        _, _, _, st_in, o_in = refs[:5]
        refs = refs[5:]
    if last:
        qt_in, gt_in = refs[:2]
        refs = refs[2:]
    e_out, p_out, k_out, st_out, o_out = refs[:5]
    refs = refs[5:]
    steps = q_ref.shape[0] * 16 // block
    if last:
        qt_out, gt_out, held, sems, sems_t = refs
        turned = [
            pltpu.make_async_copy(qt_in, qt_out, sems_t.at[0]),
            pltpu.make_async_copy(gt_in, gt_out, sems_t.at[1]),
        ]
        for copy in turned:
            copy.start()

        def leave(i):
            part = pl.ds(i * (block // 16), block // 16)
            return pltpu.make_async_copy(held.at[part], o_out.at[part], sems.at[i])

    at = off
    for ref in key_refs:
        k_out[at : at + ref.shape[0]] = ref[...]
        at += ref.shape[0]
    mine = slice(off, off + n)

    def rows(i, carry):
        here = pl.ds(pl.multiple_of(i * block, block), block)
        part = pl.ds(i * (block // 16), block // 16)
        scores = dot(q_ref[part].reshape(block, WIDE), k_out[mine], NT) + bias[...]
        top = jnp.max(scores, axis=1, keepdims=True)
        if not first:
            m_old = st_in[here, chunk - 1 : chunk]
            l_old = st_in[here, L_COL : L_COL + 1]
            r_old = st_in[here, R_COL : R_COL + 1]
            top = jnp.maximum(top, m_old)
        expo = jnp.exp2((scores - top) * EXPC)
        values = k_out[mine, :LAT]
        grads = dot(g_ref[part].reshape(block, LAT), values, NT)
        total = jnp.sum(expo, axis=1, keepdims=True)
        rdot = jnp.sum(expo * grads, axis=1, keepdims=True)
        expo = expo.astype(bf16)
        e_out[here, mine] = expo
        p_out[here, mine] = grads.astype(bf16)
        attended = dot(expo, values)
        if not first:
            fade = jnp.exp2((m_old - top) * EXPC)
            total = total + fade * l_old
            rdot = rdot + fade * r_old
            attended = attended + fade * o_in[here]
        if last:
            total = 1.0 / total
            rdot = rdot * total
            attended = attended * total
        st_out[here, chunk : chunk + 1] = top
        st_out[here, L_COL : L_COL + 1] = total
        st_out[here, R_COL : R_COL + 1] = rdot
        if last:
            held[part] = attended.astype(bf16).reshape(block // 16, 16, LAT)
            leave(i).start()
        else:
            o_out[here] = attended
        return carry

    lax.fori_loop(0, steps, rows, 0)
    if last:
        for i in range(steps):
            leave(i).wait()
        for copy in turned:
            copy.wait()


def forward(chunk, off, n, total_keys, key_parts, bias, q, g, state=(), turned=(), block=256):
    rows = q.shape[0] * 16
    last = chunk == 2
    side = jax.ShapeDtypeStruct((rows, total_keys), bf16)
    outs = [
        side,
        side,
        jax.ShapeDtypeStruct((total_keys, WIDE), bf16),
        jax.ShapeDtypeStruct((rows, 128), f32),
        jax.ShapeDtypeStruct(g.shape, bf16) if last else jax.ShapeDtypeStruct((rows, LAT), f32),
    ]
    scratch = []
    if last:
        outs += [jax.ShapeDtypeStruct(t.shape, t.dtype) for t in turned]
        scratch = [pltpu.VMEM(g.shape, bf16), pltpu.SemaphoreType.DMA((rows // block,)), pltpu.SemaphoreType.DMA((2,))]
    arrays = [*key_parts, bias, q, g, *state, *turned]
    start = len(key_parts) + 3
    return call(
        functools.partial(forward_body, len(key_parts), chunk, off, n, block),
        outs,
        (),
        arrays,
        scratch=scratch,
        direct_in=range(len(arrays) - len(turned), len(arrays)),
        direct=(4,) if last else (),
        alias={start + i: i for i in range((4 if last else 5) if state else 0)},
    )


def backward_body(chunk, off, n, step, tile, qt_ref, gt_ref, e_ref, p_ref, st_ref, k_ref, far_out, near_out, s_out, k_out, a_sc, r_sc):
    rows = qt_ref.shape[1]
    half = n // 2
    st = st_ref[...]
    a = jnp.exp2((st[:, chunk : chunk + 1] - st[:, 2:3]) * EXPC) * st[:, L_COL : L_COL + 1]
    a_sc[...] = jnp.broadcast_to(a, (rows, 128))
    r_sc[...] = jnp.broadcast_to(st[:, R_COL : R_COL + 1], (rows, 128))
    for start in range(0, n, tile):
        cols = slice(off + (start + half) % n, off + (start + half) % n + tile)
        acc = None
        for at in range(0, rows, step):
            here = slice(at, at + step)
            a = jnp.tile(a_sc[here], (1, tile // 128))
            r = jnp.tile(r_sc[here], (1, tile // 128))
            weights = (e_ref[here, cols].astype(f32) * a).astype(bf16)
            sg = (weights.astype(f32) * (p_ref[here, cols].astype(f32) - r) * SCALE).astype(bf16)
            s_out[here, cols] = sg
            key_part = dot(qt_ref[:, here], sg)
            value_part = dot(gt_ref[:, here], weights)
            if acc is None:
                acc = [key_part[:LAT] + value_part, key_part[LAT:]]
            else:
                acc = [acc[0] + (key_part[:LAT] + value_part), acc[1] + key_part[LAT:]]
        top = acc[0].T.astype(bf16)
        low = jnp.concatenate([acc[1], jnp.zeros_like(acc[1])], axis=0).T[:, : WIDE - LAT].astype(bf16)
        ref = far_out if start < half else near_out
        put = slice(start % half, start % half + tile)
        ref[put, :LAT] = top
        ref[put, LAT:] = low


def backward(chunk, off, n, qt, gt, e, p, st, k, tile=256, step=256):
    rows = e.shape[0]
    part = jax.ShapeDtypeStruct((n // 2, WIDE), bf16)
    return call(
        functools.partial(backward_body, chunk, off, n, step, tile),
        (part, part, jax.ShapeDtypeStruct(p.shape, bf16), jax.ShapeDtypeStruct(k.shape, bf16)),
        (),
        (qt, gt, e, p, st, k),
        scratch=[pltpu.VMEM((rows, 128), f32)] * 2,
        alias={3: 2, 5: 3},
    )


def query_body(block, s_ref, k_ref, out_ref, held, sems):
    steps = out_ref.shape[0] * 16 // block

    def leave(i):
        part = pl.ds(i * (block // 16), block // 16)
        return pltpu.make_async_copy(held.at[part], out_ref.at[part], sems.at[i])

    def rows(i, carry):
        here = pl.ds(pl.multiple_of(i * block, block), block)
        part = pl.ds(i * (block // 16), block // 16)
        held[part] = dot(s_ref[here], k_ref[...]).astype(bf16).reshape(block // 16, 16, WIDE)
        leave(i).start()
        return carry

    lax.fori_loop(0, steps, rows, 0)
    for i in range(steps):
        leave(i).wait()


def query_side(s, k, block=256):
    rows = s.shape[0]
    shape = (rows // 16, 16, WIDE)
    return call(
        functools.partial(query_body, block),
        (jax.ShapeDtypeStruct(shape, bf16),),
        (),
        (s, k),
        scratch=[pltpu.VMEM(shape, bf16), pltpu.SemaphoreType.DMA((rows // block,))],
        direct=(0,),
    )[0]


def per_device(queries, out_grad, latents, list_blocks, list_counts, valid_tokens):
    me = lax.axis_index("req")
    head = lax.axis_index("head")
    chip, core = head // 2, head % 2
    tokens = latents.shape[1]
    shift = lambda d: [(x * 2 + c, ((x + d) % 4) * 2 + c) for x in range(4) for c in range(2)]
    right, left, sibling = shift(1), shift(-1), [(h, h ^ 1) for h in range(8)]
    send = lambda a, perm: lax.ppermute(a, "head", perm)
    scalars = (list_blocks, list_counts, me.reshape(1).astype(jnp.int32))

    smem = lambda n: pltpu.SMEM((n,), jnp.int32)
    slots = jax.ShapeDtypeStruct((SLOTS, tokens, WIDE), bf16)
    keys = MAXL * tokens
    share_of = lambda n: jax.ShapeDtypeStruct((n, WIDE), bf16)

    dma = lambda n: pltpu.SemaphoreType.DMA((n,))
    (outgoing,) = call(
        pick_body, (slots,), scalars, (latents,), scratch=[smem(SLOTS + 1), dma(SLOTS)], direct_in=(0,), direct=(0,)
    )
    arrived = lax.all_to_all(outgoing.reshape(16, CAP, tokens, WIDE), "req", 0, 0, tiled=True)

    my_blocks = lax.dynamic_index_in_dim(list_blocks, me, 0, keepdims=False)
    my_count = lax.dynamic_index_in_dim(list_counts, me, 0, keepdims=False)
    ids = jnp.arange(valid_tokens.shape[0], dtype=jnp.int32)
    filled = jnp.sum(jnp.where(my_blocks[:, None] == ids[None, :], valid_tokens[None, :], 0), axis=1)
    filled = jnp.where(jnp.arange(MAXL, dtype=jnp.int32) < my_count, filled, 0)
    filled = jnp.repeat(filled, tokens)[None, :]
    offset = jnp.tile(jnp.arange(tokens, dtype=jnp.int32), MAXL)[None, :]
    at = lambda d, c: ((chip + d) % 4) * 2 + c
    other = 1 - core
    places = [at(0, core), at(0, other), at(3, core), at(1, core), at(3, other), at(1, other), at(2, core), at(2, other)]
    first_token = jnp.stack(places)[:, None] * tokens
    bias = jnp.where(first_token + offset < filled, 0.0, BIG).astype(f32)
    bias0, bias1, bias2 = [bias[i:j].reshape(1, -1) for i, j in ((0, 2), (2, 6), (6, 8))]

    flat = lambda a: jax.ShapeDtypeStruct((a.shape[2], a.shape[0] * a.shape[1]), bf16)
    qt, gt = call(turn_body, (flat(queries), flat(out_grad)), (), (queries, out_grad))
    arrived, qt, gt, bias0, bias1, bias2 = lax.optimization_barrier((arrived, qt, gt, bias0, bias1, bias2))

    (share,) = call(
        take_body,
        (share_of(keys),),
        scalars,
        (arrived.reshape(slots.shape),),
        scratch=[smem(MAXL), smem(16), dma(MAXL)],
        direct_in=(0,),
    )

    after = lambda a, *others: lax.optimization_barrier((a, *others))[0]
    q, g = queries, out_grad
    every = 8 * keys
    r1 = send(share, right)
    l1 = send(share, left)
    s0 = send(share, sibling)
    state = forward(0, 0, 2 * keys, every, [share, s0], bias0, q, g)
    r1 = after(r1, state[3])
    l1 = after(l1, state[3])
    r2 = send(r1, right)
    s1 = send(r1, sibling)
    s2 = send(l1, sibling)
    state = forward(1, 2 * keys, 4 * keys, every, [r1, l1, s1, s2], bias1, q, g, state)
    r2 = after(r2, state[3])
    s3 = send(r2, sibling)
    e, p, k, st, attended, qt, gt = forward(2, 6 * keys, 2 * keys, every, [r2, s3], bias2, q, g, state, (qt, gt))

    fold = lambda a: a.reshape(-1, tokens, WIDE)
    unfold = lambda a: a.reshape(-1, WIDE)
    far2, near2, p, k = backward(2, 6 * keys, 2 * keys, qt, gt, e, p, st, k)
    mate2 = send(far2, sibling)
    far1, near1, p, k = backward(1, 2 * keys, 4 * keys, qt, gt, e, p, st, k)
    mate1 = unfold(send(fold(far1), sibling))
    low, high = call(two_body, (share_of(keys // 2),) * 2, (), (after(near2, near1), mate2))
    from_left = send(low, right)
    from_right = send(high, left)
    far0, near0, p, k = backward(0, 0, 2 * keys, qt, gt, e, p, after(st, low), k)
    mate0 = send(far0, sibling)
    to_left, to_right = call(
        one_body, (share_of(keys),) * 2, (), (after(near1, near0), mate1, from_left, from_right)
    )
    got_left = send(to_right, right)
    got_right = send(to_left, left)
    query_grad = query_side(p, after(k, to_left))
    near0 = after(near0, query_grad)
    (slot_grads,) = call(
        put_body,
        (slots,),
        scalars,
        (near0, mate0, got_left, got_right),
        scratch=[smem(MAXL), smem(16), pltpu.VMEM((keys, WIDE), bf16), dma(MAXL)],
        direct=(0,),
    )
    returned = lax.all_to_all(slot_grads.reshape(16, CAP, tokens, WIDE), "req", 0, 0, tiled=True)
    (latent_grad,) = call(
        gather_body,
        (jax.ShapeDtypeStruct((16, tokens, WIDE), f32),),
        scalars,
        (returned.reshape(slots.shape),),
        scratch=[
            smem(SLOTS + 1),
            pltpu.VMEM((SLOTS, tokens, WIDE), bf16),
            pltpu.VMEM((17, tokens, WIDE), f32),
            dma(4),
            dma(4),
        ],
        direct_in=(0,),
        direct=(0,),
    )
    return (attended, query_grad, latent_grad)


def solution(mesh):
    in_specs = (
        P("req", "head", None),
        P("req", "head", None),
        P("req", "head", None),
        P(),
        P(),
        P(),
    )
    out_specs = (P("req", "head", None), P("req", "head", None), P("req", "head", None))
    return jax.shard_map(
        per_device, mesh=mesh, in_specs=in_specs, out_specs=out_specs, check_vma=False
    )
```

```python
import functools
import math

import jax
import jax.numpy as jnp
from jax import lax
from jax.experimental import pallas as pl
from jax.experimental.pallas import tpu as pltpu
from jax.sharding import PartitionSpec as P

LAT = 512
WIDE = 576
BLOCK = 128
MAXL = 16
CAP = 2
BIG = -1e30
SLOTS = 16 * CAP
SCALE = 192.0 ** (-0.5)
EXPC = SCALE * math.log2(math.e)
NT = (((1,), (1,)), ((), ()))
NN = (((1,), (0,)), ((), ()))
f32 = jnp.float32
bf16 = jnp.bfloat16


def dot(a, b, dims=NN):
    return lax.dot_general(a, b, dims, preferred_element_type=f32)


def owner_table(lists, counts, own, table, empty):
    def group(g, carry):
        table[g * CAP] = empty
        table[g * CAP + 1] = empty
        rank = jnp.int32(0)
        for j in range(MAXL):
            block = lists[g, j]
            mine = ((block >> 4) == own) & (j < counts[g])
            table[jnp.where(mine, g * CAP + rank, SLOTS)] = block & 15
            rank = jnp.where(mine, jnp.minimum(rank + 1, CAP - 1), rank)
        return carry

    lax.fori_loop(0, 16, group, 0)


def slot_table(lists, counts, own, table, seen):
    for o in range(16):
        seen[o] = 0
    for j in range(MAXL):
        owner = lists[own, j] >> 4
        rank = seen[owner]
        seen[owner] = jnp.minimum(rank + 1, CAP - 1)
        table[j] = owner * CAP + rank


def pick_body(lists, counts, me, lat_ref, out_ref, table, lat, held, sem, sems):
    load = pltpu.make_async_copy(lat_ref, lat, sem.at[0])
    load.start()
    owner_table(lists, counts, me[0], table, 0)
    load.wait()
    step = SLOTS // 4
    parts = [slice(i * step, i * step + step) for i in range(4)]
    copies = [pltpu.make_async_copy(held.at[p], out_ref.at[p], sems.at[i]) for i, p in enumerate(parts)]
    for s in range(SLOTS):
        held[s] = lat[table[s]]
        if s % step == step - 1:
            copies[s // step].start()
    for copy in copies:
        copy.wait()


def gather_body(lists, counts, me, arrived_ref, out_ref, table, held, total, sems, sems_out):
    step = SLOTS // 4
    parts = [slice(i * step, i * step + step) for i in range(4)]
    copies = [pltpu.make_async_copy(arrived_ref.at[p], held.at[p], sems.at[i]) for i, p in enumerate(parts)]
    for copy in copies:
        copy.start()
    owner_table(lists, counts, me[0], table, 16)
    total[...] = jnp.zeros(total.shape, total.dtype)
    for s in range(SLOTS):
        if s % step == 0:
            copies[s // step].wait()
        total[table[s]] = total[table[s]] + held[s].astype(f32)
    copies = [pltpu.make_async_copy(total.at[4 * i : 4 * i + 4], out_ref.at[4 * i : 4 * i + 4], sems_out.at[i]) for i in range(4)]
    for copy in copies:
        copy.start()
    for copy in copies:
        copy.wait()


def take_body(lists, counts, me, arrived_ref, out_ref, table, seen, sems):
    slot_table(lists, counts, me[0], table, seen)
    count = counts[me[0]]

    def copy(j):
        return pltpu.make_async_copy(arrived_ref.at[table[j]], out_ref.at[j * 16 : j * 16 + 16], sems.at[j])

    for j in range(MAXL):
        live = j < count

        @pl.when(live)
        def _():
            copy(j).start()

        @pl.when(jnp.logical_not(live))
        def _():
            out_ref[j * 16 : j * 16 + 16] = jnp.zeros((16, WIDE), bf16)

    for j in range(MAXL):

        @pl.when(j < count)
        def _():
            copy(j).wait()


def put_body(lists, counts, me, a_ref, b_ref, c_ref, d_ref, out_ref, table, seen, held, sems):
    slot_table(lists, counts, me[0], table, seen)
    count = counts[me[0]]

    def copy(j):
        return pltpu.make_async_copy(held.at[j * 16 : j * 16 + 16], out_ref.at[table[j]], sems.at[j])

    for j in range(MAXL):
        here = slice(j * 16, j * 16 + 16)
        total = a_ref[here].astype(f32) + b_ref[here].astype(f32)
        total = total + (c_ref[here].astype(f32) + d_ref[here].astype(f32))
        held[here] = total.astype(bf16)

        @pl.when(j < count)
        def _():
            copy(j).start()

    for j in range(MAXL):

        @pl.when(j < count)
        def _():
            copy(j).wait()


def turn_body(q_ref, g_ref, qt_ref, gt_ref):
    rows = qt_ref.shape[1]
    for at in range(0, rows, 256):
        here = slice(at, at + 256)
        part = slice(at // 16, at // 16 + 16)
        q = q_ref[part].reshape(256, WIDE)
        qt_ref[:LAT, here] = q[:, :LAT].T
        rope = jnp.concatenate([q[:, LAT:], q[:, LAT:]], axis=1)
        qt_ref[LAT:, here] = rope.T[: WIDE - LAT]
        gt_ref[:, here] = g_ref[part].reshape(256, LAT).T


def two_body(near_ref, far_ref, low_ref, high_ref):
    half = low_ref.shape[0]
    total = near_ref[...].astype(f32) + far_ref[...].astype(f32)
    low_ref[...] = total[:half].astype(bf16)
    high_ref[...] = total[half:].astype(bf16)


def one_body(near_ref, far_ref, low_ref, high_ref, left_ref, right_ref):
    size = left_ref.shape[0]
    half = size // 2
    total = near_ref[...].astype(f32) + far_ref[...].astype(f32)
    left_ref[:half] = total[:half].astype(bf16)
    left_ref[half:] = (total[half:size] + high_ref[...].astype(f32)).astype(bf16)
    right_ref[:half] = (total[size : size + half] + low_ref[...].astype(f32)).astype(bf16)
    right_ref[half:] = total[size + half :].astype(bf16)


ONCHIP = pl.BlockSpec(memory_space=pltpu.VMEM)
INPLACE = pl.BlockSpec(memory_space=pltpu.HBM)


def call(body, outs, scalars, arrays, scratch=(), direct_in=(), direct=(), alias=None, flops=None):
    args = [
        pltpu.with_memory_space_constraint(a, pltpu.HBM if i in direct_in else pltpu.VMEM)
        for i, a in enumerate(arrays)
    ]
    scalars = [pltpu.with_memory_space_constraint(a, pltpu.HBM) for a in scalars]
    shapes = [(pltpu.HBM if i in direct else pltpu.VMEM)(o.shape, o.dtype) for i, o in enumerate(outs)]
    return pl.pallas_call(
        body,
        in_specs=[pl.BlockSpec(memory_space=pltpu.SMEM)] * len(scalars)
        + [INPLACE if i in direct_in else ONCHIP for i in range(len(arrays))],
        out_specs=tuple(INPLACE if i in direct else ONCHIP for i in range(len(outs))),
        out_shape=tuple(shapes),
        scratch_shapes=list(scratch),
        input_output_aliases=alias or {},
        cost_estimate=flops and pl.CostEstimate(flops=flops, transcendentals=0, bytes_accessed=0),
        compiler_params=pltpu.CompilerParams(vmem_limit_bytes=16 * 1024 * 1024),
    )(*scalars, *args)


M_COL, L_COL, R_COL = (0, 1, 2), 3, 4


def forward_body(nkeys, chunk, off, n, block, *refs):
    refs = list(refs)
    first, last = chunk == 0, chunk == 2
    key_refs = [refs.pop(0) for _ in range(nkeys)]
    bias, q_ref, g_ref = refs[:3]
    refs = refs[3:]
    if not first:
        _, _, _, st_in, o_in = refs[:5]
        refs = refs[5:]
    if last:
        qt_in, gt_in = refs[:2]
        refs = refs[2:]
    e_out, p_out, k_out, st_out, o_out = refs[:5]
    refs = refs[5:]
    steps = q_ref.shape[0] * 16 // block
    if last:
        qt_out, gt_out, held, sems, sems_t = refs
        turned = [
            pltpu.make_async_copy(qt_in, qt_out, sems_t.at[0]),
            pltpu.make_async_copy(gt_in, gt_out, sems_t.at[1]),
        ]
        for copy in turned:
            copy.start()

        def leave(i):
            part = pl.ds(i * (block // 16), block // 16)
            return pltpu.make_async_copy(held.at[part], o_out.at[part], sems.at[i])

    at = off
    for ref in key_refs:
        k_out[at : at + ref.shape[0]] = ref[...]
        at += ref.shape[0]
    mine = slice(off, off + n)

    def rows(i, carry):
        here = pl.ds(pl.multiple_of(i * block, block), block)
        part = pl.ds(i * (block // 16), block // 16)
        scores = dot(q_ref[part].reshape(block, WIDE), k_out[mine], NT) + bias[...]
        top = jnp.max(scores, axis=1, keepdims=True)
        if not first:
            m_old = st_in[here, chunk - 1 : chunk]
            l_old = st_in[here, L_COL : L_COL + 1]
            r_old = st_in[here, R_COL : R_COL + 1]
            top = jnp.maximum(top, m_old)
        expo = jnp.exp2((scores - top) * EXPC)
        values = k_out[mine, :LAT]
        grads = dot(g_ref[part].reshape(block, LAT), values, NT)
        total = jnp.sum(expo, axis=1, keepdims=True)
        rdot = jnp.sum(expo * grads, axis=1, keepdims=True)
        expo = expo.astype(bf16)
        e_out[here, mine] = expo
        p_out[here, mine] = grads.astype(bf16)
        attended = dot(expo, values)
        if not first:
            fade = jnp.exp2((m_old - top) * EXPC)
            total = total + fade * l_old
            rdot = rdot + fade * r_old
            attended = attended + fade * o_in[here]
        if last:
            total = 1.0 / total
            rdot = rdot * total
            attended = attended * total
        st_out[here, chunk : chunk + 1] = top
        st_out[here, L_COL : L_COL + 1] = total
        st_out[here, R_COL : R_COL + 1] = rdot
        if last:
            held[part] = attended.astype(bf16).reshape(block // 16, 16, LAT)
            leave(i).start()
        else:
            o_out[here] = attended
        return carry

    lax.fori_loop(0, steps, rows, 0)
    if last:
        for i in range(steps):
            leave(i).wait()
        for copy in turned:
            copy.wait()


def forward(chunk, off, n, total_keys, key_parts, bias, q, g, state=(), turned=(), block=256):
    rows = q.shape[0] * 16
    last = chunk == 2
    side = jax.ShapeDtypeStruct((rows, total_keys), bf16)
    outs = [
        side,
        side,
        jax.ShapeDtypeStruct((total_keys, WIDE), bf16),
        jax.ShapeDtypeStruct((rows, 128), f32),
        jax.ShapeDtypeStruct(g.shape, bf16) if last else jax.ShapeDtypeStruct((rows, LAT), f32),
    ]
    scratch = []
    if last:
        outs += [jax.ShapeDtypeStruct(t.shape, t.dtype) for t in turned]
        scratch = [pltpu.VMEM(g.shape, bf16), pltpu.SemaphoreType.DMA((rows // block,)), pltpu.SemaphoreType.DMA((2,))]
    arrays = [*key_parts, bias, q, g, *state, *turned]
    start = len(key_parts) + 3
    return call(
        functools.partial(forward_body, len(key_parts), chunk, off, n, block),
        outs,
        (),
        arrays,
        scratch=scratch,
        direct_in=range(len(arrays) - len(turned), len(arrays)),
        direct=(4,) if last else (),
        alias={start + i: i for i in range((4 if last else 5) if state else 0)},
        flops=2 * rows * n * (WIDE + 2 * LAT),
    )


def backward_body(chunk, off, n, step, tile, qt_ref, gt_ref, e_ref, p_ref, st_ref, k_ref, far_out, near_out, s_out, k_out, a_sc, r_sc):
    rows = qt_ref.shape[1]
    half = n // 2
    st = st_ref[...]
    a = jnp.exp2((st[:, chunk : chunk + 1] - st[:, 2:3]) * EXPC) * st[:, L_COL : L_COL + 1]
    a_sc[...] = jnp.broadcast_to(a, (rows, 128))
    r_sc[...] = jnp.broadcast_to(st[:, R_COL : R_COL + 1], (rows, 128))
    for start in range(0, n, tile):
        cols = slice(off + (start + half) % n, off + (start + half) % n + tile)
        acc = None
        for at in range(0, rows, step):
            here = slice(at, at + step)
            a = jnp.tile(a_sc[here], (1, tile // 128))
            r = jnp.tile(r_sc[here], (1, tile // 128))
            weights = (e_ref[here, cols].astype(f32) * a).astype(bf16)
            sg = (weights.astype(f32) * (p_ref[here, cols].astype(f32) - r) * SCALE).astype(bf16)
            s_out[here, cols] = sg
            key_part = dot(qt_ref[:, here], sg)
            value_part = dot(gt_ref[:, here], weights)
            if acc is None:
                acc = [key_part[:LAT] + value_part, key_part[LAT:]]
            else:
                acc = [acc[0] + (key_part[:LAT] + value_part), acc[1] + key_part[LAT:]]
        top = acc[0].T.astype(bf16)
        low = jnp.concatenate([acc[1], jnp.zeros_like(acc[1])], axis=0).T[:, : WIDE - LAT].astype(bf16)
        ref = far_out if start < half else near_out
        put = slice(start % half, start % half + tile)
        ref[put, :LAT] = top
        ref[put, LAT:] = low


def backward(chunk, off, n, qt, gt, e, p, st, k, tile=256, step=256):
    rows = e.shape[0]
    part = jax.ShapeDtypeStruct((n // 2, WIDE), bf16)
    return call(
        functools.partial(backward_body, chunk, off, n, step, tile),
        (part, part, jax.ShapeDtypeStruct(p.shape, bf16), jax.ShapeDtypeStruct(k.shape, bf16)),
        (),
        (qt, gt, e, p, st, k),
        scratch=[pltpu.VMEM((rows, 128), f32)] * 2,
        alias={3: 2, 5: 3},
        flops=2 * rows * n * (WIDE + LAT),
    )


def query_body(block, s_ref, k_ref, out_ref, held, sems):
    steps = out_ref.shape[0] * 16 // block

    def leave(i):
        part = pl.ds(i * (block // 16), block // 16)
        return pltpu.make_async_copy(held.at[part], out_ref.at[part], sems.at[i])

    def rows(i, carry):
        here = pl.ds(pl.multiple_of(i * block, block), block)
        part = pl.ds(i * (block // 16), block // 16)
        held[part] = dot(s_ref[here], k_ref[...]).astype(bf16).reshape(block // 16, 16, WIDE)
        leave(i).start()
        return carry

    lax.fori_loop(0, steps, rows, 0)
    for i in range(steps):
        leave(i).wait()


def query_side(s, k, block=256):
    rows = s.shape[0]
    shape = (rows // 16, 16, WIDE)
    return call(
        functools.partial(query_body, block),
        (jax.ShapeDtypeStruct(shape, bf16),),
        (),
        (s, k),
        scratch=[pltpu.VMEM(shape, bf16), pltpu.SemaphoreType.DMA((rows // block,))],
        direct=(0,),
        flops=2 * rows * k.shape[0] * WIDE,
    )[0]


def per_device(queries, out_grad, latents, list_blocks, list_counts, valid_tokens):
    me = lax.axis_index("req")
    head = lax.axis_index("head")
    chip, core = head // 2, head % 2
    tokens = latents.shape[1]
    shift = lambda d: [(x * 2 + c, ((x + d) % 4) * 2 + c) for x in range(4) for c in range(2)]
    right, left, sibling = shift(1), shift(-1), [(h, h ^ 1) for h in range(8)]
    send = lambda a, perm: lax.ppermute(a, "head", perm)
    scalars = (list_blocks, list_counts, me.reshape(1).astype(jnp.int32))

    smem = lambda n: pltpu.SMEM((n,), jnp.int32)
    slots = jax.ShapeDtypeStruct((SLOTS, tokens, WIDE), bf16)
    keys = MAXL * tokens
    share_of = lambda n: jax.ShapeDtypeStruct((n, WIDE), bf16)

    dma = lambda n: pltpu.SemaphoreType.DMA((n,))
    (outgoing,) = call(
        pick_body,
        (slots,),
        scalars,
        (latents,),
        scratch=[
            smem(SLOTS + 1),
            pltpu.VMEM(latents.shape, bf16),
            pltpu.VMEM((SLOTS, tokens, WIDE), bf16),
            dma(1),
            dma(4),
        ],
        direct_in=(0,),
        direct=(0,),
    )
    arrived = lax.all_to_all(outgoing.reshape(16, CAP, tokens, WIDE), "req", 0, 0, tiled=True)

    my_blocks = lax.dynamic_index_in_dim(list_blocks, me, 0, keepdims=False)
    my_count = lax.dynamic_index_in_dim(list_counts, me, 0, keepdims=False)
    ids = jnp.arange(valid_tokens.shape[0], dtype=jnp.int32)
    filled = jnp.sum(jnp.where(my_blocks[:, None] == ids[None, :], valid_tokens[None, :], 0), axis=1)
    filled = jnp.where(jnp.arange(MAXL, dtype=jnp.int32) < my_count, filled, 0)
    filled = jnp.repeat(filled, tokens)[None, :]
    offset = jnp.tile(jnp.arange(tokens, dtype=jnp.int32), MAXL)[None, :]
    at = lambda d, c: ((chip + d) % 4) * 2 + c
    other = 1 - core
    places = [at(0, core), at(0, other), at(3, core), at(1, core), at(3, other), at(1, other), at(2, core), at(2, other)]
    first_token = jnp.stack(places)[:, None] * tokens
    bias = jnp.where(first_token + offset < filled, 0.0, BIG).astype(f32)
    bias0, bias1, bias2 = [bias[i:j].reshape(1, -1) for i, j in ((0, 2), (2, 6), (6, 8))]

    flat = lambda a: jax.ShapeDtypeStruct((a.shape[2], a.shape[0] * a.shape[1]), bf16)
    qt, gt = call(turn_body, (flat(queries), flat(out_grad)), (), (queries, out_grad))
    arrived, qt, gt, bias0, bias1, bias2 = lax.optimization_barrier((arrived, qt, gt, bias0, bias1, bias2))

    (share,) = call(
        take_body,
        (share_of(keys),),
        scalars,
        (arrived.reshape(slots.shape),),
        scratch=[smem(MAXL), smem(16), dma(MAXL)],
        direct_in=(0,),
    )

    after = lambda a, *others: lax.optimization_barrier((a, *others))[0]
    q, g = queries, out_grad
    every = 8 * keys
    r1 = send(share, right)
    l1 = send(share, left)
    s0 = send(share, sibling)
    state = forward(0, 0, 2 * keys, every, [share, s0], bias0, q, g)
    r1 = after(r1, state[3])
    l1 = after(l1, state[3])
    r2 = send(r1, right)
    s1 = send(r1, sibling)
    s2 = send(l1, sibling)
    state = forward(1, 2 * keys, 4 * keys, every, [r1, l1, s1, s2], bias1, q, g, state)
    r2 = after(r2, state[3])
    s3 = send(r2, sibling)
    e, p, k, st, attended, qt, gt = forward(2, 6 * keys, 2 * keys, every, [r2, s3], bias2, q, g, state, (qt, gt))

    fold = lambda a: a.reshape(-1, tokens, WIDE)
    unfold = lambda a: a.reshape(-1, WIDE)
    far2, near2, p, k = backward(2, 6 * keys, 2 * keys, qt, gt, e, p, st, k)
    mate2 = send(far2, sibling)
    far1, near1, p, k = backward(1, 2 * keys, 4 * keys, qt, gt, e, p, st, k)
    mate1 = unfold(send(fold(far1), sibling))
    low, high = call(two_body, (share_of(keys // 2),) * 2, (), (after(near2, near1), mate2))
    from_left = send(low, right)
    from_right = send(high, left)
    far0, near0, p, k = backward(0, 0, 2 * keys, qt, gt, e, p, after(st, low), k)
    mate0 = send(far0, sibling)
    to_left, to_right = call(
        one_body, (share_of(keys),) * 2, (), (after(near1, near0), mate1, from_left, from_right)
    )
    got_left = send(to_right, right)
    got_right = send(to_left, left)
    query_grad = query_side(p, after(k, to_left))
    near0 = after(near0, query_grad)
    (slot_grads,) = call(
        put_body,
        (slots,),
        scalars,
        (near0, mate0, got_left, got_right),
        scratch=[smem(MAXL), smem(16), pltpu.VMEM((keys, WIDE), bf16), dma(MAXL)],
        direct=(0,),
    )
    returned = lax.all_to_all(slot_grads.reshape(16, CAP, tokens, WIDE), "req", 0, 0, tiled=True)
    (latent_grad,) = call(
        gather_body,
        (jax.ShapeDtypeStruct((16, tokens, WIDE), f32),),
        scalars,
        (returned.reshape(slots.shape),),
        scratch=[
            smem(SLOTS + 1),
            pltpu.VMEM((SLOTS, tokens, WIDE), bf16),
            pltpu.VMEM((17, tokens, WIDE), f32),
            dma(4),
            dma(4),
        ],
        direct_in=(0,),
        direct=(0,),
    )
    return (attended, query_grad, latent_grad)


def solution(mesh):
    in_specs = (
        P("req", "head", None),
        P("req", "head", None),
        P("req", "head", None),
        P(),
        P(),
        P(),
    )
    out_specs = (P("req", "head", None), P("req", "head", None), P("req", "head", None))
    return jax.shard_map(
        per_device, mesh=mesh, in_specs=in_specs, out_specs=out_specs, check_vma=False
    )
```

```python
import functools
import math

import jax
import jax.numpy as jnp
from jax import lax
from jax.experimental import pallas as pl
from jax.experimental.pallas import tpu as pltpu
from jax.sharding import PartitionSpec as P


LAT = 512
WIDE = 576
MAXL = 16
CAP = 2
BIG = -1e30
SLOTS = 16 * CAP
SCALE = 192.0 ** (-0.5)
EXPC = SCALE * math.log2(math.e)
NT = (((1,), (1,)), ((), ()))
NN = (((1,), (0,)), ((), ()))
f32 = jnp.float32
bf16 = jnp.bfloat16


def dot(a, b, dims=NN):
    return lax.dot_general(a, b, dims, preferred_element_type=f32)


def owner_table(lists, counts, own, table, empty):
    def group(g, carry):
        table[g * CAP] = empty
        table[g * CAP + 1] = empty
        rank = jnp.int32(0)
        for j in range(MAXL):
            block = lists[g, j]
            mine = ((block >> 4) == own) & (j < counts[g])
            table[jnp.where(mine, g * CAP + rank, SLOTS)] = block & 15
            rank = jnp.where(mine, jnp.minimum(rank + 1, CAP - 1), rank)
        return carry

    lax.fori_loop(0, 16, group, 0)


def slot_table(lists, own, table, seen):
    for o in range(16):
        seen[o] = 0
    for j in range(MAXL):
        owner = lists[own, j] >> 4
        rank = seen[owner]
        seen[owner] = jnp.minimum(rank + 1, CAP - 1)
        table[j] = owner * CAP + rank


def pick_body(lists, counts, me, lat_ref, out_ref, table, lat, held, sem, sems):
    load = pltpu.make_async_copy(lat_ref, lat, sem.at[0])
    load.start()
    owner_table(lists, counts, me[0], table, 0)
    load.wait()
    step = SLOTS // 4
    parts = [slice(i * step, i * step + step) for i in range(4)]
    copies = [pltpu.make_async_copy(held.at[p], out_ref.at[p], sems.at[i]) for i, p in enumerate(parts)]
    for s in range(SLOTS):
        held[s] = lat[table[s]]
        if s % step == step - 1:
            copies[s // step].start()
    for copy in copies:
        copy.wait()


def gather_body(lists, counts, me, arrived_ref, out_ref, table, held, total, sems, sems_out):
    step = SLOTS // 4
    parts = [slice(i * step, i * step + step) for i in range(4)]
    copies = [pltpu.make_async_copy(arrived_ref.at[p], held.at[p], sems.at[i]) for i, p in enumerate(parts)]
    for copy in copies:
        copy.start()
    owner_table(lists, counts, me[0], table, 16)
    total[...] = jnp.zeros(total.shape, total.dtype)
    for s in range(SLOTS):
        if s % step == 0:
            copies[s // step].wait()
        total[table[s]] = total[table[s]] + held[s].astype(f32)
    copies = [pltpu.make_async_copy(total.at[4 * i : 4 * i + 4], out_ref.at[4 * i : 4 * i + 4], sems_out.at[i]) for i in range(4)]
    for copy in copies:
        copy.start()
    for copy in copies:
        copy.wait()


def take_body(lists, counts, me, arrived_ref, out_ref, table, seen, sems):
    slot_table(lists, me[0], table, seen)
    count = counts[me[0]]

    def copy(j):
        return pltpu.make_async_copy(arrived_ref.at[table[j]], out_ref.at[j * 16 : j * 16 + 16], sems.at[j])

    for j in range(MAXL):
        live = j < count

        @pl.when(live)
        def _():
            copy(j).start()

        @pl.when(jnp.logical_not(live))
        def _():
            out_ref[j * 16 : j * 16 + 16] = jnp.zeros((16, WIDE), bf16)

    for j in range(MAXL):

        @pl.when(j < count)
        def _():
            copy(j).wait()


def put_body(lists, counts, me, a_ref, b_ref, c_ref, d_ref, out_ref, table, seen, held, sems):
    slot_table(lists, me[0], table, seen)
    count = counts[me[0]]

    def copy(j):
        return pltpu.make_async_copy(held.at[j * 16 : j * 16 + 16], out_ref.at[table[j]], sems.at[j])

    for j in range(MAXL):
        here = slice(j * 16, j * 16 + 16)
        total = a_ref[here].astype(f32) + b_ref[here].astype(f32)
        total = total + (c_ref[here].astype(f32) + d_ref[here].astype(f32))
        held[here] = total.astype(bf16)

        @pl.when(j < count)
        def _():
            copy(j).start()

    for j in range(MAXL):

        @pl.when(j < count)
        def _():
            copy(j).wait()


def turn_body(q_ref, g_ref, qt_ref, gt_ref):
    rows = qt_ref.shape[1]
    for at in range(0, rows, 256):
        here = slice(at, at + 256)
        part = slice(at // 16, at // 16 + 16)
        q = q_ref[part].reshape(256, WIDE)
        qt_ref[:LAT, here] = q[:, :LAT].T
        rope = jnp.concatenate([q[:, LAT:], q[:, LAT:]], axis=1)
        qt_ref[LAT:, here] = rope.T[: WIDE - LAT]
        gt_ref[:, here] = g_ref[part].reshape(256, LAT).T


def two_body(near_ref, far_ref, low_ref, high_ref):
    half = low_ref.shape[0]
    total = near_ref[...].astype(f32) + far_ref[...].astype(f32)
    low_ref[...] = total[:half].astype(bf16)
    high_ref[...] = total[half:].astype(bf16)


def one_body(near_ref, far_ref, low_ref, high_ref, left_ref, right_ref):
    size = left_ref.shape[0]
    half = size // 2
    total = near_ref[...].astype(f32) + far_ref[...].astype(f32)
    left_ref[:half] = total[:half].astype(bf16)
    left_ref[half:] = (total[half:size] + high_ref[...].astype(f32)).astype(bf16)
    right_ref[:half] = (total[size : size + half] + low_ref[...].astype(f32)).astype(bf16)
    right_ref[half:] = total[size + half :].astype(bf16)


ONCHIP = pl.BlockSpec(memory_space=pltpu.VMEM)
INPLACE = pl.BlockSpec(memory_space=pltpu.HBM)


def call(body, outs, scalars, arrays, scratch=(), direct_in=(), direct=(), alias=None, flops=None, anywhere=()):
    args = [
        a
        if i in anywhere
        else pltpu.with_memory_space_constraint(a, pltpu.HBM if i in direct_in else pltpu.VMEM)
        for i, a in enumerate(arrays)
    ]
    scalars = [pltpu.with_memory_space_constraint(a, pltpu.HBM) for a in scalars]
    shapes = [(pltpu.HBM if i in direct else pltpu.VMEM)(o.shape, o.dtype) for i, o in enumerate(outs)]
    return pl.pallas_call(
        body,
        in_specs=[pl.BlockSpec(memory_space=pltpu.SMEM)] * len(scalars)
        + [
            pl.BlockSpec(memory_space=pl.ANY) if i in anywhere else INPLACE if i in direct_in else ONCHIP
            for i in range(len(arrays))
        ],
        out_specs=tuple(INPLACE if i in direct else ONCHIP for i in range(len(outs))),
        out_shape=tuple(shapes),
        scratch_shapes=list(scratch),
        input_output_aliases=alias or {},
        cost_estimate=flops and pl.CostEstimate(flops=flops, transcendentals=0, bytes_accessed=0),
        compiler_params=pltpu.CompilerParams(vmem_limit_bytes=16 * 1024 * 1024),
    )(*scalars, *args)


def forward_body(nkeys, chunk, off, n, block, *refs):
    refs = list(refs)
    last = chunk == 2
    key_refs = [refs.pop(0) for _ in range(nkeys)]
    bias, q_ref, g_ref = refs[:3]
    refs = refs[3 + (4 if chunk else 0) :]
    turned = []
    if last:
        (qt_in, gt_in), refs = refs[:2], refs[2:]
    (e_out, p_out, k_out, st_out), refs = refs[:4], refs[4:]
    if last:
        qt_out, gt_out, sems = refs
        turned = [
            pltpu.make_async_copy(qt_in, qt_out, sems.at[0]),
            pltpu.make_async_copy(gt_in, gt_out, sems.at[1]),
        ]
    for copy in turned:
        copy.start()
    at = off
    for ref in key_refs:
        k_out[at : at + ref.shape[0]] = ref[...]
        at += ref.shape[0]
    mine = slice(off, off + n)

    def rows(i, carry):
        here = pl.ds(pl.multiple_of(i * block, block), block)
        part = pl.ds(i * (block // 16), block // 16)
        scores = dot(q_ref[part].reshape(block, WIDE), k_out[mine], NT) + bias[...]
        top = jnp.max(scores, axis=1, keepdims=True)
        expo = jnp.exp2((scores - top) * EXPC)
        grads = dot(g_ref[part].reshape(block, LAT), k_out[mine, :LAT], NT)
        e_out[here, mine] = expo.astype(bf16)
        p_out[here, mine] = grads.astype(bf16)
        wide = lambda x: jnp.broadcast_to(x, (block, 128))
        st_out[chunk, here] = wide(top)
        st_out[3 + chunk, here] = wide(jnp.sum(expo, axis=1, keepdims=True))
        st_out[6 + chunk, here] = wide(jnp.sum(expo * grads, axis=1, keepdims=True))
        return carry

    lax.fori_loop(0, q_ref.shape[0] * 16 // block, rows, 0)
    for copy in turned:
        copy.wait()


def forward(chunk, off, n, total_keys, key_parts, bias, q, g, state=(), turned=(), block=768):
    rows = q.shape[0] * 16
    side = jax.ShapeDtypeStruct((rows, total_keys), bf16)
    outs = [side, side, jax.ShapeDtypeStruct((total_keys, WIDE), bf16), jax.ShapeDtypeStruct((9, rows, 128), f32)]
    outs += [jax.ShapeDtypeStruct(t.shape, t.dtype) for t in turned]
    arrays = [*key_parts, bias, q, g, *state, *turned]
    start = len(key_parts) + 3
    return call(
        functools.partial(forward_body, len(key_parts), chunk, off, n, block),
        outs,
        (),
        arrays,
        scratch=[pltpu.SemaphoreType.DMA((2,))] if turned else [],
        direct_in=range(len(arrays) - len(turned), len(arrays)),
        alias={start + i: i for i in range(len(state))},
        flops=2 * rows * n * (WIDE + LAT),
    )


def backward_body(chunk, off, n, early, step, tile, *refs):
    refs = list(refs)
    lead, final = chunk == 2, chunk == 0
    qt_ref, gt_ref, e_ref, p_ref, row_ref, k_ref = refs[:6]
    far_out, near_out, e_out, p_out, row_out, _, s_out = refs[6:13]
    held, sems = refs[-2:]
    rows = qt_ref.shape[1]
    half = n // 2
    if final:
        kept, sem = refs[13], refs[14]
        save = pltpu.make_async_copy(k_ref, kept, sem.at[0])
        save.start()
    if lead:
        for at in range(0, rows, step):
            here = slice(at, at + step)
            col = lambda c: row_ref[c, here]
            top = jnp.maximum(jnp.maximum(col(0), col(1)), col(2))
            fade = [jnp.exp2((col(c) - top) * EXPC) for c in range(3)]
            total = fade[0] * col(3) + fade[1] * col(4) + fade[2] * col(5)
            rdot = fade[0] * col(6) + fade[1] * col(7) + fade[2] * col(8)
            total = 1.0 / total
            for c in range(3):
                row_out[c, here] = fade[c] * total
            row_out[3, here] = rdot * total
    copies = []
    for start in range(0, n, tile):
        local = slice((start + half) % n, (start + half) % n + tile)
        cols = slice(off + local.start, off + local.stop)
        acc = None
        for at in range(0, rows, step):
            here = slice(at, at + step)
            a = jnp.tile(row_out[chunk, here], (1, tile // 128))
            r = jnp.tile(row_out[3, here], (1, tile // 128))
            weights = (e_ref[here, cols].astype(f32) * a).astype(bf16)
            sg = (weights.astype(f32) * (p_ref[here, cols].astype(f32) - r) * SCALE).astype(bf16)
            e_out[here, cols] = weights
            if at < early:
                p_out[here, cols] = sg
            else:
                held[local.start // tile, at - early : at - early + step] = sg
            key_part = dot(qt_ref[:, here], sg)
            value_part = dot(gt_ref[:, here], weights)
            if acc is None:
                acc = [key_part[:LAT] + value_part, key_part[LAT:]]
            else:
                acc = [acc[0] + (key_part[:LAT] + value_part), acc[1] + key_part[LAT:]]
        spot = local.start // tile
        copy = pltpu.make_async_copy(held.at[spot], s_out.at[spot], sems.at[spot])
        copy.start()
        copies.append(copy)
        top = acc[0].T.astype(bf16)
        low = jnp.concatenate([acc[1], jnp.zeros_like(acc[1])], axis=0).T[:, : WIDE - LAT].astype(bf16)
        ref = far_out if start < half else near_out
        put = slice(start % half, start % half + tile)
        ref[put, :LAT] = top
        ref[put, LAT:] = low
    for copy in copies:
        copy.wait()
    if final:
        save.wait()


def backward(chunk, off, n, early, qt, gt, e, p, row, k, tile=256, step=256):
    rows = e.shape[0]
    lead, final = chunk == 2, chunk == 0
    like = lambda a: jax.ShapeDtypeStruct(a.shape, a.dtype)
    part = jax.ShapeDtypeStruct((n // 2, WIDE), bf16)
    merged = jax.ShapeDtypeStruct((4, rows, 128), f32) if lead else like(row)
    late = (n // tile, rows - early, tile)
    outs = [part, part, like(e), like(p), merged, like(k), jax.ShapeDtypeStruct(late, bf16)]
    alias = {2: 2, 3: 3, 5: 5}
    scratch = [pltpu.VMEM(late, bf16), pltpu.SemaphoreType.DMA((n // tile,))]
    direct = (6,)
    if not lead:
        alias[4] = 4
    if final:
        outs.append(like(k))
        direct = (6, 7)
        scratch = [pltpu.SemaphoreType.DMA((1,)), *scratch]
    return call(
        functools.partial(backward_body, chunk, off, n, early, step, tile),
        outs,
        (),
        (qt, gt, e, p, row, k),
        scratch=scratch,
        alias=alias,
        direct=direct,
        flops=2 * rows * n * (WIDE + LAT),
    )


def leaving(held, out_ref, sems, block):
    def copy(i):
        part = pl.ds(i * (block // 16), block // 16)
        return pltpu.make_async_copy(held.at[part], out_ref.at[part], sems.at[i])

    return copy


def value_body(block, early, w_ref, s_ref, k_ref, out_ref, q_ref, held, held_q, sems, sems_q):
    steps = out_ref.shape[0] * 16 // block
    leave = leaving(held, out_ref, sems, block)
    leave_q = leaving(held_q, q_ref, sems_q, block)
    for i in range(early // block):
        here = slice(i * block, i * block + block)
        part = slice(i * (block // 16), (i + 1) * (block // 16))
        held_q[part] = dot(s_ref[here], k_ref[...]).astype(bf16).reshape(block // 16, 16, WIDE)
        leave_q(i).start()

    def rows(i, carry):
        here = pl.ds(pl.multiple_of(i * block, block), block)
        part = pl.ds(i * (block // 16), block // 16)
        held[part] = dot(w_ref[here], k_ref[:, :LAT]).astype(bf16).reshape(block // 16, 16, LAT)
        leave(i).start()
        return carry

    lax.fori_loop(0, steps, rows, 0)
    for i in range(early // block):
        leave_q(i).wait()
    for i in range(steps):
        leave(i).wait()


def value_side(w, s, k, early, block=512):
    rows = w.shape[0]
    shape = (rows // 16, 16, LAT)
    dma = lambda n: pltpu.SemaphoreType.DMA((n,))
    return call(
        functools.partial(value_body, block, early),
        (jax.ShapeDtypeStruct(shape, bf16), jax.ShapeDtypeStruct((rows // 16, 16, WIDE), bf16)),
        (),
        (w, s, k),
        scratch=[
            pltpu.VMEM(shape, bf16),
            pltpu.VMEM((early // 16, 16, WIDE), bf16),
            dma(rows // block),
            dma(early // block),
        ],
        direct=(0, 1),
        flops=2 * k.shape[0] * (rows * LAT + early * WIDE),
    )


def query_body(offs, early, block, *refs):
    s_refs, (k_ref, _, out_ref, s_v, k_v, held, sems_k, sems_s, sems) = refs[: len(offs)], refs[len(offs) :]
    steps = s_v.shape[1] // block
    load_k = pltpu.make_async_copy(k_ref, k_v, sems_k.at[0])
    load_k.start()
    loads = []
    for i in range(steps):
        here = slice(i * block, i * block + block)
        loads.append(
            [
                pltpu.make_async_copy(ref.at[t, here], s_v.at[off + t, here], sems_s.at[i * s_v.shape[0] + off + t])
                for ref, off in zip(s_refs, offs)
                for t in range(ref.shape[0])
            ]
        )
        for copy in loads[-1]:
            copy.start()
    load_k.wait()
    leave = []
    for i in range(steps):
        for copy in loads[i]:
            copy.wait()
        here = slice(i * block, i * block + block)
        part = slice(i * (block // 16), (i + 1) * (block // 16))
        to = slice(early // 16 + part.start, early // 16 + part.stop)
        sg = jnp.concatenate([s_v[t, here] for t in range(s_v.shape[0])], axis=1)
        held[part] = dot(sg, k_v[...]).astype(bf16).reshape(block // 16, 16, WIDE)
        leave.append(pltpu.make_async_copy(held.at[part], out_ref.at[to], sems.at[i]))
        leave[-1].start()
    for copy in leave:
        copy.wait()


def query_side(sgs, offs, early, k, out, block=512):
    tile, rows = sgs[0].shape[2], sgs[0].shape[1]
    dma = lambda n: pltpu.SemaphoreType.DMA((n,))
    steps, tiles = rows // block, k.shape[0] // tile
    return call(
        functools.partial(query_body, [off // tile for off in offs], early, block),
        (jax.ShapeDtypeStruct(out.shape, bf16),),
        (),
        (*sgs, k, out),
        scratch=[
            pltpu.VMEM((tiles, rows, tile), bf16),
            pltpu.VMEM(k.shape, bf16),
            pltpu.VMEM((rows // 16, 16, WIDE), bf16),
            dma(1),
            dma(steps * tiles),
            dma(steps),
        ],
        direct_in=range(len(sgs) + 2),
        direct=(0,),
        alias={len(sgs) + 1: 0},
        flops=2 * rows * k.shape[0] * WIDE,
    )[0]


def per_device(queries, out_grad, latents, list_blocks, list_counts, valid_tokens):
    me = lax.axis_index("req")
    head = lax.axis_index("head")
    chip, core = head // 2, head % 2
    tokens = latents.shape[1]
    shift = lambda d: [(x * 2 + c, ((x + d) % 4) * 2 + c) for x in range(4) for c in range(2)]
    right, left, sibling = shift(1), shift(-1), [(h, h ^ 1) for h in range(8)]
    send = lambda a, perm: lax.ppermute(a, "head", perm)
    scalars = (list_blocks, list_counts, me.reshape(1).astype(jnp.int32))

    smem = lambda n: pltpu.SMEM((n,), jnp.int32)
    slots = jax.ShapeDtypeStruct((SLOTS, tokens, WIDE), bf16)
    keys = MAXL * tokens
    share_of = lambda n: jax.ShapeDtypeStruct((n, WIDE), bf16)

    dma = lambda n: pltpu.SemaphoreType.DMA((n,))
    (outgoing,) = call(
        pick_body,
        (slots,),
        scalars,
        (latents,),
        scratch=[
            smem(SLOTS + 1),
            pltpu.VMEM(latents.shape, bf16),
            pltpu.VMEM((SLOTS, tokens, WIDE), bf16),
            dma(1),
            dma(4),
        ],
        direct_in=(0,),
        direct=(0,),
    )
    arrived = lax.all_to_all(outgoing.reshape(16, CAP, tokens, WIDE), "req", 0, 0, tiled=True)

    my_blocks = lax.dynamic_index_in_dim(list_blocks, me, 0, keepdims=False)
    my_count = lax.dynamic_index_in_dim(list_counts, me, 0, keepdims=False)
    ids = jnp.arange(valid_tokens.shape[0], dtype=jnp.int32)
    filled = jnp.sum(jnp.where(my_blocks[:, None] == ids[None, :], valid_tokens[None, :], 0), axis=1)
    filled = jnp.where(jnp.arange(MAXL, dtype=jnp.int32) < my_count, filled, 0)
    filled = jnp.repeat(filled, tokens)[None, :]
    offset = jnp.tile(jnp.arange(tokens, dtype=jnp.int32), MAXL)[None, :]
    at = lambda d, c: ((chip + d) % 4) * 2 + c
    other = 1 - core
    places = [at(0, core), at(0, other), at(3, core), at(1, core), at(3, other), at(1, other), at(2, core), at(2, other)]
    first_token = jnp.stack(places)[:, None] * tokens
    bias = jnp.where(first_token + offset < filled, 0.0, BIG).astype(f32)
    bias0, bias1, bias2 = [bias[i:j].reshape(1, -1) for i, j in ((0, 2), (2, 6), (6, 8))]

    flat = lambda a: jax.ShapeDtypeStruct((a.shape[2], a.shape[0] * a.shape[1]), bf16)
    qt, gt = call(turn_body, (flat(queries), flat(out_grad)), (), (queries, out_grad))
    arrived, qt, gt, bias0, bias1, bias2 = lax.optimization_barrier((arrived, qt, gt, bias0, bias1, bias2))

    (share,) = call(
        take_body,
        (share_of(keys),),
        scalars,
        (arrived.reshape(slots.shape),),
        scratch=[smem(MAXL), smem(16), dma(MAXL)],
        direct_in=(0,),
    )

    after = lambda a, *others: lax.optimization_barrier((a, *others))[0]
    q, g = queries, out_grad
    every = 8 * keys
    r1 = send(share, right)
    l1 = send(share, left)
    s0 = send(share, sibling)
    state = forward(0, 0, 2 * keys, every, [share, s0], bias0, q, g)
    r1 = after(r1, state[3])
    l1 = after(l1, state[3])
    r2 = send(r1, right)
    s1 = send(r1, sibling)
    s2 = send(l1, sibling)
    state = forward(1, 2 * keys, 4 * keys, every, [r1, l1, s1, s2], bias1, q, g, state)
    r2 = after(r2, state[3])
    s3 = send(r2, sibling)
    e, p, k, row, qt, gt = forward(2, 6 * keys, 2 * keys, every, [r2, s3], bias2, q, g, state, (qt, gt))

    fold = lambda a: a.reshape(-1, tokens, WIDE)
    unfold = lambda a: a.reshape(-1, WIDE)
    early = 512
    far2, near2, e, p, row, k, sg2 = backward(2, 6 * keys, 2 * keys, early, qt, gt, e, p, row, k)
    mate2 = send(far2, sibling)
    far1, near1, e, p, row, k, sg1 = backward(1, 2 * keys, 4 * keys, early, qt, gt, e, p, row, k)
    mate1 = unfold(send(fold(far1), sibling))
    low, high = call(two_body, (share_of(keys // 2),) * 2, (), (after(near2, near1), mate2))
    from_left = send(low, right)
    from_right = send(high, left)
    far0, near0, e, p, row, k, sg0, k_saved = backward(
        0, 0, 2 * keys, early, qt, gt, e, p, after(row, low), k
    )
    mate0 = send(far0, sibling)
    to_left, to_right = call(
        one_body, (share_of(keys),) * 2, (), (after(near1, near0), mate1, from_left, from_right)
    )
    got_left = send(to_right, right)
    got_right = send(to_left, left)
    attended, query_grad = value_side(e, p, after(k, to_left), early)
    near0 = after(near0, attended)
    (slot_grads,) = call(
        put_body,
        (slots,),
        scalars,
        (near0, mate0, got_left, got_right),
        scratch=[smem(MAXL), smem(16), pltpu.VMEM((keys, WIDE), bf16), dma(MAXL)],
        direct=(0,),
    )
    k_saved = after(k_saved, slot_grads)
    query_grad = query_side((sg2, sg1, sg0), (6 * keys, 2 * keys, 0), early, k_saved, query_grad)
    returned = lax.all_to_all(slot_grads.reshape(16, CAP, tokens, WIDE), "req", 0, 0, tiled=True)
    (latent_grad,) = call(
        gather_body,
        (jax.ShapeDtypeStruct((16, tokens, WIDE), f32),),
        scalars,
        (returned.reshape(slots.shape),),
        scratch=[
            smem(SLOTS + 1),
            pltpu.VMEM((SLOTS, tokens, WIDE), bf16),
            pltpu.VMEM((17, tokens, WIDE), f32),
            dma(4),
            dma(4),
        ],
        anywhere=(0,),
        direct=(0,),
    )
    return (attended, query_grad, latent_grad)


def solution(mesh):
    in_specs = (
        P("req", "head", None),
        P("req", "head", None),
        P("req", "head", None),
        P(),
        P(),
        P(),
    )
    out_specs = (P("req", "head", None), P("req", "head", None), P("req", "head", None))
    return jax.shard_map(per_device, mesh=mesh, in_specs=in_specs, out_specs=out_specs, check_vma=False)
```

```python
import functools
import math

import jax
import jax.numpy as jnp
from jax import lax
from jax.experimental import pallas as pl
from jax.experimental.pallas import tpu as pltpu
from jax.sharding import PartitionSpec as P


LAT = 512
WIDE = 576
MAXL = 16
CAP = 2
BIG = -1e30
SLOTS = 16 * CAP
SCALE = 192.0 ** (-0.5)
EXPC = SCALE * math.log2(math.e)
NT = (((1,), (1,)), ((), ()))
NN = (((1,), (0,)), ((), ()))
f32 = jnp.float32
bf16 = jnp.bfloat16


def dot(a, b, dims=NN):
    return lax.dot_general(a, b, dims, preferred_element_type=f32)


def owner_table(lists, counts, own, table, empty):
    def group(g, carry):
        table[g * CAP] = empty
        table[g * CAP + 1] = empty
        rank = jnp.int32(0)
        for j in range(MAXL):
            block = lists[g, j]
            mine = ((block >> 4) == own) & (j < counts[g])
            table[jnp.where(mine, g * CAP + rank, SLOTS)] = block & 15
            rank = jnp.where(mine, jnp.minimum(rank + 1, CAP - 1), rank)
        return carry

    lax.fori_loop(0, 16, group, 0)


def slot_table(lists, own, table, seen):
    for o in range(16):
        seen[o] = 0
    for j in range(MAXL):
        owner = lists[own, j] >> 4
        rank = seen[owner]
        seen[owner] = jnp.minimum(rank + 1, CAP - 1)
        table[j] = owner * CAP + rank


def pick_body(lists, counts, me, lat_ref, out_ref, table, lat, held, sem, sems):
    load = pltpu.make_async_copy(lat_ref, lat, sem.at[0])
    load.start()
    owner_table(lists, counts, me[0], table, 16)
    load.wait()
    step = SLOTS // 4
    parts = [slice(i * step, i * step + step) for i in range(4)]
    copies = [pltpu.make_async_copy(held.at[p], out_ref.at[p], sems.at[i]) for i, p in enumerate(parts)]
    for s in range(SLOTS):
        held[s] = lat[table[s] & 15]
        if s % step == step - 1:
            copies[s // step].start()
    for copy in copies:
        copy.wait()


def gather_body(table, arrived_ref, out_ref, total, sems):
    total[...] = jnp.zeros(total.shape, total.dtype)
    for s in range(SLOTS):
        total[table[s]] = total[table[s]] + arrived_ref[s].astype(f32)
    parts = [slice(i * 4, i * 4 + 4) for i in range(4)]
    copies = [pltpu.make_async_copy(total.at[p], out_ref.at[p], sems.at[i]) for i, p in enumerate(parts)]
    for copy in copies:
        copy.start()
    for copy in copies:
        copy.wait()


def take_body(lists, counts, me, arrived_ref, out_ref, table, seen):
    slot_table(lists, me[0], table, seen)
    count = counts[me[0]]
    for j in range(MAXL):
        live = j < count

        @pl.when(live)
        def _():
            out_ref[j * 16 : j * 16 + 16] = arrived_ref[table[j]]

        @pl.when(jnp.logical_not(live))
        def _():
            out_ref[j * 16 : j * 16 + 16] = jnp.zeros((16, WIDE), bf16)


def put_body(lists, counts, me, a_ref, b_ref, c_ref, d_ref, out_ref, table, seen, held, sems):
    slot_table(lists, me[0], table, seen)
    count = counts[me[0]]

    def copy(j):
        return pltpu.make_async_copy(held.at[j * 16 : j * 16 + 16], out_ref.at[table[j]], sems.at[j])

    for j in range(MAXL):
        here = slice(j * 16, j * 16 + 16)
        total = a_ref[here].astype(f32) + b_ref[here].astype(f32)
        total = total + (c_ref[here].astype(f32) + d_ref[here].astype(f32))
        held[here] = total.astype(bf16)

        @pl.when(j < count)
        def _():
            copy(j).start()

    for j in range(MAXL):

        @pl.when(j < count)
        def _():
            copy(j).wait()


def turn_body(q_ref, g_ref, qt_ref, gt_ref):
    rows = qt_ref.shape[1]
    for at in range(0, rows, 256):
        here = slice(at, at + 256)
        part = slice(at // 16, at // 16 + 16)
        q = q_ref[part].reshape(256, WIDE)
        qt_ref[:LAT, here] = q[:, :LAT].T
        rope = jnp.concatenate([q[:, LAT:], q[:, LAT:]], axis=1)
        qt_ref[LAT:, here] = rope.T[: WIDE - LAT]
        gt_ref[:, here] = g_ref[part].reshape(256, LAT).T


def two_body(near_ref, far_ref, low_ref, high_ref):
    half = low_ref.shape[0]
    total = near_ref[...].astype(f32) + far_ref[...].astype(f32)
    low_ref[...] = total[:half].astype(bf16)
    high_ref[...] = total[half:].astype(bf16)


def one_body(near_ref, far_ref, low_ref, high_ref, left_ref, right_ref):
    size = left_ref.shape[0]
    half = size // 2
    total = near_ref[...].astype(f32) + far_ref[...].astype(f32)
    left_ref[:half] = total[:half].astype(bf16)
    left_ref[half:] = (total[half:size] + high_ref[...].astype(f32)).astype(bf16)
    right_ref[:half] = (total[size : size + half] + low_ref[...].astype(f32)).astype(bf16)
    right_ref[half:] = total[size + half :].astype(bf16)


ONCHIP = pl.BlockSpec(memory_space=pltpu.VMEM)
INPLACE = pl.BlockSpec(memory_space=pltpu.HBM)


def call(body, outs, scalars, arrays, scratch=(), direct_in=(), direct=(), alias=None, flops=None, smem_out=()):
    args = [
        pltpu.with_memory_space_constraint(a, pltpu.HBM if i in direct_in else pltpu.VMEM)
        for i, a in enumerate(arrays)
    ]
    scalars = [pltpu.with_memory_space_constraint(a, pltpu.HBM) for a in scalars]
    shapes = [
        o if i in smem_out else (pltpu.HBM if i in direct else pltpu.VMEM)(o.shape, o.dtype)
        for i, o in enumerate(outs)
    ]
    small = pl.BlockSpec(memory_space=pltpu.SMEM)
    return pl.pallas_call(
        body,
        in_specs=[small] * len(scalars)
        + [INPLACE if i in direct_in else ONCHIP for i in range(len(arrays))],
        out_specs=tuple(small if i in smem_out else INPLACE if i in direct else ONCHIP for i in range(len(outs))),
        out_shape=tuple(shapes),
        scratch_shapes=list(scratch),
        input_output_aliases=alias or {},
        cost_estimate=flops and pl.CostEstimate(flops=flops, transcendentals=0, bytes_accessed=0),
        compiler_params=pltpu.CompilerParams(vmem_limit_bytes=16 * 1024 * 1024),
    )(*scalars, *args)


def forward_body(nkeys, chunk, off, n, block, *refs):
    refs = list(refs)
    last = chunk == 2
    key_refs = [refs.pop(0) for _ in range(nkeys)]
    bias, q_ref, g_ref = refs[:3]
    refs = refs[3 + (4 if chunk else 0) :]
    turned = []
    if last:
        (qt_in, gt_in), refs = refs[:2], refs[2:]
    (e_out, p_out, k_out, st_out), refs = refs[:4], refs[4:]
    if last:
        qt_out, gt_out, sems = refs
        turned = [
            pltpu.make_async_copy(qt_in, qt_out, sems.at[0]),
            pltpu.make_async_copy(gt_in, gt_out, sems.at[1]),
        ]
    for copy in turned:
        copy.start()
    at = off
    for ref in key_refs:
        k_out[at : at + ref.shape[0]] = ref[...]
        at += ref.shape[0]
    mine = slice(off, off + n)

    def rows(i, carry):
        here = pl.ds(pl.multiple_of(i * block, block), block)
        part = pl.ds(i * (block // 16), block // 16)
        scores = dot(q_ref[part].reshape(block, WIDE), k_out[mine], NT) + bias[...]
        top = jnp.max(scores, axis=1, keepdims=True)
        expo = jnp.exp2((scores - top) * EXPC)
        grads = dot(g_ref[part].reshape(block, LAT), k_out[mine, :LAT], NT)
        e_out[here, mine] = expo.astype(bf16)
        p_out[here, mine] = grads.astype(bf16)
        wide = lambda x: jnp.broadcast_to(x, (block, 128))
        st_out[chunk, here] = wide(top)
        st_out[3 + chunk, here] = wide(jnp.sum(expo, axis=1, keepdims=True))
        st_out[6 + chunk, here] = wide(jnp.sum(expo * grads, axis=1, keepdims=True))
        return carry

    lax.fori_loop(0, q_ref.shape[0] * 16 // block, rows, 0)
    for copy in turned:
        copy.wait()


def forward(chunk, off, n, total_keys, key_parts, bias, q, g, state=(), turned=(), block=768):
    rows = q.shape[0] * 16
    side = jax.ShapeDtypeStruct((rows, total_keys), bf16)
    outs = [side, side, jax.ShapeDtypeStruct((total_keys, WIDE), bf16), jax.ShapeDtypeStruct((9, rows, 128), f32)]
    outs += [jax.ShapeDtypeStruct(t.shape, t.dtype) for t in turned]
    arrays = [*key_parts, bias, q, g, *state, *turned]
    start = len(key_parts) + 3
    return call(
        functools.partial(forward_body, len(key_parts), chunk, off, n, block),
        outs,
        (),
        arrays,
        scratch=[pltpu.SemaphoreType.DMA((2,))] if turned else [],
        direct_in=range(len(arrays) - len(turned), len(arrays)),
        alias={start + i: i for i in range(len(state))},
        flops=2 * rows * n * (WIDE + LAT),
    )


def backward_body(chunk, offs, n, lead, final, early, step, tile, *refs):
    refs = list(refs)
    qt_ref, gt_ref, e_ref, p_ref, row_ref, k_ref = refs[:6]
    parts, refs = refs[6 : 6 + len(offs)], refs[6 + len(offs) :]
    e_out, p_out, row_out, _, s_out = refs[:5]
    held, sems = refs[-2:]
    rows = qt_ref.shape[1]
    if final:
        kept, sem = refs[5], refs[6]
        save = pltpu.make_async_copy(k_ref, kept, sem.at[0])
        save.start()
    if lead:
        for at in range(0, rows, step):
            here = slice(at, at + step)
            col = lambda c: row_ref[c, here]
            top = jnp.maximum(jnp.maximum(col(0), col(1)), col(2))
            fade = [jnp.exp2((col(c) - top) * EXPC) for c in range(3)]
            total = fade[0] * col(3) + fade[1] * col(4) + fade[2] * col(5)
            rdot = fade[0] * col(6) + fade[1] * col(7) + fade[2] * col(8)
            total = 1.0 / total
            for c in range(3):
                row_out[c, here] = fade[c] * total
            row_out[3, here] = rdot * total
    copies = []
    for ref, off in zip(parts, offs):
        for start in range(0, n, tile):
            cols = slice(off + start, off + start + tile)
            spot = len(copies)
            acc = None
            for at in range(0, rows, step):
                here = slice(at, at + step)
                a = jnp.tile(row_out[chunk, here], (1, tile // 128))
                r = jnp.tile(row_out[3, here], (1, tile // 128))
                weights = (e_ref[here, cols].astype(f32) * a).astype(bf16)
                sg = (weights.astype(f32) * (p_ref[here, cols].astype(f32) - r) * SCALE).astype(bf16)
                e_out[here, cols] = weights
                if at < early:
                    p_out[here, cols] = sg
                else:
                    held[spot, at - early : at - early + step] = sg
                key_part = dot(qt_ref[:, here], sg)
                value_part = dot(gt_ref[:, here], weights)
                if acc is None:
                    acc = [key_part[:LAT] + value_part, key_part[LAT:]]
                else:
                    acc = [acc[0] + (key_part[:LAT] + value_part), acc[1] + key_part[LAT:]]
            copies.append(pltpu.make_async_copy(held.at[spot], s_out.at[spot], sems.at[spot]))
            copies[-1].start()
            ref[start : start + tile, :LAT] = acc[0].T.astype(bf16)
            low = jnp.concatenate([acc[1], jnp.zeros_like(acc[1])], axis=0).T[:, : WIDE - LAT]
            ref[start : start + tile, LAT:] = low.astype(bf16)
    for copy in copies:
        copy.wait()
    if final:
        save.wait()


def backward(chunk, offs, n, early, qt, gt, e, p, row, k, lead=False, final=False, tile=256, step=256):
    rows = e.shape[0]
    count = len(offs)
    like = lambda a: jax.ShapeDtypeStruct(a.shape, a.dtype)
    part = jax.ShapeDtypeStruct((n, WIDE), bf16)
    merged = jax.ShapeDtypeStruct((4, rows, 128), f32) if lead else like(row)
    late = (count * n // tile, rows - early, tile)
    outs = [part] * count + [like(e), like(p), merged, like(k), jax.ShapeDtypeStruct(late, bf16)]
    alias = {2: count, 3: count + 1, 5: count + 3}
    scratch = [pltpu.VMEM(late, bf16), pltpu.SemaphoreType.DMA((late[0],))]
    direct = (count + 4,)
    if not lead:
        alias[4] = count + 2
    if final:
        outs.append(like(k))
        direct = (count + 4, count + 5)
        scratch = [pltpu.SemaphoreType.DMA((1,)), *scratch]
    return call(
        functools.partial(backward_body, chunk, offs, n, lead, final, early, step, tile),
        outs,
        (),
        (qt, gt, e, p, row, k),
        scratch=scratch,
        alias=alias,
        direct=direct,
        flops=2 * rows * n * count * (WIDE + LAT),
    )


def leaving(held, out_ref, sems, block):
    def copy(i):
        part = pl.ds(i * (block // 16), block // 16)
        return pltpu.make_async_copy(held.at[part], out_ref.at[part], sems.at[i])

    return copy


def value_body(block, early, w_ref, s_ref, k_ref, out_ref, q_ref, held, held_q, sems, sems_q):
    steps = out_ref.shape[0] * 16 // block
    leave = leaving(held, out_ref, sems, block)
    leave_q = leaving(held_q, q_ref, sems_q, block)
    for i in range(early // block):
        here = slice(i * block, i * block + block)
        part = slice(i * (block // 16), (i + 1) * (block // 16))
        held_q[part] = dot(s_ref[here], k_ref[...]).astype(bf16).reshape(block // 16, 16, WIDE)
        leave_q(i).start()

    def rows(i, carry):
        here = pl.ds(pl.multiple_of(i * block, block), block)
        part = pl.ds(i * (block // 16), block // 16)
        held[part] = dot(w_ref[here], k_ref[:, :LAT]).astype(bf16).reshape(block // 16, 16, LAT)
        leave(i).start()
        return carry

    lax.fori_loop(0, steps, rows, 0)
    for i in range(early // block):
        leave_q(i).wait()
    for i in range(steps):
        leave(i).wait()


def value_side(w, s, k, early, block=512):
    rows = w.shape[0]
    shape = (rows // 16, 16, LAT)
    dma = lambda n: pltpu.SemaphoreType.DMA((n,))
    return call(
        functools.partial(value_body, block, early),
        (jax.ShapeDtypeStruct(shape, bf16), jax.ShapeDtypeStruct((rows // 16, 16, WIDE), bf16)),
        (),
        (w, s, k),
        scratch=[
            pltpu.VMEM(shape, bf16),
            pltpu.VMEM((early // 16, 16, WIDE), bf16),
            dma(rows // block),
            dma(early // block),
        ],
        direct=(0, 1),
        flops=2 * k.shape[0] * (rows * LAT + early * WIDE),
    )


def query_body(offs, early, block, *refs):
    s_refs, (k_ref, _, out_ref, s_v, k_v, held, sems_k, sems_s, sems) = refs[: len(offs)], refs[len(offs) :]
    steps = s_v.shape[1] // block
    load_k = pltpu.make_async_copy(k_ref, k_v, sems_k.at[0])
    load_k.start()
    loads = []
    for i in range(steps):
        here = slice(i * block, i * block + block)
        loads.append(
            [
                pltpu.make_async_copy(ref.at[t, here], s_v.at[spot, here], sems_s.at[i * s_v.shape[0] + spot])
                for ref, spots in zip(s_refs, offs)
                for t, spot in enumerate(spots)
            ]
        )
        for copy in loads[-1]:
            copy.start()
    load_k.wait()
    leave = []
    for i in range(steps):
        for copy in loads[i]:
            copy.wait()
        here = slice(i * block, i * block + block)
        part = slice(i * (block // 16), (i + 1) * (block // 16))
        to = slice(early // 16 + part.start, early // 16 + part.stop)
        sg = jnp.concatenate([s_v[t, here] for t in range(s_v.shape[0])], axis=1)
        held[part] = dot(sg, k_v[...]).astype(bf16).reshape(block // 16, 16, WIDE)
        leave.append(pltpu.make_async_copy(held.at[part], out_ref.at[to], sems.at[i]))
        leave[-1].start()
    for copy in leave:
        copy.wait()


def query_side(sgs, offs, early, k, out, block=512):
    tile, rows = sgs[0].shape[2], sgs[0].shape[1]
    dma = lambda n: pltpu.SemaphoreType.DMA((n,))
    steps, tiles = rows // block, k.shape[0] // tile
    return call(
        functools.partial(query_body, [[off // tile for off in o] for o in offs], early, block),
        (jax.ShapeDtypeStruct(out.shape, bf16),),
        (),
        (*sgs, k, out),
        scratch=[
            pltpu.VMEM((tiles, rows, tile), bf16),
            pltpu.VMEM(k.shape, bf16),
            pltpu.VMEM((rows // 16, 16, WIDE), bf16),
            dma(1),
            dma(steps * tiles),
            dma(steps),
        ],
        direct_in=range(len(sgs) + 2),
        direct=(0,),
        alias={len(sgs) + 1: 0},
        flops=2 * rows * k.shape[0] * WIDE,
    )[0]


def per_device(queries, out_grad, latents, list_blocks, list_counts, valid_tokens):
    me = lax.axis_index("req")
    head = lax.axis_index("head")
    chip, core = head // 2, head % 2
    tokens = latents.shape[1]
    shift = lambda d: [(x * 2 + c, ((x + d) % 4) * 2 + c) for x in range(4) for c in range(2)]
    right, left, sibling = shift(1), shift(-1), [(h, h ^ 1) for h in range(8)]
    send = lambda a, perm: lax.ppermute(a, "head", perm)
    scalars = (list_blocks, list_counts, me.reshape(1).astype(jnp.int32))

    smem = lambda n: pltpu.SMEM((n,), jnp.int32)
    slots = jax.ShapeDtypeStruct((SLOTS, tokens, WIDE), bf16)
    keys = MAXL * tokens
    share_of = lambda n: jax.ShapeDtypeStruct((n, WIDE), bf16)

    dma = lambda n: pltpu.SemaphoreType.DMA((n,))
    outgoing, owned = call(
        pick_body,
        (slots, jax.ShapeDtypeStruct((SLOTS + 1,), jnp.int32)),
        scalars,
        (latents,),
        scratch=[
            pltpu.VMEM(latents.shape, bf16),
            pltpu.VMEM((SLOTS, tokens, WIDE), bf16),
            dma(1),
            dma(4),
        ],
        direct_in=(0,),
        direct=(0,),
        smem_out=(1,),
    )
    arrived = lax.all_to_all(outgoing.reshape(16, CAP, tokens, WIDE), "req", 0, 0, tiled=True)

    my_blocks = lax.dynamic_index_in_dim(list_blocks, me, 0, keepdims=False)
    my_count = lax.dynamic_index_in_dim(list_counts, me, 0, keepdims=False)
    ids = jnp.arange(valid_tokens.shape[0], dtype=jnp.int32)
    filled = jnp.sum(jnp.where(my_blocks[:, None] == ids[None, :], valid_tokens[None, :], 0), axis=1)
    filled = jnp.where(jnp.arange(MAXL, dtype=jnp.int32) < my_count, filled, 0)
    filled = jnp.repeat(filled, tokens)[None, :]
    offset = jnp.tile(jnp.arange(tokens, dtype=jnp.int32), MAXL)[None, :]
    at = lambda d, c: ((chip + d) % 4) * 2 + c
    other = 1 - core
    places = [at(0, core), at(0, other), at(3, core), at(1, core), at(3, other), at(1, other), at(2, core), at(2, other)]
    first_token = jnp.stack(places)[:, None] * tokens
    bias = jnp.where(first_token + offset < filled, 0.0, BIG).astype(f32)
    bias0, bias1, bias2 = [bias[i:j].reshape(1, -1) for i, j in ((0, 2), (2, 6), (6, 8))]

    flat = lambda a: jax.ShapeDtypeStruct((a.shape[2], a.shape[0] * a.shape[1]), bf16)
    qt, gt = call(turn_body, (flat(queries), flat(out_grad)), (), (queries, out_grad))
    arrived, qt, gt, bias0, bias1, bias2 = lax.optimization_barrier((arrived, qt, gt, bias0, bias1, bias2))

    (share,) = call(
        take_body,
        (share_of(keys),),
        scalars,
        (arrived.reshape(slots.shape),),
        scratch=[smem(MAXL), smem(16)],
    )

    after = lambda a, *others: lax.optimization_barrier((a, *others))[0]
    q, g = queries, out_grad
    every = 8 * keys
    r1 = send(share, right)
    l1 = send(share, left)
    s0 = send(share, sibling)
    state = forward(0, 0, 2 * keys, every, [share, s0], bias0, q, g)
    r1 = after(r1, state[3])
    l1 = after(l1, state[3])
    r2 = send(r1, right)
    s1 = send(r1, sibling)
    s2 = send(l1, sibling)
    state = forward(1, 2 * keys, 4 * keys, every, [r1, l1, s1, s2], bias1, q, g, state)
    r2 = after(r2, state[3])
    s3 = send(r2, sibling)
    e, p, k, row, qt, gt = forward(2, 6 * keys, 2 * keys, every, [r2, s3], bias2, q, g, state, (qt, gt))

    fold = lambda a: a.reshape(-1, tokens, WIDE)
    unfold = lambda a: a.reshape(-1, WIDE)
    early = 512
    back = functools.partial(backward, early=early, qt=qt, gt=gt)
    far2, near2, e, p, row, k, sg2 = back(2, (7 * keys, 6 * keys), keys, e=e, p=p, row=row, k=k, lead=True)
    mate2 = send(far2, sibling)
    far0, near0, e, p, row, k, sg0, k_saved = back(0, (keys, 0), keys, e=e, p=p, row=row, k=k, final=True)
    low, high = call(two_body, (share_of(keys // 2),) * 2, (), (after(near2, near0), mate2))
    from_left = send(low, right)
    from_right = send(high, left)
    far1, e, p, row, k, sg1f = back(1, (4 * keys,), 2 * keys, e=e, p=p, row=after(row, low), k=k)
    mate1 = unfold(send(fold(far1), sibling))
    near1, e, p, row, k, sg1n = back(1, (2 * keys,), 2 * keys, e=e, p=p, row=row, k=k)
    mate0 = send(far0, sibling)
    to_left, to_right = call(one_body, (share_of(keys),) * 2, (), (near1, mate1, from_left, from_right))
    got_left = send(to_right, right)
    got_right = send(to_left, left)
    attended, query_grad = value_side(e, p, after(k, to_left), early)
    near0 = after(near0, attended)
    (slot_grads,) = call(
        put_body,
        (slots,),
        scalars,
        (near0, mate0, got_left, got_right),
        scratch=[smem(MAXL), smem(16), pltpu.VMEM((keys, WIDE), bf16), dma(MAXL)],
        direct=(0,),
    )
    k_saved = after(k_saved, slot_grads)
    query_grad = query_side(
        (sg2, sg0, sg1f, sg1n),
        ((7 * keys, 6 * keys), (keys, 0), (4 * keys, 5 * keys), (2 * keys, 3 * keys)),
        early,
        k_saved,
        query_grad,
    )
    returned = lax.all_to_all(slot_grads.reshape(16, CAP, tokens, WIDE), "req", 0, 0, tiled=True)
    (latent_grad,) = call(
        gather_body,
        (jax.ShapeDtypeStruct((16, tokens, WIDE), f32),),
        (owned,),
        (returned.reshape(slots.shape),),
        scratch=[pltpu.VMEM((17, tokens, WIDE), f32), dma(4)],
        direct=(0,),
    )
    return (attended, query_grad, latent_grad)


def solution(mesh):
    in_specs = (
        P("req", "head", None),
        P("req", "head", None),
        P("req", "head", None),
        P(),
        P(),
        P(),
    )
    out_specs = (P("req", "head", None), P("req", "head", None), P("req", "head", None))
    return jax.shard_map(per_device, mesh=mesh, in_specs=in_specs, out_specs=out_specs, check_vma=False)
```

```python
import functools
import math

import jax
import jax.numpy as jnp
from jax import lax
from jax.experimental import pallas as pl
from jax.experimental.pallas import tpu as pltpu
from jax.sharding import PartitionSpec as P


LAT = 512
WIDE = 576
MAXL = 16
CAP = 2
BIG = -1e30
SLOTS = 16 * CAP
SCALE = 192.0 ** (-0.5)
EXPC = SCALE * math.log2(math.e)
NT = (((1,), (1,)), ((), ()))
NN = (((1,), (0,)), ((), ()))
f32 = jnp.float32
bf16 = jnp.bfloat16


def dot(a, b, dims=NN):
    return lax.dot_general(a, b, dims, preferred_element_type=f32)


def owner_table(lists, counts, own, table, empty):
    def group(g, carry):
        table[g * CAP] = empty
        table[g * CAP + 1] = empty
        rank = jnp.int32(0)
        for j in range(MAXL):
            block = lists[g, j]
            mine = ((block >> 4) == own) & (j < counts[g])
            table[jnp.where(mine, g * CAP + rank, SLOTS)] = block & 15
            rank = jnp.where(mine, jnp.minimum(rank + 1, CAP - 1), rank)
        return carry

    lax.fori_loop(0, 16, group, 0)


def slot_table(lists, own, table, seen):
    for o in range(16):
        seen[o] = 0
    for j in range(MAXL):
        owner = lists[own, j] >> 4
        rank = seen[owner]
        seen[owner] = jnp.minimum(rank + 1, CAP - 1)
        table[j] = owner * CAP + rank


def pick_body(lists, counts, me, lat_ref, out_ref, table, lat, held, sem, sems):
    load = pltpu.make_async_copy(lat_ref, lat, sem.at[0])
    load.start()
    owner_table(lists, counts, me[0], table, 16)
    load.wait()
    step = SLOTS // 4
    parts = [slice(i * step, i * step + step) for i in range(4)]
    copies = [pltpu.make_async_copy(held.at[p], out_ref.at[p], sems.at[i]) for i, p in enumerate(parts)]
    for s in range(SLOTS):
        held[s] = lat[table[s] & 15]
        if s % step == step - 1:
            copies[s // step].start()
    for copy in copies:
        copy.wait()


def gather_body(table, arrived_ref, out_ref, total, sems):
    total[...] = jnp.zeros(total.shape, total.dtype)
    for s in range(SLOTS):
        total[table[s]] = total[table[s]] + arrived_ref[s].astype(f32)
    parts = [slice(i * 4, i * 4 + 4) for i in range(4)]
    copies = [pltpu.make_async_copy(total.at[p], out_ref.at[p], sems.at[i]) for i, p in enumerate(parts)]
    for copy in copies:
        copy.start()
    for copy in copies:
        copy.wait()


def take_body(lists, counts, me, arrived_ref, out_ref, table, seen):
    slot_table(lists, me[0], table, seen)
    count = counts[me[0]]
    for j in range(MAXL):
        live = j < count

        @pl.when(live)
        def _():
            out_ref[j * 16 : j * 16 + 16] = arrived_ref[table[j]]

        @pl.when(jnp.logical_not(live))
        def _():
            out_ref[j * 16 : j * 16 + 16] = jnp.zeros((16, WIDE), bf16)


def put_body(lists, counts, me, a_ref, b_ref, c_ref, d_ref, out_ref, table, seen, held, sems):
    slot_table(lists, me[0], table, seen)
    count = counts[me[0]]

    def copy(j):
        return pltpu.make_async_copy(held.at[j * 16 : j * 16 + 16], out_ref.at[table[j]], sems.at[j])

    for j in range(MAXL):
        here = slice(j * 16, j * 16 + 16)
        total = a_ref[here].astype(f32) + b_ref[here].astype(f32)
        total = total + (c_ref[here].astype(f32) + d_ref[here].astype(f32))
        held[here] = total.astype(bf16)

        @pl.when(j < count)
        def _():
            copy(j).start()

    for j in range(MAXL):

        @pl.when(j < count)
        def _():
            copy(j).wait()


def turn_body(q_ref, g_ref, qt_ref, gt_ref):
    rows = qt_ref.shape[1]
    for at in range(0, rows, 256):
        here = slice(at, at + 256)
        part = slice(at // 16, at // 16 + 16)
        q = q_ref[part].reshape(256, WIDE)
        qt_ref[:LAT, here] = q[:, :LAT].T
        rope = jnp.concatenate([q[:, LAT:], q[:, LAT:]], axis=1)
        qt_ref[LAT:, here] = rope.T[: WIDE - LAT]
        gt_ref[:, here] = g_ref[part].reshape(256, LAT).T


def two_body(near_ref, far_ref, out_ref):
    out_ref[...] = (near_ref[...].astype(f32) + far_ref[...].astype(f32)).astype(bf16)


def one_body(near_ref, far_ref, two_ref, a_ref, b_ref):
    size = a_ref.shape[0]
    total = near_ref[...].astype(f32) + far_ref[...].astype(f32)
    a_ref[...] = total[:size].astype(bf16)
    b_ref[...] = (total[size:] + two_ref[...].astype(f32)).astype(bf16)


ONCHIP = pl.BlockSpec(memory_space=pltpu.VMEM)
INPLACE = pl.BlockSpec(memory_space=pltpu.HBM)


def call(body, outs, scalars, arrays, scratch=(), direct_in=(), direct=(), alias=None, flops=None, smem_out=()):
    args = [
        pltpu.with_memory_space_constraint(a, pltpu.HBM if i in direct_in else pltpu.VMEM)
        for i, a in enumerate(arrays)
    ]
    scalars = [pltpu.with_memory_space_constraint(a, pltpu.HBM) for a in scalars]
    shapes = [
        (pltpu.HBM if i in direct or i in smem_out else pltpu.VMEM)(o.shape, o.dtype) for i, o in enumerate(outs)
    ]
    small = pl.BlockSpec(memory_space=pltpu.SMEM)
    return pl.pallas_call(
        body,
        in_specs=[small] * len(scalars)
        + [INPLACE if i in direct_in else ONCHIP for i in range(len(arrays))],
        out_specs=tuple(small if i in smem_out else INPLACE if i in direct else ONCHIP for i in range(len(outs))),
        out_shape=tuple(shapes),
        scratch_shapes=list(scratch),
        input_output_aliases=alias or {},
        cost_estimate=flops and pl.CostEstimate(flops=flops, transcendentals=0, bytes_accessed=0),
        compiler_params=pltpu.CompilerParams(vmem_limit_bytes=16 * 1024 * 1024),
    )(*scalars, *args)


def forward_body(nkeys, chunk, kept, off, n, block, *refs):
    key_refs, refs = refs[:nkeys], refs[nkeys:]
    bias, q_ref, g_ref = refs[:3]
    e_out, p_out, k_out, st_out = refs[3 + kept : 7 + kept]
    at = off
    for ref in key_refs:
        k_out[at : at + ref.shape[0]] = ref[...]
        at += ref.shape[0]
    mine = slice(off, off + n)

    def rows(i, carry):
        here = pl.ds(pl.multiple_of(i * block, block), block)
        part = pl.ds(i * (block // 16), block // 16)
        scores = dot(q_ref[part].reshape(block, WIDE), k_out[mine], NT) + bias[...]
        top = jnp.max(scores, axis=1, keepdims=True)
        expo = jnp.exp2((scores - top) * EXPC)
        grads = dot(g_ref[part].reshape(block, LAT), k_out[mine, :LAT], NT)
        e_out[here, mine] = expo.astype(bf16)
        p_out[here, mine] = grads.astype(bf16)
        wide = lambda x: jnp.broadcast_to(x, (block, 128))
        st_out[chunk, here] = wide(top)
        st_out[3 + chunk, here] = wide(jnp.sum(expo, axis=1, keepdims=True))
        st_out[6 + chunk, here] = wide(jnp.sum(expo * grads, axis=1, keepdims=True))
        return carry

    lax.fori_loop(0, q_ref.shape[0] * 16 // block, rows, 0)


def forward(chunk, off, n, total_keys, key_parts, bias, q, g, state=(), block=768):
    rows = q.shape[0] * 16
    side = jax.ShapeDtypeStruct((rows, total_keys), bf16)
    outs = [side, side, jax.ShapeDtypeStruct((total_keys, WIDE), bf16), jax.ShapeDtypeStruct((9, rows, 128), f32)]
    if state:
        outs = [jax.ShapeDtypeStruct(a.shape, a.dtype) for a in state]
    start = len(key_parts) + 3
    return call(
        functools.partial(forward_body, len(key_parts), chunk, len(state), off, n, block),
        outs,
        (),
        [*key_parts, bias, q, g, *state],
        alias={start + i: i for i in range(len(state))},
        flops=2 * rows * n * (WIDE + LAT),
    )


def backward_body(chunk, offs, n, lead, final, early, step, tile, *refs):
    refs = list(refs)
    qt_ref, gt_ref, e_ref, p_ref, row_ref, k_ref = refs[:6]
    parts, refs = refs[6 : 6 + len(offs)], refs[6 + len(offs) :]
    e_out, p_out, row_out, _, s_out = refs[:5]
    held, sems = refs[-2:]
    rows = qt_ref.shape[1]
    if final:
        kept, sem = refs[5], refs[6]
        save = pltpu.make_async_copy(k_ref, kept, sem.at[0])
        save.start()
    if lead:
        for at in range(0, rows, step):
            here = slice(at, at + step)
            col = lambda c: row_ref[c, here]
            top = jnp.maximum(jnp.maximum(col(0), col(1)), col(2))
            fade = [jnp.exp2((col(c) - top) * EXPC) for c in range(3)]
            total = fade[0] * col(3) + fade[1] * col(4) + fade[2] * col(5)
            rdot = fade[0] * col(6) + fade[1] * col(7) + fade[2] * col(8)
            total = 1.0 / total
            for c in range(3):
                row_out[c, here] = fade[c] * total
            row_out[3, here] = rdot * total
    copies = []
    for ref, off in zip(parts, offs):
        for start in range(0, n, tile):
            cols = slice(off + start, off + start + tile)
            spot = len(copies)
            acc = None
            for at in range(0, rows, step):
                here = slice(at, at + step)
                a = jnp.tile(row_out[chunk, here], (1, tile // 128))
                r = jnp.tile(row_out[3, here], (1, tile // 128))
                weights = (e_ref[here, cols].astype(f32) * a).astype(bf16)
                sg = (weights.astype(f32) * (p_ref[here, cols].astype(f32) - r) * SCALE).astype(bf16)
                e_out[here, cols] = weights
                if at < early:
                    p_out[here, cols] = sg
                else:
                    held[spot, at - early : at - early + step] = sg
                key_part = dot(qt_ref[:, here], sg)
                value_part = dot(gt_ref[:, here], weights)
                if acc is None:
                    acc = [key_part[:LAT] + value_part, key_part[LAT:]]
                else:
                    acc = [acc[0] + (key_part[:LAT] + value_part), acc[1] + key_part[LAT:]]
            copies.append(pltpu.make_async_copy(held.at[spot], s_out.at[spot], sems.at[spot]))
            copies[-1].start()
            ref[start : start + tile, :LAT] = acc[0].T.astype(bf16)
            low = jnp.concatenate([acc[1], jnp.zeros_like(acc[1])], axis=0).T[:, : WIDE - LAT]
            ref[start : start + tile, LAT:] = low.astype(bf16)
    for copy in copies:
        copy.wait()
    if final:
        save.wait()


def backward(chunk, offs, n, early, qt, gt, e, p, row, k, lead=False, final=False, tile=256, step=256):
    rows = e.shape[0]
    count = len(offs)
    like = lambda a: jax.ShapeDtypeStruct(a.shape, a.dtype)
    part = jax.ShapeDtypeStruct((n, WIDE), bf16)
    merged = jax.ShapeDtypeStruct((4, rows, 128), f32) if lead else like(row)
    late = (count * n // tile, rows - early, tile)
    outs = [part] * count + [like(e), like(p), merged, like(k), jax.ShapeDtypeStruct(late, bf16)]
    alias = {2: count, 3: count + 1, 5: count + 3}
    scratch = [pltpu.VMEM(late, bf16), pltpu.SemaphoreType.DMA((late[0],))]
    direct = (count + 4,)
    if not lead:
        alias[4] = count + 2
    if final:
        outs.append(like(k))
        direct = (count + 4, count + 5)
        scratch = [pltpu.SemaphoreType.DMA((1,)), *scratch]
    return call(
        functools.partial(backward_body, chunk, offs, n, lead, final, early, step, tile),
        outs,
        (),
        (qt, gt, e, p, row, k),
        scratch=scratch,
        alias=alias,
        direct=direct,
        flops=2 * rows * n * count * (WIDE + LAT),
    )


def leaving(held, out_ref, sems, block):
    def copy(i):
        part = pl.ds(i * (block // 16), block // 16)
        return pltpu.make_async_copy(held.at[part], out_ref.at[part], sems.at[i])

    return copy


def value_body(block, early, w_ref, s_ref, k_ref, out_ref, q_ref, held, held_q, sems, sems_q):
    steps = out_ref.shape[0] * 16 // block
    leave = leaving(held, out_ref, sems, block)
    leave_q = leaving(held_q, q_ref, sems_q, block)
    for i in range(early // block):
        here = slice(i * block, i * block + block)
        part = slice(i * (block // 16), (i + 1) * (block // 16))
        held_q[part] = dot(s_ref[here], k_ref[...]).astype(bf16).reshape(block // 16, 16, WIDE)
        leave_q(i).start()

    def rows(i, carry):
        here = pl.ds(pl.multiple_of(i * block, block), block)
        part = pl.ds(i * (block // 16), block // 16)
        held[part] = dot(w_ref[here], k_ref[:, :LAT]).astype(bf16).reshape(block // 16, 16, LAT)
        leave(i).start()
        return carry

    lax.fori_loop(0, steps, rows, 0)
    for i in range(early // block):
        leave_q(i).wait()
    for i in range(steps):
        leave(i).wait()


def value_side(w, s, k, early, block=512):
    rows = w.shape[0]
    shape = (rows // 16, 16, LAT)
    dma = lambda n: pltpu.SemaphoreType.DMA((n,))
    return call(
        functools.partial(value_body, block, early),
        (jax.ShapeDtypeStruct(shape, bf16), jax.ShapeDtypeStruct((rows // 16, 16, WIDE), bf16)),
        (),
        (w, s, k),
        scratch=[
            pltpu.VMEM(shape, bf16),
            pltpu.VMEM((early // 16, 16, WIDE), bf16),
            dma(rows // block),
            dma(early // block),
        ],
        direct=(0, 1),
        flops=2 * k.shape[0] * (rows * LAT + early * WIDE),
    )


def query_body(offs, early, block, *refs):
    s_refs, (k_ref, _, out_ref, s_v, k_v, held, sems_k, sems_s, sems) = refs[: len(offs)], refs[len(offs) :]
    steps = s_v.shape[1] // block
    load_k = pltpu.make_async_copy(k_ref, k_v, sems_k.at[0])
    load_k.start()
    loads = []
    for i in range(steps):
        here = slice(i * block, i * block + block)
        loads.append(
            [
                pltpu.make_async_copy(ref.at[t, here], s_v.at[spot, here], sems_s.at[i * s_v.shape[0] + spot])
                for ref, spots in zip(s_refs, offs)
                for t, spot in enumerate(spots)
            ]
        )
        for copy in loads[-1]:
            copy.start()
    load_k.wait()
    leave = []
    for i in range(steps):
        for copy in loads[i]:
            copy.wait()
        here = slice(i * block, i * block + block)
        part = slice(i * (block // 16), (i + 1) * (block // 16))
        to = slice(early // 16 + part.start, early // 16 + part.stop)
        sg = jnp.concatenate([s_v[t, here] for t in range(s_v.shape[0])], axis=1)
        held[part] = dot(sg, k_v[...]).astype(bf16).reshape(block // 16, 16, WIDE)
        leave.append(pltpu.make_async_copy(held.at[part], out_ref.at[to], sems.at[i]))
        leave[-1].start()
    for copy in leave:
        copy.wait()


def query_side(sgs, offs, early, k, out, block=512):
    tile, rows = sgs[0].shape[2], sgs[0].shape[1]
    dma = lambda n: pltpu.SemaphoreType.DMA((n,))
    steps, tiles = rows // block, k.shape[0] // tile
    return call(
        functools.partial(query_body, [[off // tile for off in o] for o in offs], early, block),
        (jax.ShapeDtypeStruct(out.shape, bf16),),
        (),
        (*sgs, k, out),
        scratch=[
            pltpu.VMEM((tiles, rows, tile), bf16),
            pltpu.VMEM(k.shape, bf16),
            pltpu.VMEM((rows // 16, 16, WIDE), bf16),
            dma(1),
            dma(steps * tiles),
            dma(steps),
        ],
        direct_in=range(len(sgs) + 2),
        direct=(0,),
        alias={len(sgs) + 1: 0},
        flops=2 * rows * k.shape[0] * WIDE,
    )[0]


def per_device(queries, out_grad, latents, list_blocks, list_counts, valid_tokens):
    me = lax.axis_index("req")
    head = lax.axis_index("head")
    chip, core = head // 2, head % 2
    tokens = latents.shape[1]
    pair_a, pair_b, sibling = [[(h, h ^ d) for h in range(8)] for d in (2, 6, 1)]
    send = lambda a, perm: lax.ppermute(a, "head", perm)
    scalars = (list_blocks, list_counts, me.reshape(1).astype(jnp.int32))

    smem = lambda n: pltpu.SMEM((n,), jnp.int32)
    slots = jax.ShapeDtypeStruct((SLOTS, tokens, WIDE), bf16)
    keys = MAXL * tokens
    share_of = lambda n: jax.ShapeDtypeStruct((n, WIDE), bf16)

    dma = lambda n: pltpu.SemaphoreType.DMA((n,))
    outgoing, owned = call(
        pick_body,
        (slots, jax.ShapeDtypeStruct((SLOTS + 1,), jnp.int32)),
        scalars,
        (latents,),
        scratch=[
            pltpu.VMEM(latents.shape, bf16),
            pltpu.VMEM((SLOTS, tokens, WIDE), bf16),
            dma(1),
            dma(4),
        ],
        direct_in=(0,),
        direct=(0,),
        smem_out=(1,),
    )
    arrived = lax.all_to_all(outgoing.reshape(16, CAP, tokens, WIDE), "req", 0, 0, tiled=True)

    my_blocks = lax.dynamic_index_in_dim(list_blocks, me, 0, keepdims=False)
    my_count = lax.dynamic_index_in_dim(list_counts, me, 0, keepdims=False)
    ids = jnp.arange(valid_tokens.shape[0], dtype=jnp.int32)
    filled = jnp.sum(jnp.where(my_blocks[:, None] == ids[None, :], valid_tokens[None, :], 0), axis=1)
    filled = jnp.where(jnp.arange(MAXL, dtype=jnp.int32) < my_count, filled, 0)
    filled = jnp.repeat(filled, tokens)[None, :]
    offset = jnp.tile(jnp.arange(tokens, dtype=jnp.int32), MAXL)[None, :]
    at = lambda d, c: (chip ^ d) * 2 + c
    other = 1 - core
    places = [at(0, core), at(0, other), at(1, core), at(3, core), at(1, other), at(3, other), at(2, core), at(2, other)]
    first_token = jnp.stack(places)[:, None] * tokens
    bias = jnp.where(first_token + offset < filled, 0.0, BIG).astype(f32)
    bias0, bias1, bias2 = [bias[i:j].reshape(1, -1) for i, j in ((0, 2), (2, 6), (6, 8))]

    arrived, bias0, bias1, bias2 = lax.optimization_barrier((arrived, bias0, bias1, bias2))

    (share,) = call(
        take_body,
        (share_of(keys),),
        scalars,
        (arrived.reshape(slots.shape),),
        scratch=[smem(MAXL), smem(16)],
    )

    after = lambda a, *others: lax.optimization_barrier((a, *others))[0]
    q, g = queries, out_grad
    every = 8 * keys
    from_b = send(share, pair_b)
    from_a = send(share, pair_a)
    s0 = send(share, sibling)
    state = forward(0, 0, 2 * keys, every, [share, s0], bias0, q, g)
    flat = lambda a: jax.ShapeDtypeStruct((a.shape[2], a.shape[0] * a.shape[1]), bf16)
    qt, gt = call(turn_body, (flat(queries), flat(out_grad)), (), (q, after(g, state[3])))
    from_b = after(from_b, gt)
    from_a = after(from_a, gt)
    r2 = send(from_b, pair_a)
    sa = send(from_a, sibling)
    sb = send(from_b, sibling)
    state = forward(1, 2 * keys, 4 * keys, every, [from_a, from_b, sa, sb], bias1, q, g, (*state, qt, gt))
    r2 = after(r2, state[3])
    s3 = send(r2, sibling)
    e, p, k, row, qt, gt = forward(2, 6 * keys, 2 * keys, every, [r2, s3], bias2, q, g, state)

    fold = lambda a: a.reshape(-1, tokens, WIDE)
    unfold = lambda a: a.reshape(-1, WIDE)
    early = 512
    back = functools.partial(backward, early=early, qt=qt, gt=gt)
    far2, near2, e, p, row, k, sg2 = back(2, (7 * keys, 6 * keys), keys, e=e, p=p, row=row, k=k, lead=True)
    mate2 = send(far2, sibling)
    far0, near0, e, p, row, k, sg0, k_saved = back(0, (keys, 0), keys, e=e, p=p, row=row, k=k, final=True)
    (two,) = call(two_body, (share_of(keys),), (), (after(near2, near0), mate2))
    got_two = send(two, pair_a)
    far1, e, p, row, k, sg1f = back(1, (4 * keys,), 2 * keys, e=e, p=p, row=after(row, two), k=k)
    mate1 = unfold(send(fold(far1), sibling))
    near1, e, p, row, k, sg1n = back(1, (2 * keys,), 2 * keys, e=e, p=p, row=row, k=k)
    mate0 = send(far0, sibling)
    to_a, to_b = call(one_body, (share_of(keys),) * 2, (), (near1, mate1, got_two))
    got_b = send(to_b, pair_b)
    got_a = send(to_a, pair_a)
    attended, query_grad = value_side(e, p, after(k, to_a), early)
    near0 = after(near0, attended)
    (slot_grads,) = call(
        put_body,
        (slots,),
        scalars,
        (near0, mate0, got_a, got_b),
        scratch=[smem(MAXL), smem(16), pltpu.VMEM((keys, WIDE), bf16), dma(MAXL)],
        direct=(0,),
    )
    k_saved = after(k_saved, slot_grads)
    query_grad = query_side(
        (sg2, sg0, sg1f, sg1n),
        ((7 * keys, 6 * keys), (keys, 0), (4 * keys, 5 * keys), (2 * keys, 3 * keys)),
        early,
        k_saved,
        query_grad,
    )
    returned = lax.all_to_all(slot_grads.reshape(16, CAP, tokens, WIDE), "req", 0, 0, tiled=True)
    (latent_grad,) = call(
        gather_body,
        (jax.ShapeDtypeStruct((16, tokens, WIDE), f32),),
        (owned,),
        (returned.reshape(slots.shape),),
        scratch=[pltpu.VMEM((17, tokens, WIDE), f32), dma(4)],
        direct=(0,),
    )
    return (attended, query_grad, latent_grad)


def solution(mesh):
    in_specs = (
        P("req", "head", None),
        P("req", "head", None),
        P("req", "head", None),
        P(),
        P(),
        P(),
    )
    out_specs = (P("req", "head", None), P("req", "head", None), P("req", "head", None))
    return jax.shard_map(per_device, mesh=mesh, in_specs=in_specs, out_specs=out_specs, check_vma=False)
```

```python
import functools
import math

import jax
import jax.numpy as jnp
from jax import lax
from jax.experimental import pallas as pl
from jax.experimental.pallas import tpu as pltpu
from jax.sharding import PartitionSpec as P


LAT = 512
WIDE = 576
MAXL = 16
CAP = 2
BIG = -1e30
SLOTS = 16 * CAP
SCALE = 192.0 ** (-0.5)
EXPC = SCALE * math.log2(math.e)
NT = (((1,), (1,)), ((), ()))
NN = (((1,), (0,)), ((), ()))
f32 = jnp.float32
bf16 = jnp.bfloat16


def dot(a, b, dims=NN):
    return lax.dot_general(a, b, dims, preferred_element_type=f32)


def owner_table(lists, counts, own, table, empty):
    def group(g, carry):
        table[g * CAP] = empty
        table[g * CAP + 1] = empty
        rank = jnp.int32(0)
        for j in range(MAXL):
            block = lists[g, j]
            mine = ((block >> 4) == own) & (j < counts[g])
            table[jnp.where(mine, g * CAP + rank, SLOTS)] = block & 15
            rank = jnp.where(mine, jnp.minimum(rank + 1, CAP - 1), rank)
        return carry

    lax.fori_loop(0, 16, group, 0)


def slot_table(lists, own, table, seen):
    for o in range(16):
        seen[o] = 0
    for j in range(MAXL):
        owner = lists[own, j] >> 4
        rank = seen[owner]
        seen[owner] = jnp.minimum(rank + 1, CAP - 1)
        table[j] = owner * CAP + rank


def pick_body(lists, counts, me, lat_ref, out_ref, table, lat, held, sem, sems):
    load = pltpu.make_async_copy(lat_ref, lat, sem.at[0])
    load.start()
    owner_table(lists, counts, me[0], table, 16)
    load.wait()
    step = SLOTS // 4
    parts = [slice(i * step, i * step + step) for i in range(4)]
    copies = [pltpu.make_async_copy(held.at[p], out_ref.at[p], sems.at[i]) for i, p in enumerate(parts)]
    for s in range(SLOTS):
        held[s] = lat[table[s] & 15]
        if s % step == step - 1:
            copies[s // step].start()
    for copy in copies:
        copy.wait()


def gather_body(table, arrived_ref, out_ref, total, sems):
    total[...] = jnp.zeros(total.shape, total.dtype)
    for s in range(SLOTS):
        total[table[s]] = total[table[s]] + arrived_ref[s].astype(f32)
    parts = [slice(i * 4, i * 4 + 4) for i in range(4)]
    copies = [pltpu.make_async_copy(total.at[p], out_ref.at[p], sems.at[i]) for i, p in enumerate(parts)]
    for copy in copies:
        copy.start()
    for copy in copies:
        copy.wait()


def take_body(lists, counts, me, arrived_ref, out_ref, table, seen):
    slot_table(lists, me[0], table, seen)
    count = counts[me[0]]
    for j in range(MAXL):
        live = j < count

        @pl.when(live)
        def _():
            out_ref[j * 16 : j * 16 + 16] = arrived_ref[table[j]]

        @pl.when(jnp.logical_not(live))
        def _():
            out_ref[j * 16 : j * 16 + 16] = jnp.zeros((16, WIDE), bf16)


def put_body(lists, counts, me, a_ref, b_ref, c_ref, d_ref, out_ref, table, seen, held, sems):
    slot_table(lists, me[0], table, seen)
    count = counts[me[0]]

    def copy(j):
        return pltpu.make_async_copy(held.at[j * 16 : j * 16 + 16], out_ref.at[table[j]], sems.at[j])

    for j in range(MAXL):
        here = slice(j * 16, j * 16 + 16)
        total = a_ref[here].astype(f32) + b_ref[here].astype(f32)
        total = total + (c_ref[here].astype(f32) + d_ref[here].astype(f32))
        held[here] = total.astype(bf16)

        @pl.when(j < count)
        def _():
            copy(j).start()

    for j in range(MAXL):

        @pl.when(j < count)
        def _():
            copy(j).wait()


def turn_body(q_ref, g_ref, qt_ref, gt_ref):
    rows = qt_ref.shape[1]
    for at in range(0, rows, 256):
        here = slice(at, at + 256)
        part = slice(at // 16, at // 16 + 16)
        q = q_ref[part].reshape(256, WIDE)
        qt_ref[:LAT, here] = q[:, :LAT].T
        rope = jnp.concatenate([q[:, LAT:], q[:, LAT:]], axis=1)
        qt_ref[LAT:, here] = rope.T[: WIDE - LAT]
        gt_ref[:, here] = g_ref[part].reshape(256, LAT).T


def two_body(near_ref, far_ref, out_ref):
    out_ref[...] = (near_ref[...].astype(f32) + far_ref[...].astype(f32)).astype(bf16)


def one_body(near_ref, far_ref, two_ref, a_ref, b_ref):
    size = a_ref.shape[0]
    total = near_ref[...].astype(f32) + far_ref[...].astype(f32)
    a_ref[...] = total[:size].astype(bf16)
    b_ref[...] = (total[size:] + two_ref[...].astype(f32)).astype(bf16)


ONCHIP = pl.BlockSpec(memory_space=pltpu.VMEM)
INPLACE = pl.BlockSpec(memory_space=pltpu.HBM)


def call(body, outs, scalars, arrays, scratch=(), direct_in=(), direct=(), alias=None, flops=None, smem_out=()):
    args = [
        pltpu.with_memory_space_constraint(a, pltpu.HBM if i in direct_in else pltpu.VMEM)
        for i, a in enumerate(arrays)
    ]
    scalars = [pltpu.with_memory_space_constraint(a, pltpu.HBM) for a in scalars]
    shapes = [
        (pltpu.HBM if i in direct or i in smem_out else pltpu.VMEM)(o.shape, o.dtype) for i, o in enumerate(outs)
    ]
    small = pl.BlockSpec(memory_space=pltpu.SMEM)
    return pl.pallas_call(
        body,
        in_specs=[small] * len(scalars)
        + [INPLACE if i in direct_in else ONCHIP for i in range(len(arrays))],
        out_specs=tuple(small if i in smem_out else INPLACE if i in direct else ONCHIP for i in range(len(outs))),
        out_shape=tuple(shapes),
        scratch_shapes=list(scratch),
        input_output_aliases=alias or {},
        cost_estimate=flops and pl.CostEstimate(flops=flops, transcendentals=0, bytes_accessed=0),
        compiler_params=pltpu.CompilerParams(vmem_limit_bytes=16 * 1024 * 1024),
    )(*scalars, *args)


def forward_body(nkeys, chunk, off, n, block, *refs):
    refs = list(refs)
    first = chunk == 0
    key_refs, bias, refs = refs[:nkeys], refs[nkeys], refs[nkeys + 1 :]
    if first:
        (q_in, g_in), refs = refs[:2], refs[2:]
        sems, refs = refs[-1], refs[:-1]
    else:
        refs = refs[len(refs) // 2 :]
    e_out, p_out, k_out, st_out, q_ref, g_ref = refs
    steps = q_ref.shape[0] * 16 // block

    def loads(i):
        part = pl.ds(i * (block // 16), block // 16)
        return (
            pltpu.make_async_copy(q_in.at[part], q_ref.at[part], sems.at[2 * i]),
            pltpu.make_async_copy(g_in.at[part], g_ref.at[part], sems.at[2 * i + 1]),
        )

    if first:
        for i in range(steps):
            for copy in loads(i):
                copy.start()
    at = off
    for ref in key_refs:
        k_out[at : at + ref.shape[0]] = ref[...]
        at += ref.shape[0]
    mine = slice(off, off + n)

    def rows(i, carry):
        here = pl.ds(pl.multiple_of(i * block, block), block)
        part = pl.ds(i * (block // 16), block // 16)
        if first:
            for copy in loads(i):
                copy.wait()
        scores = dot(q_ref[part].reshape(block, WIDE), k_out[mine], NT) + bias[...]
        top = jnp.max(scores, axis=1, keepdims=True)
        expo = jnp.exp2((scores - top) * EXPC)
        grads = dot(g_ref[part].reshape(block, LAT), k_out[mine, :LAT], NT)
        e_out[here, mine] = expo.astype(bf16)
        p_out[here, mine] = grads.astype(bf16)
        wide = lambda x: jnp.broadcast_to(x, (block, 128))
        st_out[chunk, here] = wide(top)
        st_out[3 + chunk, here] = wide(jnp.sum(expo, axis=1, keepdims=True))
        st_out[6 + chunk, here] = wide(jnp.sum(expo * grads, axis=1, keepdims=True))
        return carry

    lax.fori_loop(0, steps, rows, 0)


def forward(chunk, off, n, total_keys, key_parts, bias, state):
    first = chunk == 0
    block = 384 if first else 768
    if first:
        rows = state[0].shape[0] * 16
        side = jax.ShapeDtypeStruct((rows, total_keys), bf16)
        outs = [side, side, jax.ShapeDtypeStruct((total_keys, WIDE), bf16), jax.ShapeDtypeStruct((9, rows, 128), f32)]
    else:
        rows, outs = state[0].shape[0], []
    outs += [jax.ShapeDtypeStruct(a.shape, a.dtype) for a in state]
    start = len(key_parts) + 1
    return call(
        functools.partial(forward_body, len(key_parts), chunk, off, n, block),
        outs,
        (),
        [*key_parts, bias, *state],
        direct_in=(start, start + 1) if first else (),
        scratch=[pltpu.SemaphoreType.DMA((2 * rows // block,))] if first else [],
        alias={} if first else {start + i: i for i in range(len(state))},
        flops=2 * rows * n * (WIDE + LAT),
    )


def backward_body(chunk, offs, n, lead, final, early, step, tile, *refs):
    refs = list(refs)
    qt_ref, gt_ref, e_ref, p_ref, row_ref, k_ref = refs[:6]
    parts, refs = refs[6 : 6 + len(offs)], refs[6 + len(offs) :]
    e_out, p_out, row_out, _, s_out = refs[:5]
    held, sems = refs[-2:]
    rows = qt_ref.shape[1]
    if final:
        kept, sem = refs[5], refs[6]
        save = pltpu.make_async_copy(k_ref, kept, sem.at[0])
        save.start()
    if lead:
        for at in range(0, rows, step):
            here = slice(at, at + step)
            col = lambda c: row_ref[c, here]
            top = jnp.maximum(jnp.maximum(col(0), col(1)), col(2))
            fade = [jnp.exp2((col(c) - top) * EXPC) for c in range(3)]
            total = fade[0] * col(3) + fade[1] * col(4) + fade[2] * col(5)
            rdot = fade[0] * col(6) + fade[1] * col(7) + fade[2] * col(8)
            total = 1.0 / total
            for c in range(3):
                row_out[c, here] = fade[c] * total
            row_out[3, here] = rdot * total
    copies = []
    for ref, off in zip(parts, offs):
        for start in range(0, n, tile):
            cols = slice(off + start, off + start + tile)
            spot = len(copies)
            acc = None
            for at in range(0, rows, step):
                here = slice(at, at + step)
                a = jnp.tile(row_out[chunk, here], (1, tile // 128))
                r = jnp.tile(row_out[3, here], (1, tile // 128))
                weights = (e_ref[here, cols].astype(f32) * a).astype(bf16)
                sg = (weights.astype(f32) * (p_ref[here, cols].astype(f32) - r) * SCALE).astype(bf16)
                e_out[here, cols] = weights
                if at < early:
                    p_out[here, cols] = sg
                else:
                    held[spot, at - early : at - early + step] = sg
                key_part = dot(qt_ref[:, here], sg)
                value_part = dot(gt_ref[:, here], weights)
                if acc is None:
                    acc = [key_part[:LAT] + value_part, key_part[LAT:]]
                else:
                    acc = [acc[0] + (key_part[:LAT] + value_part), acc[1] + key_part[LAT:]]
            copies.append(pltpu.make_async_copy(held.at[spot], s_out.at[spot], sems.at[spot]))
            copies[-1].start()
            ref[start : start + tile, :LAT] = acc[0].T.astype(bf16)
            low = jnp.concatenate([acc[1], jnp.zeros_like(acc[1])], axis=0).T[:, : WIDE - LAT]
            ref[start : start + tile, LAT:] = low.astype(bf16)
    for copy in copies:
        copy.wait()
    if final:
        save.wait()


def backward(chunk, offs, n, early, qt, gt, e, p, row, k, lead=False, final=False, tile=256, step=256):
    rows = e.shape[0]
    count = len(offs)
    like = lambda a: jax.ShapeDtypeStruct(a.shape, a.dtype)
    part = jax.ShapeDtypeStruct((n, WIDE), bf16)
    merged = jax.ShapeDtypeStruct((4, rows, 128), f32) if lead else like(row)
    late = (count * n // tile, rows - early, tile)
    outs = [part] * count + [like(e), like(p), merged, like(k), jax.ShapeDtypeStruct(late, bf16)]
    alias = {2: count, 3: count + 1, 5: count + 3}
    scratch = [pltpu.VMEM(late, bf16), pltpu.SemaphoreType.DMA((late[0],))]
    direct = (count + 4,)
    if not lead:
        alias[4] = count + 2
    if final:
        outs.append(like(k))
        direct = (count + 4, count + 5)
        scratch = [pltpu.SemaphoreType.DMA((1,)), *scratch]
    return call(
        functools.partial(backward_body, chunk, offs, n, lead, final, early, step, tile),
        outs,
        (),
        (qt, gt, e, p, row, k),
        scratch=scratch,
        alias=alias,
        direct=direct,
        flops=2 * rows * n * count * (WIDE + LAT),
    )


def leaving(held, out_ref, sems, block):
    def copy(i):
        part = pl.ds(i * (block // 16), block // 16)
        return pltpu.make_async_copy(held.at[part], out_ref.at[part], sems.at[i])

    return copy


def value_body(block, early, w_ref, s_ref, k_ref, out_ref, q_ref, held, held_q, sems, sems_q):
    steps = out_ref.shape[0] * 16 // block
    leave = leaving(held, out_ref, sems, block)
    leave_q = leaving(held_q, q_ref, sems_q, block)
    for i in range(early // block):
        here = slice(i * block, i * block + block)
        part = slice(i * (block // 16), (i + 1) * (block // 16))
        held_q[part] = dot(s_ref[here], k_ref[...]).astype(bf16).reshape(block // 16, 16, WIDE)
        leave_q(i).start()

    def rows(i, carry):
        here = pl.ds(pl.multiple_of(i * block, block), block)
        part = pl.ds(i * (block // 16), block // 16)
        held[part] = dot(w_ref[here], k_ref[:, :LAT]).astype(bf16).reshape(block // 16, 16, LAT)
        leave(i).start()
        return carry

    lax.fori_loop(0, steps, rows, 0)
    for i in range(early // block):
        leave_q(i).wait()
    for i in range(steps):
        leave(i).wait()


def value_side(w, s, k, early, block=512):
    rows = w.shape[0]
    shape = (rows // 16, 16, LAT)
    dma = lambda n: pltpu.SemaphoreType.DMA((n,))
    return call(
        functools.partial(value_body, block, early),
        (jax.ShapeDtypeStruct(shape, bf16), jax.ShapeDtypeStruct((rows // 16, 16, WIDE), bf16)),
        (),
        (w, s, k),
        scratch=[
            pltpu.VMEM(shape, bf16),
            pltpu.VMEM((early // 16, 16, WIDE), bf16),
            dma(rows // block),
            dma(early // block),
        ],
        direct=(0, 1),
        flops=2 * k.shape[0] * (rows * LAT + early * WIDE),
    )


def query_body(offs, early, block, *refs):
    s_refs, (k_ref, _, out_ref, s_v, k_v, held, sems_k, sems_s, sems) = refs[: len(offs)], refs[len(offs) :]
    steps = s_v.shape[1] // block
    load_k = pltpu.make_async_copy(k_ref, k_v, sems_k.at[0])
    load_k.start()
    loads = []
    for i in range(steps):
        here = slice(i * block, i * block + block)
        loads.append(
            [
                pltpu.make_async_copy(ref.at[t, here], s_v.at[spot, here], sems_s.at[i * s_v.shape[0] + spot])
                for ref, spots in zip(s_refs, offs)
                for t, spot in enumerate(spots)
            ]
        )
        for copy in loads[-1]:
            copy.start()
    load_k.wait()
    leave = []
    for i in range(steps):
        for copy in loads[i]:
            copy.wait()
        here = slice(i * block, i * block + block)
        part = slice(i * (block // 16), (i + 1) * (block // 16))
        to = slice(early // 16 + part.start, early // 16 + part.stop)
        sg = jnp.concatenate([s_v[t, here] for t in range(s_v.shape[0])], axis=1)
        held[part] = dot(sg, k_v[...]).astype(bf16).reshape(block // 16, 16, WIDE)
        leave.append(pltpu.make_async_copy(held.at[part], out_ref.at[to], sems.at[i]))
        leave[-1].start()
    for copy in leave:
        copy.wait()


def query_side(sgs, offs, early, k, out, block=512):
    tile, rows = sgs[0].shape[2], sgs[0].shape[1]
    dma = lambda n: pltpu.SemaphoreType.DMA((n,))
    steps, tiles = rows // block, k.shape[0] // tile
    return call(
        functools.partial(query_body, [[off // tile for off in o] for o in offs], early, block),
        (jax.ShapeDtypeStruct(out.shape, bf16),),
        (),
        (*sgs, k, out),
        scratch=[
            pltpu.VMEM((tiles, rows, tile), bf16),
            pltpu.VMEM(k.shape, bf16),
            pltpu.VMEM((rows // 16, 16, WIDE), bf16),
            dma(1),
            dma(steps * tiles),
            dma(steps),
        ],
        direct_in=range(len(sgs) + 2),
        direct=(0,),
        alias={len(sgs) + 1: 0},
        flops=2 * rows * k.shape[0] * WIDE,
    )[0]


def per_device(queries, out_grad, latents, list_blocks, list_counts, valid_tokens):
    me = lax.axis_index("req")
    head = lax.axis_index("head")
    chip, core = head // 2, head % 2
    tokens = latents.shape[1]
    pair_a, pair_b, sibling = [[(h, h ^ d) for h in range(8)] for d in (2, 6, 1)]
    send = lambda a, perm: lax.ppermute(a, "head", perm)
    scalars = (list_blocks, list_counts, me.reshape(1).astype(jnp.int32))

    smem = lambda n: pltpu.SMEM((n,), jnp.int32)
    slots = jax.ShapeDtypeStruct((SLOTS, tokens, WIDE), bf16)
    keys = MAXL * tokens
    share_of = lambda n: jax.ShapeDtypeStruct((n, WIDE), bf16)

    dma = lambda n: pltpu.SemaphoreType.DMA((n,))
    outgoing, owned = call(
        pick_body,
        (slots, jax.ShapeDtypeStruct((SLOTS + 1,), jnp.int32)),
        scalars,
        (latents,),
        scratch=[
            pltpu.VMEM(latents.shape, bf16),
            pltpu.VMEM((SLOTS, tokens, WIDE), bf16),
            dma(1),
            dma(4),
        ],
        direct_in=(0,),
        direct=(0,),
        smem_out=(1,),
    )
    arrived = lax.all_to_all(outgoing.reshape(16, CAP, tokens, WIDE), "req", 0, 0, tiled=True)

    my_blocks = lax.dynamic_index_in_dim(list_blocks, me, 0, keepdims=False)
    my_count = lax.dynamic_index_in_dim(list_counts, me, 0, keepdims=False)
    ids = jnp.arange(valid_tokens.shape[0], dtype=jnp.int32)
    filled = jnp.sum(jnp.where(my_blocks[:, None] == ids[None, :], valid_tokens[None, :], 0), axis=1)
    filled = jnp.where(jnp.arange(MAXL, dtype=jnp.int32) < my_count, filled, 0)
    filled = jnp.repeat(filled, tokens)[None, :]
    offset = jnp.tile(jnp.arange(tokens, dtype=jnp.int32), MAXL)[None, :]
    at = lambda d, c: (chip ^ d) * 2 + c
    other = 1 - core
    places = [at(0, core), at(0, other), at(1, core), at(3, core), at(1, other), at(3, other), at(2, core), at(2, other)]
    first_token = jnp.stack(places)[:, None] * tokens
    bias = jnp.where(first_token + offset < filled, 0.0, BIG).astype(f32)
    bias0, bias1, bias2 = [bias[i:j].reshape(1, -1) for i, j in ((0, 2), (2, 6), (6, 8))]

    arrived, bias0, bias1, bias2 = lax.optimization_barrier((arrived, bias0, bias1, bias2))

    (share,) = call(
        take_body,
        (share_of(keys),),
        scalars,
        (arrived.reshape(slots.shape),),
        scratch=[smem(MAXL), smem(16)],
    )

    after = lambda a, *others: lax.optimization_barrier((a, *others))[0]
    every = 8 * keys
    from_b = send(share, pair_b)
    from_a = send(share, pair_a)
    s0 = send(share, sibling)
    state = forward(0, 0, 2 * keys, every, [share, s0], bias0, (queries, out_grad))
    from_b = after(from_b, state[3])
    from_a = after(from_a, state[3])
    r2 = send(from_b, pair_a)
    sa = send(from_a, sibling)
    sb = send(from_b, sibling)
    state = forward(1, 2 * keys, 4 * keys, every, [from_a, from_b, sa, sb], bias1, state)
    r2 = after(r2, state[3])
    s3 = send(r2, sibling)
    flat = lambda a: jax.ShapeDtypeStruct((a.shape[2], a.shape[0] * a.shape[1]), bf16)
    e, p, k, row, q, g = state
    qt, gt = call(turn_body, (flat(queries), flat(out_grad)), (), (q, after(g, r2)))
    e, p, k, row, q, g = forward(2, 6 * keys, 2 * keys, every, [r2, s3], bias2, (e, p, k, after(row, gt), q, g))

    fold = lambda a: a.reshape(-1, tokens, WIDE)
    unfold = lambda a: a.reshape(-1, WIDE)
    early = 512
    back = functools.partial(backward, early=early, qt=qt, gt=gt)
    far2, e, p, row, k, sg2f = back(2, (7 * keys,), keys, e=e, p=p, row=row, k=k, lead=True)
    mate2 = send(far2, sibling)
    near2, e, p, row, k, sg2n = back(2, (6 * keys,), keys, e=e, p=p, row=row, k=k)
    far0, e, p, row, k, sg0f = back(0, (keys,), keys, e=e, p=p, row=row, k=k)
    (two,) = call(two_body, (share_of(keys),), (), (after(near2, far0), mate2))
    got_two = send(two, pair_a)
    far1, e, p, row, k, sg1f = back(1, (4 * keys,), 2 * keys, e=e, p=p, row=after(row, two), k=k)
    mate1 = unfold(send(fold(far1), sibling))
    near1, e, p, row, k, sg1n = back(1, (2 * keys,), 2 * keys, e=e, p=p, row=row, k=k)
    mate0 = send(far0, sibling)
    near0, e, p, row, k, sg0n, k_saved = back(0, (0,), keys, e=e, p=p, row=row, k=k, final=True)
    near1 = after(near1, near0)
    to_a, to_b = call(one_body, (share_of(keys),) * 2, (), (near1, mate1, got_two))
    got_b = send(to_b, pair_b)
    got_a = send(to_a, pair_a)
    attended, query_grad = value_side(e, p, after(k, to_a), early)
    near0 = after(near0, attended)
    (slot_grads,) = call(
        put_body,
        (slots,),
        scalars,
        (near0, mate0, got_a, got_b),
        scratch=[smem(MAXL), smem(16), pltpu.VMEM((keys, WIDE), bf16), dma(MAXL)],
        direct=(0,),
    )
    k_saved = after(k_saved, slot_grads)
    query_grad = query_side(
        (sg2f, sg2n, sg0f, sg0n, sg1f, sg1n),
        ((7 * keys,), (6 * keys,), (keys,), (0,), (4 * keys, 5 * keys), (2 * keys, 3 * keys)),
        early,
        k_saved,
        query_grad,
    )
    returned = lax.all_to_all(slot_grads.reshape(16, CAP, tokens, WIDE), "req", 0, 0, tiled=True)
    (latent_grad,) = call(
        gather_body,
        (jax.ShapeDtypeStruct((16, tokens, WIDE), f32),),
        (owned,),
        (returned.reshape(slots.shape),),
        scratch=[pltpu.VMEM((17, tokens, WIDE), f32), dma(4)],
        direct=(0,),
    )
    return (attended, query_grad, latent_grad)


def solution(mesh):
    in_specs = (
        P("req", "head", None),
        P("req", "head", None),
        P("req", "head", None),
        P(),
        P(),
        P(),
    )
    out_specs = (P("req", "head", None), P("req", "head", None), P("req", "head", None))
    return jax.shard_map(per_device, mesh=mesh, in_specs=in_specs, out_specs=out_specs, check_vma=False)
```

```python
import functools
import math

import jax
import jax.numpy as jnp
from jax import lax
from jax.experimental import pallas as pl
from jax.experimental.pallas import tpu as pltpu
from jax.sharding import PartitionSpec as P


LAT = 512
WIDE = 576
MAXL = 16
CAP = 2
BIG = -1e30
SLOTS = 16 * CAP
SCALE = 192.0 ** (-0.5)
EXPC = SCALE * math.log2(math.e)
NT = (((1,), (1,)), ((), ()))
NN = (((1,), (0,)), ((), ()))
f32 = jnp.float32
bf16 = jnp.bfloat16


def dot(a, b, dims=NN):
    return lax.dot_general(a, b, dims, preferred_element_type=f32)


def owner_table(lists, counts, own, table, empty):
    def group(g, carry):
        table[g * CAP] = empty
        table[g * CAP + 1] = empty
        rank = jnp.int32(0)
        for j in range(MAXL):
            block = lists[g, j]
            mine = ((block >> 4) == own) & (j < counts[g])
            table[jnp.where(mine, g * CAP + rank, SLOTS)] = block & 15
            rank = jnp.where(mine, jnp.minimum(rank + 1, CAP - 1), rank)
        return carry

    lax.fori_loop(0, 16, group, 0)


def slot_table(lists, own, table, seen):
    for o in range(16):
        seen[o] = 0
    for j in range(MAXL):
        owner = lists[own, j] >> 4
        rank = seen[owner]
        seen[owner] = jnp.minimum(rank + 1, CAP - 1)
        table[j] = owner * CAP + rank


def pick_body(lists, counts, me, lat_ref, out_ref, table, lat, held, sem, sems):
    load = pltpu.make_async_copy(lat_ref, lat, sem.at[0])
    load.start()
    owner_table(lists, counts, me[0], table, 16)
    load.wait()
    step = SLOTS // 4
    parts = [slice(i * step, i * step + step) for i in range(4)]
    copies = [pltpu.make_async_copy(held.at[p], out_ref.at[p], sems.at[i]) for i, p in enumerate(parts)]
    for s in range(SLOTS):
        held[s] = lat[table[s] & 15]
        if s % step == step - 1:
            copies[s // step].start()
    for copy in copies:
        copy.wait()


def gather_body(table, arrived_ref, out_ref, total, sems):
    total[...] = jnp.zeros(total.shape, total.dtype)
    for s in range(SLOTS):
        total[table[s]] = total[table[s]] + arrived_ref[s].astype(f32)
    parts = [slice(i * 4, i * 4 + 4) for i in range(4)]
    copies = [pltpu.make_async_copy(total.at[p], out_ref.at[p], sems.at[i]) for i, p in enumerate(parts)]
    for copy in copies:
        copy.start()
    for copy in copies:
        copy.wait()


def take_body(lists, counts, me, arrived_ref, out_ref, table, seen):
    slot_table(lists, me[0], table, seen)
    count = counts[me[0]]
    for j in range(MAXL):
        live = j < count

        @pl.when(live)
        def _():
            out_ref[j * 16 : j * 16 + 16] = arrived_ref[table[j]]

        @pl.when(jnp.logical_not(live))
        def _():
            out_ref[j * 16 : j * 16 + 16] = jnp.zeros((16, WIDE), bf16)


def put_body(lists, counts, me, a_ref, b_ref, c_ref, d_ref, out_ref, table, seen, held, sems):
    slot_table(lists, me[0], table, seen)
    count = counts[me[0]]

    def copy(j):
        return pltpu.make_async_copy(held.at[j * 16 : j * 16 + 16], out_ref.at[table[j]], sems.at[j])

    for j in range(MAXL):
        here = slice(j * 16, j * 16 + 16)
        total = a_ref[here].astype(f32) + b_ref[here].astype(f32)
        total = total + (c_ref[here].astype(f32) + d_ref[here].astype(f32))
        held[here] = total.astype(bf16)

        @pl.when(j < count)
        def _():
            copy(j).start()

    for j in range(MAXL):

        @pl.when(j < count)
        def _():
            copy(j).wait()


def turn_body(q_ref, g_ref, qt_ref, gt_ref):
    rows = qt_ref.shape[1]
    for at in range(0, rows, 256):
        here = slice(at, at + 256)
        part = slice(at // 16, at // 16 + 16)
        q = q_ref[part].reshape(256, WIDE)
        qt_ref[:LAT, here] = q[:, :LAT].T
        rope = jnp.concatenate([q[:, LAT:], q[:, LAT:]], axis=1)
        qt_ref[LAT:, here] = rope.T[: WIDE - LAT]
        gt_ref[:, here] = g_ref[part].reshape(256, LAT).T


def two_body(near_ref, far_ref, out_ref):
    out_ref[...] = (near_ref[...].astype(f32) + far_ref[...].astype(f32)).astype(bf16)


def wrap_body(near_ref, far_ref, out_ref):
    size = out_ref.shape[0]
    out_ref[...] = (near_ref[size:].astype(f32) + far_ref[size:].astype(f32)).astype(bf16)


def next_body(near_ref, far_ref, two_ref, out_ref):
    size = out_ref.shape[0]
    total = near_ref[:size].astype(f32) + far_ref[:size].astype(f32)
    out_ref[...] = (total + two_ref[...].astype(f32)).astype(bf16)


ONCHIP = pl.BlockSpec(memory_space=pltpu.VMEM)
INPLACE = pl.BlockSpec(memory_space=pltpu.HBM)


def call(body, outs, scalars, arrays, scratch=(), direct_in=(), direct=(), alias=None, flops=None, smem_out=()):
    args = [
        pltpu.with_memory_space_constraint(a, pltpu.HBM if i in direct_in else pltpu.VMEM)
        for i, a in enumerate(arrays)
    ]
    scalars = [pltpu.with_memory_space_constraint(a, pltpu.HBM) for a in scalars]
    shapes = [
        (pltpu.HBM if i in direct or i in smem_out else pltpu.VMEM)(o.shape, o.dtype) for i, o in enumerate(outs)
    ]
    small = pl.BlockSpec(memory_space=pltpu.SMEM)
    return pl.pallas_call(
        body,
        in_specs=[small] * len(scalars)
        + [INPLACE if i in direct_in else ONCHIP for i in range(len(arrays))],
        out_specs=tuple(small if i in smem_out else INPLACE if i in direct else ONCHIP for i in range(len(outs))),
        out_shape=tuple(shapes),
        scratch_shapes=list(scratch),
        input_output_aliases=alias or {},
        cost_estimate=flops and pl.CostEstimate(flops=flops, transcendentals=0, bytes_accessed=0),
        compiler_params=pltpu.CompilerParams(vmem_limit_bytes=16 * 1024 * 1024),
    )(*scalars, *args)


def forward_body(nkeys, chunk, off, n, block, *refs):
    refs = list(refs)
    first = chunk == 0
    key_refs, bias, refs = refs[:nkeys], refs[nkeys], refs[nkeys + 1 :]
    if first:
        (q_in, g_in), refs = refs[:2], refs[2:]
        sems, refs = refs[-1], refs[:-1]
    else:
        refs = refs[len(refs) // 2 :]
    e_out, p_out, k_out, st_out, q_ref, g_ref = refs
    steps = q_ref.shape[0] * 16 // block

    def loads(i):
        part = pl.ds(i * (block // 16), block // 16)
        return (
            pltpu.make_async_copy(q_in.at[part], q_ref.at[part], sems.at[2 * i]),
            pltpu.make_async_copy(g_in.at[part], g_ref.at[part], sems.at[2 * i + 1]),
        )

    if first:
        for i in range(steps):
            for copy in loads(i):
                copy.start()
    at = off
    for ref in key_refs:
        k_out[at : at + ref.shape[0]] = ref[...]
        at += ref.shape[0]
    mine = slice(off, off + n)

    def rows(i, carry):
        here = pl.ds(pl.multiple_of(i * block, block), block)
        part = pl.ds(i * (block // 16), block // 16)
        if first:
            for copy in loads(i):
                copy.wait()
        scores = dot(q_ref[part].reshape(block, WIDE), k_out[mine], NT) + bias[...]
        top = jnp.max(scores, axis=1, keepdims=True)
        expo = jnp.exp2((scores - top) * EXPC)
        grads = dot(g_ref[part].reshape(block, LAT), k_out[mine, :LAT], NT)
        e_out[here, mine] = expo.astype(bf16)
        p_out[here, mine] = grads.astype(bf16)
        wide = lambda x: jnp.broadcast_to(x, (block, 128))
        st_out[chunk, here] = wide(top)
        st_out[3 + chunk, here] = wide(jnp.sum(expo, axis=1, keepdims=True))
        st_out[6 + chunk, here] = wide(jnp.sum(expo * grads, axis=1, keepdims=True))
        return carry

    lax.fori_loop(0, steps, rows, 0)


def forward(chunk, off, n, total_keys, key_parts, bias, state):
    first = chunk == 0
    block = 384 if first else 768
    if first:
        rows = state[0].shape[0] * 16
        side = jax.ShapeDtypeStruct((rows, total_keys), bf16)
        outs = [side, side, jax.ShapeDtypeStruct((total_keys, WIDE), bf16), jax.ShapeDtypeStruct((9, rows, 128), f32)]
    else:
        rows, outs = state[0].shape[0], []
    outs += [jax.ShapeDtypeStruct(a.shape, a.dtype) for a in state]
    start = len(key_parts) + 1
    return call(
        functools.partial(forward_body, len(key_parts), chunk, off, n, block),
        outs,
        (),
        [*key_parts, bias, *state],
        direct_in=(start, start + 1) if first else (),
        scratch=[pltpu.SemaphoreType.DMA((2 * rows // block,))] if first else [],
        alias={} if first else {start + i: i for i in range(len(state))},
        flops=2 * rows * n * (WIDE + LAT),
    )


def backward_body(chunk, offs, n, lead, final, early, step, tile, *refs):
    refs = list(refs)
    qt_ref, gt_ref, e_ref, p_ref, row_ref, k_ref = refs[:6]
    parts, refs = refs[6 : 6 + len(offs)], refs[6 + len(offs) :]
    e_out, p_out, row_out, _, s_out = refs[:5]
    held, sems = refs[-2:]
    rows = qt_ref.shape[1]
    if final:
        kept, sem = refs[5], refs[6]
        save = pltpu.make_async_copy(k_ref, kept, sem.at[0])
        save.start()
    if lead:
        for at in range(0, rows, step):
            here = slice(at, at + step)
            col = lambda c: row_ref[c, here]
            top = jnp.maximum(jnp.maximum(col(0), col(1)), col(2))
            fade = [jnp.exp2((col(c) - top) * EXPC) for c in range(3)]
            total = fade[0] * col(3) + fade[1] * col(4) + fade[2] * col(5)
            rdot = fade[0] * col(6) + fade[1] * col(7) + fade[2] * col(8)
            total = 1.0 / total
            for c in range(3):
                row_out[c, here] = fade[c] * total
            row_out[3, here] = rdot * total
    copies = []
    for ref, off in zip(parts, offs):
        for start in range(0, n, tile):
            cols = slice(off + start, off + start + tile)
            spot = len(copies)
            acc = None
            for at in range(0, rows, step):
                here = slice(at, at + step)
                a = jnp.tile(row_out[chunk, here], (1, tile // 128))
                r = jnp.tile(row_out[3, here], (1, tile // 128))
                weights = (e_ref[here, cols].astype(f32) * a).astype(bf16)
                sg = (weights.astype(f32) * (p_ref[here, cols].astype(f32) - r) * SCALE).astype(bf16)
                e_out[here, cols] = weights
                if at < early:
                    p_out[here, cols] = sg
                else:
                    held[spot, at - early : at - early + step] = sg
                key_part = dot(qt_ref[:, here], sg)
                value_part = dot(gt_ref[:, here], weights)
                if acc is None:
                    acc = [key_part[:LAT] + value_part, key_part[LAT:]]
                else:
                    acc = [acc[0] + (key_part[:LAT] + value_part), acc[1] + key_part[LAT:]]
            copies.append(pltpu.make_async_copy(held.at[spot], s_out.at[spot], sems.at[spot]))
            copies[-1].start()
            ref[start : start + tile, :LAT] = acc[0].T.astype(bf16)
            low = jnp.concatenate([acc[1], jnp.zeros_like(acc[1])], axis=0).T[:, : WIDE - LAT]
            ref[start : start + tile, LAT:] = low.astype(bf16)
    for copy in copies:
        copy.wait()
    if final:
        save.wait()


def backward(chunk, offs, n, early, qt, gt, e, p, row, k, lead=False, final=False, tile=256, step=256):
    rows = e.shape[0]
    count = len(offs)
    like = lambda a: jax.ShapeDtypeStruct(a.shape, a.dtype)
    part = jax.ShapeDtypeStruct((n, WIDE), bf16)
    merged = jax.ShapeDtypeStruct((4, rows, 128), f32) if lead else like(row)
    late = (count * n // tile, rows - early, tile)
    outs = [part] * count + [like(e), like(p), merged, like(k), jax.ShapeDtypeStruct(late, bf16)]
    alias = {2: count, 3: count + 1, 5: count + 3}
    scratch = [pltpu.VMEM(late, bf16), pltpu.SemaphoreType.DMA((late[0],))]
    direct = (count + 4,)
    if not lead:
        alias[4] = count + 2
    if final:
        outs.append(like(k))
        direct = (count + 4, count + 5)
        scratch = [pltpu.SemaphoreType.DMA((1,)), *scratch]
    return call(
        functools.partial(backward_body, chunk, offs, n, lead, final, early, step, tile),
        outs,
        (),
        (qt, gt, e, p, row, k),
        scratch=scratch,
        alias=alias,
        direct=direct,
        flops=2 * rows * n * count * (WIDE + LAT),
    )


def leaving(held, out_ref, sems, block):
    def copy(i):
        part = pl.ds(i * (block // 16), block // 16)
        return pltpu.make_async_copy(held.at[part], out_ref.at[part], sems.at[i])

    return copy


def value_body(block, early, w_ref, s_ref, k_ref, out_ref, q_ref, held, held_q, sems, sems_q):
    steps = out_ref.shape[0] * 16 // block
    leave = leaving(held, out_ref, sems, block)
    leave_q = leaving(held_q, q_ref, sems_q, block)
    for i in range(early // block):
        here = slice(i * block, i * block + block)
        part = slice(i * (block // 16), (i + 1) * (block // 16))
        held_q[part] = dot(s_ref[here], k_ref[...]).astype(bf16).reshape(block // 16, 16, WIDE)
        leave_q(i).start()

    def rows(i, carry):
        here = pl.ds(pl.multiple_of(i * block, block), block)
        part = pl.ds(i * (block // 16), block // 16)
        held[part] = dot(w_ref[here], k_ref[:, :LAT]).astype(bf16).reshape(block // 16, 16, LAT)
        leave(i).start()
        return carry

    lax.fori_loop(0, steps, rows, 0)
    for i in range(early // block):
        leave_q(i).wait()
    for i in range(steps):
        leave(i).wait()


def value_side(w, s, k, early, block=512):
    rows = w.shape[0]
    shape = (rows // 16, 16, LAT)
    dma = lambda n: pltpu.SemaphoreType.DMA((n,))
    return call(
        functools.partial(value_body, block, early),
        (jax.ShapeDtypeStruct(shape, bf16), jax.ShapeDtypeStruct((rows // 16, 16, WIDE), bf16)),
        (),
        (w, s, k),
        scratch=[
            pltpu.VMEM(shape, bf16),
            pltpu.VMEM((early // 16, 16, WIDE), bf16),
            dma(rows // block),
            dma(early // block),
        ],
        direct=(0, 1),
        flops=2 * k.shape[0] * (rows * LAT + early * WIDE),
    )


def query_body(offs, early, block, *refs):
    s_refs, (k_ref, _, out_ref, s_v, k_v, held, sems_k, sems_s, sems) = refs[: len(offs)], refs[len(offs) :]
    steps = s_v.shape[1] // block
    load_k = pltpu.make_async_copy(k_ref, k_v, sems_k.at[0])
    load_k.start()
    loads = []
    for i in range(steps):
        here = slice(i * block, i * block + block)
        loads.append(
            [
                pltpu.make_async_copy(ref.at[t, here], s_v.at[spot, here], sems_s.at[i * s_v.shape[0] + spot])
                for ref, spots in zip(s_refs, offs)
                for t, spot in enumerate(spots)
            ]
        )
        for copy in loads[-1]:
            copy.start()
    load_k.wait()
    leave = []
    for i in range(steps):
        for copy in loads[i]:
            copy.wait()
        here = slice(i * block, i * block + block)
        part = slice(i * (block // 16), (i + 1) * (block // 16))
        to = slice(early // 16 + part.start, early // 16 + part.stop)
        sg = jnp.concatenate([s_v[t, here] for t in range(s_v.shape[0])], axis=1)
        held[part] = dot(sg, k_v[...]).astype(bf16).reshape(block // 16, 16, WIDE)
        leave.append(pltpu.make_async_copy(held.at[part], out_ref.at[to], sems.at[i]))
        leave[-1].start()
    for copy in leave:
        copy.wait()


def query_side(sgs, offs, early, k, out, block=512):
    tile, rows = sgs[0].shape[2], sgs[0].shape[1]
    dma = lambda n: pltpu.SemaphoreType.DMA((n,))
    steps, tiles = rows // block, k.shape[0] // tile
    return call(
        functools.partial(query_body, [[off // tile for off in o] for o in offs], early, block),
        (jax.ShapeDtypeStruct(out.shape, bf16),),
        (),
        (*sgs, k, out),
        scratch=[
            pltpu.VMEM((tiles, rows, tile), bf16),
            pltpu.VMEM(k.shape, bf16),
            pltpu.VMEM((rows // 16, 16, WIDE), bf16),
            dma(1),
            dma(steps * tiles),
            dma(steps),
        ],
        direct_in=range(len(sgs) + 2),
        direct=(0,),
        alias={len(sgs) + 1: 0},
        flops=2 * rows * k.shape[0] * WIDE,
    )[0]


def per_device(queries, out_grad, latents, list_blocks, list_counts, valid_tokens):
    me = lax.axis_index("req")
    head = lax.axis_index("head")
    chip, core = head // 2, head % 2
    tokens = latents.shape[1]
    pair_a, pair_b, sibling = [[(h, h ^ d) for h in range(8)] for d in (2, 6, 1)]
    send = lambda a, perm: lax.ppermute(a, "head", perm)
    scalars = (list_blocks, list_counts, me.reshape(1).astype(jnp.int32))

    smem = lambda n: pltpu.SMEM((n,), jnp.int32)
    slots = jax.ShapeDtypeStruct((SLOTS, tokens, WIDE), bf16)
    keys = MAXL * tokens
    share_of = lambda n: jax.ShapeDtypeStruct((n, WIDE), bf16)

    dma = lambda n: pltpu.SemaphoreType.DMA((n,))
    outgoing, owned = call(
        pick_body,
        (slots, jax.ShapeDtypeStruct((SLOTS + 1,), jnp.int32)),
        scalars,
        (latents,),
        scratch=[
            pltpu.VMEM(latents.shape, bf16),
            pltpu.VMEM((SLOTS, tokens, WIDE), bf16),
            dma(1),
            dma(4),
        ],
        direct_in=(0,),
        direct=(0,),
        smem_out=(1,),
    )
    arrived = lax.all_to_all(outgoing.reshape(16, CAP, tokens, WIDE), "req", 0, 0, tiled=True)

    my_blocks = lax.dynamic_index_in_dim(list_blocks, me, 0, keepdims=False)
    my_count = lax.dynamic_index_in_dim(list_counts, me, 0, keepdims=False)
    ids = jnp.arange(valid_tokens.shape[0], dtype=jnp.int32)
    filled = jnp.sum(jnp.where(my_blocks[:, None] == ids[None, :], valid_tokens[None, :], 0), axis=1)
    filled = jnp.where(jnp.arange(MAXL, dtype=jnp.int32) < my_count, filled, 0)
    filled = jnp.repeat(filled, tokens)[None, :]
    offset = jnp.tile(jnp.arange(tokens, dtype=jnp.int32), MAXL)[None, :]
    at = lambda d, c: (chip ^ d) * 2 + c
    other = 1 - core
    places = [at(0, core), at(0, other), at(1, core), at(3, core), at(1, other), at(3, other), at(2, core), at(2, other)]
    first_token = jnp.stack(places)[:, None] * tokens
    bias = jnp.where(first_token + offset < filled, 0.0, BIG).astype(f32)
    bias0, bias1, bias2 = [bias[i:j].reshape(1, -1) for i, j in ((0, 2), (2, 6), (6, 8))]

    arrived, bias0, bias1, bias2 = lax.optimization_barrier((arrived, bias0, bias1, bias2))

    (share,) = call(
        take_body,
        (share_of(keys),),
        scalars,
        (arrived.reshape(slots.shape),),
        scratch=[smem(MAXL), smem(16)],
    )

    after = lambda a, *others: lax.optimization_barrier((a, *others))[0]
    every = 8 * keys
    from_b = send(share, pair_b)
    from_a = send(share, pair_a)
    s0 = send(share, sibling)
    state = forward(0, 0, 2 * keys, every, [share, s0], bias0, (queries, out_grad))
    from_b = after(from_b, state[3])
    from_a = after(from_a, state[3])
    r2 = send(from_b, pair_a)
    sa = send(from_a, sibling)
    sb = send(from_b, sibling)
    state = forward(1, 2 * keys, 4 * keys, every, [from_a, from_b, sa, sb], bias1, state)
    r2 = after(r2, state[3])
    s3 = send(r2, sibling)
    flat = lambda a: jax.ShapeDtypeStruct((a.shape[2], a.shape[0] * a.shape[1]), bf16)
    e, p, k, row, q, g = state
    qt, gt = call(turn_body, (flat(queries), flat(out_grad)), (), (q, after(g, r2)))
    e, p, k, row, q, g = forward(2, 6 * keys, 2 * keys, every, [r2, s3], bias2, (e, p, k, after(row, gt), q, g))

    fold = lambda a: a.reshape(-1, tokens, WIDE)
    unfold = lambda a: a.reshape(-1, WIDE)
    early = 512
    back = functools.partial(backward, early=early, qt=qt, gt=gt)
    far2, e, p, row, k, sg2f = back(2, (7 * keys,), keys, e=e, p=p, row=row, k=k, lead=True)
    mate2 = send(far2, sibling)
    near2, e, p, row, k, sg2n = back(2, (6 * keys,), keys, e=e, p=p, row=row, k=k)
    far0, e, p, row, k, sg0f = back(0, (keys,), keys, e=e, p=p, row=row, k=k)
    (two,) = call(two_body, (share_of(keys),), (), (after(near2, far0), mate2))
    got_two = send(two, pair_b)
    far1, e, p, row, k, sg1f, k_saved = back(1, (4 * keys,), 2 * keys, e=e, p=p, row=after(row, two), k=k, final=True)
    mate1 = unfold(send(fold(far1), sibling))
    near1, e, p, row, k, sg1n = back(1, (2 * keys,), 2 * keys, e=e, p=p, row=row, k=k)
    mate0 = send(far0, sibling)
    (to_b,) = call(wrap_body, (share_of(keys),), (), (near1, mate1))
    got_b = send(to_b, pair_b)
    near0, e, p, row, k, sg0n = back(0, (0,), keys, e=e, p=p, row=after(row, to_b), k=k)
    (to_a,) = call(next_body, (share_of(keys),), (), (after(near1, near0), mate1, got_two))
    got_a = send(to_a, pair_a)
    attended, query_grad = value_side(e, p, after(k, to_a), early)
    near0 = after(near0, attended)
    (slot_grads,) = call(
        put_body,
        (slots,),
        scalars,
        (near0, mate0, got_a, got_b),
        scratch=[smem(MAXL), smem(16), pltpu.VMEM((keys, WIDE), bf16), dma(MAXL)],
        direct=(0,),
    )
    k_saved = after(k_saved, slot_grads)
    query_grad = query_side(
        (sg2f, sg2n, sg0f, sg0n, sg1f, sg1n),
        ((7 * keys,), (6 * keys,), (keys,), (0,), (4 * keys, 5 * keys), (2 * keys, 3 * keys)),
        early,
        k_saved,
        query_grad,
    )
    returned = lax.all_to_all(slot_grads.reshape(16, CAP, tokens, WIDE), "req", 0, 0, tiled=True)
    (latent_grad,) = call(
        gather_body,
        (jax.ShapeDtypeStruct((16, tokens, WIDE), f32),),
        (owned,),
        (returned.reshape(slots.shape),),
        scratch=[pltpu.VMEM((17, tokens, WIDE), f32), dma(4)],
        direct=(0,),
    )
    return (attended, query_grad, latent_grad)


def solution(mesh):
    in_specs = (
        P("req", "head", None),
        P("req", "head", None),
        P("req", "head", None),
        P(),
        P(),
        P(),
    )
    out_specs = (P("req", "head", None), P("req", "head", None), P("req", "head", None))
    return jax.shard_map(per_device, mesh=mesh, in_specs=in_specs, out_specs=out_specs, check_vma=False)
```

```python
import functools
import math

import jax
import jax.numpy as jnp
from jax import lax
from jax.experimental import pallas as pl
from jax.experimental.pallas import tpu as pltpu
from jax.sharding import PartitionSpec as P


LAT = 512
WIDE = 576
MAXL = 16
CAP = 2
BIG = -1e30
SLOTS = 16 * CAP
SCALE = 192.0 ** (-0.5)
EXPC = SCALE * math.log2(math.e)
NT = (((1,), (1,)), ((), ()))
NN = (((1,), (0,)), ((), ()))
f32 = jnp.float32
bf16 = jnp.bfloat16


def dot(a, b, dims=NN):
    return lax.dot_general(a, b, dims, preferred_element_type=f32)


def owner_table(lists, counts, own, table, empty, low=0, high=16):
    def group(g, carry):
        table[g * CAP] = empty
        table[g * CAP + 1] = empty
        rank = jnp.int32(0)
        for j in range(MAXL):
            block = lists[g, j]
            mine = ((block >> 4) == own) & (j < counts[g])
            table[jnp.where(mine, g * CAP + rank, SLOTS)] = block & 15
            rank = jnp.where(mine, jnp.minimum(rank + 1, CAP - 1), rank)
        return carry

    lax.fori_loop(low, high, group, 0)


def slot_table(lists, own, table, seen):
    for o in range(16):
        seen[o] = 0
    for j in range(MAXL):
        owner = lists[own, j] >> 4
        rank = seen[owner]
        seen[owner] = jnp.minimum(rank + 1, CAP - 1)
        table[j] = owner * CAP + rank


def pick_body(lists, counts, me, lat_ref, out_ref, table, lat, held, sem, sems):
    load = pltpu.make_async_copy(lat_ref, lat, sem.at[0])
    load.start()
    step = SLOTS // 4
    parts = [slice(i * step, i * step + step) for i in range(4)]
    copies = [pltpu.make_async_copy(held.at[p], out_ref.at[p], sems.at[i]) for i, p in enumerate(parts)]
    for i, copy in enumerate(copies):
        owner_table(lists, counts, me[0], table, 16, 4 * i, 4 * i + 4)
        if i == 0:
            load.wait()
        for s in range(i * step, i * step + step):
            held[s] = lat[table[s] & 15]
        copy.start()
    for copy in copies:
        copy.wait()


def gather_body(table, arrived_ref, out_ref, total, sems):
    total[...] = jnp.zeros(total.shape, total.dtype)
    for s in range(SLOTS):
        total[table[s]] = total[table[s]] + arrived_ref[s].astype(f32)
    parts = [slice(i * 4, i * 4 + 4) for i in range(4)]
    copies = [pltpu.make_async_copy(total.at[p], out_ref.at[p], sems.at[i]) for i, p in enumerate(parts)]
    for copy in copies:
        copy.start()
    for copy in copies:
        copy.wait()


def take_body(lists, counts, me, arrived_ref, out_ref, table, seen):
    slot_table(lists, me[0], table, seen)
    count = counts[me[0]]
    for j in range(MAXL):
        live = j < count

        @pl.when(live)
        def _():
            out_ref[j * 16 : j * 16 + 16] = arrived_ref[table[j]]

        @pl.when(jnp.logical_not(live))
        def _():
            out_ref[j * 16 : j * 16 + 16] = jnp.zeros((16, WIDE), bf16)


def put_body(lists, counts, me, a_ref, b_ref, c_ref, d_ref, out_ref, table, seen, held, sems):
    slot_table(lists, me[0], table, seen)
    count = counts[me[0]]

    def copy(j):
        return pltpu.make_async_copy(held.at[j * 16 : j * 16 + 16], out_ref.at[table[j]], sems.at[j])

    for j in range(MAXL):
        here = slice(j * 16, j * 16 + 16)
        total = a_ref[here].astype(f32) + b_ref[here].astype(f32)
        total = total + (c_ref[here].astype(f32) + d_ref[here].astype(f32))
        held[here] = total.astype(bf16)

        @pl.when(j < count)
        def _():
            copy(j).start()

    for j in range(MAXL):

        @pl.when(j < count)
        def _():
            copy(j).wait()


def turn_body(q_ref, g_ref, qt_ref, gt_ref):
    rows = qt_ref.shape[1]
    for at in range(0, rows, 256):
        here = slice(at, at + 256)
        part = slice(at // 16, at // 16 + 16)
        q = q_ref[part].reshape(256, WIDE)
        qt_ref[:LAT, here] = q[:, :LAT].T
        rope = jnp.concatenate([q[:, LAT:], q[:, LAT:]], axis=1)
        qt_ref[LAT:, here] = rope.T[: WIDE - LAT]
        gt_ref[:, here] = g_ref[part].reshape(256, LAT).T


def two_body(near_ref, far_ref, out_ref):
    out_ref[...] = (near_ref[...].astype(f32) + far_ref[...].astype(f32)).astype(bf16)


def wrap_body(near_ref, far_ref, out_ref):
    size = out_ref.shape[0]
    out_ref[...] = (near_ref[size:].astype(f32) + far_ref[size:].astype(f32)).astype(bf16)


def next_body(near_ref, far_ref, two_ref, out_ref):
    size = out_ref.shape[0]
    total = near_ref[:size].astype(f32) + far_ref[:size].astype(f32)
    out_ref[...] = (total + two_ref[...].astype(f32)).astype(bf16)


ONCHIP = pl.BlockSpec(memory_space=pltpu.VMEM)
INPLACE = pl.BlockSpec(memory_space=pltpu.HBM)


def call(body, outs, scalars, arrays, scratch=(), direct_in=(), direct=(), alias=None, flops=None, smem_out=()):
    args = [
        pltpu.with_memory_space_constraint(a, pltpu.HBM if i in direct_in else pltpu.VMEM)
        for i, a in enumerate(arrays)
    ]
    scalars = [pltpu.with_memory_space_constraint(a, pltpu.HBM) for a in scalars]
    shapes = [
        (pltpu.HBM if i in direct or i in smem_out else pltpu.VMEM)(o.shape, o.dtype) for i, o in enumerate(outs)
    ]
    small = pl.BlockSpec(memory_space=pltpu.SMEM)
    return pl.pallas_call(
        body,
        in_specs=[small] * len(scalars)
        + [INPLACE if i in direct_in else ONCHIP for i in range(len(arrays))],
        out_specs=tuple(small if i in smem_out else INPLACE if i in direct else ONCHIP for i in range(len(outs))),
        out_shape=tuple(shapes),
        scratch_shapes=list(scratch),
        input_output_aliases=alias or {},
        cost_estimate=flops and pl.CostEstimate(flops=flops, transcendentals=0, bytes_accessed=0),
        compiler_params=pltpu.CompilerParams(vmem_limit_bytes=16 * 1024 * 1024),
    )(*scalars, *args)


def forward_body(nkeys, chunk, off, n, block, *refs):
    refs = list(refs)
    first = chunk == 0
    key_refs, bias, refs = refs[:nkeys], refs[nkeys], refs[nkeys + 1 :]
    if first:
        (q_in, g_in), refs = refs[:2], refs[2:]
        sems, refs = refs[-1], refs[:-1]
    else:
        refs = refs[len(refs) // 2 :]
    e_out, p_out, k_out, st_out, q_ref, g_ref = refs
    steps = q_ref.shape[0] * 16 // block

    def loads(i):
        part = pl.ds(i * (block // 16), block // 16)
        return (
            pltpu.make_async_copy(q_in.at[part], q_ref.at[part], sems.at[2 * i]),
            pltpu.make_async_copy(g_in.at[part], g_ref.at[part], sems.at[2 * i + 1]),
        )

    if first:
        for i in range(steps):
            for copy in loads(i):
                copy.start()
    at = off
    for ref in key_refs:
        k_out[at : at + ref.shape[0]] = ref[...]
        at += ref.shape[0]
    mine = slice(off, off + n)

    def rows(i, carry):
        here = pl.ds(pl.multiple_of(i * block, block), block)
        part = pl.ds(i * (block // 16), block // 16)
        if first:
            loads(i)[0].wait()
        scores = dot(q_ref[part].reshape(block, WIDE), k_out[mine], NT) + bias[...]
        top = jnp.max(scores, axis=1, keepdims=True)
        expo = jnp.exp2((scores - top) * EXPC)
        if first:
            loads(i)[1].wait()
        grads = dot(g_ref[part].reshape(block, LAT), k_out[mine, :LAT], NT)
        e_out[here, mine] = expo.astype(bf16)
        p_out[here, mine] = grads.astype(bf16)
        wide = lambda x: jnp.broadcast_to(x, (block, 128))
        st_out[chunk, here] = wide(top)
        st_out[3 + chunk, here] = wide(jnp.sum(expo, axis=1, keepdims=True))
        st_out[6 + chunk, here] = wide(jnp.sum(expo * grads, axis=1, keepdims=True))
        return carry

    lax.fori_loop(0, steps, rows, 0)


def forward(chunk, off, n, total_keys, key_parts, bias, state):
    first = chunk == 0
    block = 384 if first else 768
    if first:
        rows = state[0].shape[0] * 16
        side = jax.ShapeDtypeStruct((rows, total_keys), bf16)
        outs = [side, side, jax.ShapeDtypeStruct((total_keys, WIDE), bf16), jax.ShapeDtypeStruct((9, rows, 128), f32)]
    else:
        rows, outs = state[0].shape[0], []
    outs += [jax.ShapeDtypeStruct(a.shape, a.dtype) for a in state]
    start = len(key_parts) + 1
    return call(
        functools.partial(forward_body, len(key_parts), chunk, off, n, block),
        outs,
        (),
        [*key_parts, bias, *state],
        direct_in=(start, start + 1) if first else (),
        scratch=[pltpu.SemaphoreType.DMA((2 * rows // block,))] if first else [],
        alias={} if first else {start + i: i for i in range(len(state))},
        flops=2 * rows * n * (WIDE + LAT),
    )


def backward_body(chunk, offs, n, lead, final, early, step, tile, *refs):
    refs = list(refs)
    qt_ref, gt_ref, e_ref, p_ref, row_ref, k_ref = refs[:6]
    parts, refs = refs[6 : 6 + len(offs)], refs[6 + len(offs) :]
    e_out, p_out, row_out, _, s_out = refs[:5]
    held, sems = refs[-2:]
    rows = qt_ref.shape[1]
    if final:
        kept, sem = refs[5], refs[6]
        save = pltpu.make_async_copy(k_ref, kept, sem.at[0])
        save.start()
    if lead:
        for at in range(0, rows, step):
            here = slice(at, at + step)
            col = lambda c: row_ref[c, here]
            top = jnp.maximum(jnp.maximum(col(0), col(1)), col(2))
            fade = [jnp.exp2((col(c) - top) * EXPC) for c in range(3)]
            total = fade[0] * col(3) + fade[1] * col(4) + fade[2] * col(5)
            rdot = fade[0] * col(6) + fade[1] * col(7) + fade[2] * col(8)
            total = 1.0 / total
            for c in range(3):
                row_out[c, here] = fade[c] * total
            row_out[3, here] = rdot * total
    copies = []
    for ref, off in zip(parts, offs):
        for start in range(0, n, tile):
            cols = slice(off + start, off + start + tile)
            spot = len(copies)
            acc = None
            for at in range(0, rows, step):
                here = slice(at, at + step)
                a = jnp.tile(row_out[chunk, here], (1, tile // 128))
                r = jnp.tile(row_out[3, here], (1, tile // 128))
                weights = (e_ref[here, cols].astype(f32) * a).astype(bf16)
                sg = (weights.astype(f32) * (p_ref[here, cols].astype(f32) - r) * SCALE).astype(bf16)
                e_out[here, cols] = weights
                if at < early:
                    p_out[here, cols] = sg
                else:
                    held[spot, at - early : at - early + step] = sg
                key_part = dot(qt_ref[:, here], sg)
                value_part = dot(gt_ref[:, here], weights)
                if acc is None:
                    acc = [key_part[:LAT] + value_part, key_part[LAT:]]
                else:
                    acc = [acc[0] + (key_part[:LAT] + value_part), acc[1] + key_part[LAT:]]
            copies.append(pltpu.make_async_copy(held.at[spot], s_out.at[spot], sems.at[spot]))
            copies[-1].start()
            ref[start : start + tile, :LAT] = acc[0].T.astype(bf16)
            low = jnp.concatenate([acc[1], jnp.zeros_like(acc[1])], axis=0).T[:, : WIDE - LAT]
            ref[start : start + tile, LAT:] = low.astype(bf16)
    for copy in copies:
        copy.wait()
    if final:
        save.wait()


def backward(chunk, offs, n, early, qt, gt, e, p, row, k, lead=False, final=False, tile=256, step=256):
    rows = e.shape[0]
    count = len(offs)
    like = lambda a: jax.ShapeDtypeStruct(a.shape, a.dtype)
    part = jax.ShapeDtypeStruct((n, WIDE), bf16)
    merged = jax.ShapeDtypeStruct((4, rows, 128), f32) if lead else like(row)
    late = (count * n // tile, rows - early, tile)
    outs = [part] * count + [like(e), like(p), merged, like(k), jax.ShapeDtypeStruct(late, bf16)]
    alias = {2: count, 3: count + 1, 5: count + 3}
    scratch = [pltpu.VMEM(late, bf16), pltpu.SemaphoreType.DMA((late[0],))]
    direct = (count + 4,)
    if not lead:
        alias[4] = count + 2
    if final:
        outs.append(like(k))
        direct = (count + 4, count + 5)
        scratch = [pltpu.SemaphoreType.DMA((1,)), *scratch]
    return call(
        functools.partial(backward_body, chunk, offs, n, lead, final, early, step, tile),
        outs,
        (),
        (qt, gt, e, p, row, k),
        scratch=scratch,
        alias=alias,
        direct=direct,
        flops=2 * rows * n * count * (WIDE + LAT),
    )


def leaving(held, out_ref, sems, block):
    def copy(i):
        part = pl.ds(i * (block // 16), block // 16)
        return pltpu.make_async_copy(held.at[part], out_ref.at[part], sems.at[i])

    return copy


def value_body(block, early, w_ref, s_ref, k_ref, out_ref, q_ref, held, held_q, sems, sems_q):
    steps = out_ref.shape[0] * 16 // block
    leave = leaving(held, out_ref, sems, block)
    leave_q = leaving(held_q, q_ref, sems_q, block)
    for i in range(early // block):
        here = slice(i * block, i * block + block)
        part = slice(i * (block // 16), (i + 1) * (block // 16))
        held_q[part] = dot(s_ref[here], k_ref[...]).astype(bf16).reshape(block // 16, 16, WIDE)
        leave_q(i).start()

    def rows(i, carry):
        here = pl.ds(pl.multiple_of(i * block, block), block)
        part = pl.ds(i * (block // 16), block // 16)
        held[part] = dot(w_ref[here], k_ref[:, :LAT]).astype(bf16).reshape(block // 16, 16, LAT)
        leave(i).start()
        return carry

    lax.fori_loop(0, steps, rows, 0)
    for i in range(early // block):
        leave_q(i).wait()
    for i in range(steps):
        leave(i).wait()


def value_side(w, s, k, early, block=512):
    rows = w.shape[0]
    shape = (rows // 16, 16, LAT)
    dma = lambda n: pltpu.SemaphoreType.DMA((n,))
    return call(
        functools.partial(value_body, block, early),
        (jax.ShapeDtypeStruct(shape, bf16), jax.ShapeDtypeStruct((rows // 16, 16, WIDE), bf16)),
        (),
        (w, s, k),
        scratch=[
            pltpu.VMEM(shape, bf16),
            pltpu.VMEM((early // 16, 16, WIDE), bf16),
            dma(rows // block),
            dma(early // block),
        ],
        direct=(0, 1),
        flops=2 * k.shape[0] * (rows * LAT + early * WIDE),
    )


def query_body(offs, early, block, *refs):
    s_refs, (k_ref, _, out_ref, s_v, k_v, held, sems_k, sems_s, sems) = refs[: len(offs)], refs[len(offs) :]
    steps = s_v.shape[1] // block
    load_k = pltpu.make_async_copy(k_ref, k_v, sems_k.at[0])
    load_k.start()
    loads = []
    for i in range(steps):
        here = slice(i * block, i * block + block)
        loads.append(
            [
                pltpu.make_async_copy(ref.at[t, here], s_v.at[spot, here], sems_s.at[i * s_v.shape[0] + spot])
                for ref, spots in zip(s_refs, offs)
                for t, spot in enumerate(spots)
            ]
        )
        for copy in loads[-1]:
            copy.start()
    load_k.wait()
    leave = []
    for i in range(steps):
        for copy in loads[i]:
            copy.wait()
        here = slice(i * block, i * block + block)
        part = slice(i * (block // 16), (i + 1) * (block // 16))
        to = slice(early // 16 + part.start, early // 16 + part.stop)
        sg = jnp.concatenate([s_v[t, here] for t in range(s_v.shape[0])], axis=1)
        held[part] = dot(sg, k_v[...]).astype(bf16).reshape(block // 16, 16, WIDE)
        leave.append(pltpu.make_async_copy(held.at[part], out_ref.at[to], sems.at[i]))
        leave[-1].start()
    for copy in leave:
        copy.wait()


def query_side(sgs, offs, early, k, out, block=512):
    tile, rows = sgs[0].shape[2], sgs[0].shape[1]
    dma = lambda n: pltpu.SemaphoreType.DMA((n,))
    steps, tiles = rows // block, k.shape[0] // tile
    return call(
        functools.partial(query_body, [[off // tile for off in o] for o in offs], early, block),
        (jax.ShapeDtypeStruct(out.shape, bf16),),
        (),
        (*sgs, k, out),
        scratch=[
            pltpu.VMEM((tiles, rows, tile), bf16),
            pltpu.VMEM(k.shape, bf16),
            pltpu.VMEM((rows // 16, 16, WIDE), bf16),
            dma(1),
            dma(steps * tiles),
            dma(steps),
        ],
        direct_in=range(len(sgs) + 2),
        direct=(0,),
        alias={len(sgs) + 1: 0},
        flops=2 * rows * k.shape[0] * WIDE,
    )[0]


def per_device(queries, out_grad, latents, list_blocks, list_counts, valid_tokens):
    me = lax.axis_index("req")
    head = lax.axis_index("head")
    chip, core = head // 2, head % 2
    tokens = latents.shape[1]
    pair_a, pair_b, sibling = [[(h, h ^ d) for h in range(8)] for d in (2, 6, 1)]
    send = lambda a, perm: lax.ppermute(a, "head", perm)
    scalars = (list_blocks, list_counts, me.reshape(1).astype(jnp.int32))

    smem = lambda n: pltpu.SMEM((n,), jnp.int32)
    slots = jax.ShapeDtypeStruct((SLOTS, tokens, WIDE), bf16)
    keys = MAXL * tokens
    share_of = lambda n: jax.ShapeDtypeStruct((n, WIDE), bf16)

    dma = lambda n: pltpu.SemaphoreType.DMA((n,))
    outgoing, owned = call(
        pick_body,
        (slots, jax.ShapeDtypeStruct((SLOTS + 1,), jnp.int32)),
        scalars,
        (latents,),
        scratch=[
            pltpu.VMEM(latents.shape, bf16),
            pltpu.VMEM((SLOTS, tokens, WIDE), bf16),
            dma(1),
            dma(4),
        ],
        direct_in=(0,),
        direct=(0,),
        smem_out=(1,),
    )
    arrived = lax.all_to_all(outgoing.reshape(16, CAP, tokens, WIDE), "req", 0, 0, tiled=True)

    my_blocks = lax.dynamic_index_in_dim(list_blocks, me, 0, keepdims=False)
    my_count = lax.dynamic_index_in_dim(list_counts, me, 0, keepdims=False)
    ids = jnp.arange(valid_tokens.shape[0], dtype=jnp.int32)
    filled = jnp.sum(jnp.where(my_blocks[:, None] == ids[None, :], valid_tokens[None, :], 0), axis=1)
    filled = jnp.where(jnp.arange(MAXL, dtype=jnp.int32) < my_count, filled, 0)
    filled = jnp.repeat(filled, tokens)[None, :]
    offset = jnp.tile(jnp.arange(tokens, dtype=jnp.int32), MAXL)[None, :]
    at = lambda d, c: (chip ^ d) * 2 + c
    other = 1 - core
    places = [at(0, core), at(0, other), at(1, core), at(3, core), at(1, other), at(3, other), at(2, core), at(2, other)]
    first_token = jnp.stack(places)[:, None] * tokens
    bias = jnp.where(first_token + offset < filled, 0.0, BIG).astype(f32)
    bias0, bias1, bias2 = [bias[i:j].reshape(1, -1) for i, j in ((0, 2), (2, 6), (6, 8))]

    arrived, bias0, bias1, bias2 = lax.optimization_barrier((arrived, bias0, bias1, bias2))

    (share,) = call(
        take_body,
        (share_of(keys),),
        scalars,
        (arrived.reshape(slots.shape),),
        scratch=[smem(MAXL), smem(16)],
    )

    after = lambda a, *others: lax.optimization_barrier((a, *others))[0]
    every = 8 * keys
    from_b = send(share, pair_b)
    from_a = send(share, pair_a)
    s0 = send(share, sibling)
    state = forward(0, 0, 2 * keys, every, [share, s0], bias0, (queries, out_grad))
    from_b = after(from_b, state[3])
    from_a = after(from_a, state[3])
    r2 = send(from_b, pair_a)
    sa = send(from_a, sibling)
    sb = send(from_b, sibling)
    state = forward(1, 2 * keys, 4 * keys, every, [from_a, from_b, sa, sb], bias1, state)
    r2 = after(r2, state[3])
    s3 = send(r2, sibling)
    flat = lambda a: jax.ShapeDtypeStruct((a.shape[2], a.shape[0] * a.shape[1]), bf16)
    e, p, k, row, q, g = state
    qt, gt = call(turn_body, (flat(queries), flat(out_grad)), (), (q, after(g, r2)))
    e, p, k, row, q, g = forward(2, 6 * keys, 2 * keys, every, [r2, s3], bias2, (e, p, k, after(row, gt), q, g))

    fold = lambda a: a.reshape(-1, tokens, WIDE)
    unfold = lambda a: a.reshape(-1, WIDE)
    early = 512
    back = functools.partial(backward, early=early, qt=qt, gt=gt)
    far2, e, p, row, k, sg2f = back(2, (7 * keys,), keys, e=e, p=p, row=row, k=k, lead=True)
    mate2 = send(far2, sibling)
    near2, e, p, row, k, sg2n = back(2, (6 * keys,), keys, e=e, p=p, row=row, k=k)
    far0, e, p, row, k, sg0f = back(0, (keys,), keys, e=e, p=p, row=row, k=k)
    (two,) = call(two_body, (share_of(keys),), (), (after(near2, far0), mate2))
    got_two = send(two, pair_b)
    far1, e, p, row, k, sg1f, k_saved = back(1, (4 * keys,), 2 * keys, e=e, p=p, row=after(row, two), k=k, final=True)
    mate1 = unfold(send(fold(far1), sibling))
    near1, e, p, row, k, sg1n = back(1, (2 * keys,), 2 * keys, e=e, p=p, row=row, k=k)
    mate0 = send(far0, sibling)
    (to_b,) = call(wrap_body, (share_of(keys),), (), (near1, mate1))
    got_b = send(to_b, pair_b)
    (to_a,) = call(next_body, (share_of(keys),), (), (after(near1, to_b), mate1, got_two))
    got_a = send(to_a, pair_a)
    near0, e, p, row, k, sg0n = back(0, (0,), keys, e=e, p=p, row=after(row, to_a), k=k)
    attended, query_grad = value_side(e, p, after(k, to_a), early)
    near0 = after(near0, attended)
    (slot_grads,) = call(
        put_body,
        (slots,),
        scalars,
        (near0, mate0, got_a, got_b),
        scratch=[smem(MAXL), smem(16), pltpu.VMEM((keys, WIDE), bf16), dma(MAXL)],
        direct=(0,),
    )
    k_saved = after(k_saved, slot_grads)
    query_grad = query_side(
        (sg2f, sg2n, sg0f, sg0n, sg1f, sg1n),
        ((7 * keys,), (6 * keys,), (keys,), (0,), (4 * keys, 5 * keys), (2 * keys, 3 * keys)),
        early,
        k_saved,
        query_grad,
    )
    returned = lax.all_to_all(slot_grads.reshape(16, CAP, tokens, WIDE), "req", 0, 0, tiled=True)
    (latent_grad,) = call(
        gather_body,
        (jax.ShapeDtypeStruct((16, tokens, WIDE), f32),),
        (owned,),
        (returned.reshape(slots.shape),),
        scratch=[pltpu.VMEM((17, tokens, WIDE), f32), dma(4)],
        direct=(0,),
    )
    return (attended, query_grad, latent_grad)


def solution(mesh):
    in_specs = (
        P("req", "head", None),
        P("req", "head", None),
        P("req", "head", None),
        P(),
        P(),
        P(),
    )
    out_specs = (P("req", "head", None), P("req", "head", None), P("req", "head", None))
    return jax.shard_map(per_device, mesh=mesh, in_specs=in_specs, out_specs=out_specs, check_vma=False)
```

```python
import functools
import math

import jax
import jax.numpy as jnp
from jax import lax
from jax.experimental import pallas as pl
from jax.experimental.pallas import tpu as pltpu
from jax.sharding import PartitionSpec as P


LAT = 512
WIDE = 576
MAXL = 16
CAP = 2
BIG = -1e30
SLOTS = 16 * CAP
SCALE = 192.0 ** (-0.5)
EXPC = SCALE * math.log2(math.e)
NT = (((1,), (1,)), ((), ()))
NN = (((1,), (0,)), ((), ()))
f32 = jnp.float32
bf16 = jnp.bfloat16


def dot(a, b, dims=NN):
    return lax.dot_general(a, b, dims, preferred_element_type=f32)


def owner_table(lists, counts, own, table, empty):
    def group(g, carry):
        table[g * CAP] = empty
        table[g * CAP + 1] = empty
        rank = jnp.int32(0)
        for j in range(MAXL):
            block = lists[g, j]
            mine = ((block >> 4) == own) & (j < counts[g])
            table[jnp.where(mine, g * CAP + rank, SLOTS)] = block & 15
            rank = jnp.where(mine, jnp.minimum(rank + 1, CAP - 1), rank)
        return carry

    lax.fori_loop(0, 16, group, 0)


def slot_table(lists, own, table, seen):
    for o in range(16):
        seen[o] = 0
    for j in range(MAXL):
        owner = lists[own, j] >> 4
        rank = seen[owner]
        seen[owner] = jnp.minimum(rank + 1, CAP - 1)
        table[j] = owner * CAP + rank


def pick_body(lists, counts, me, lat_ref, out_ref, table, lat, held, sem, sems):
    load = pltpu.make_async_copy(lat_ref, lat, sem.at[0])
    load.start()
    owner_table(lists, counts, me[0], table, 16)
    load.wait()
    step = SLOTS // 4
    parts = [slice(i * step, i * step + step) for i in range(4)]
    copies = [pltpu.make_async_copy(held.at[p], out_ref.at[p], sems.at[i]) for i, p in enumerate(parts)]
    for i, copy in enumerate(copies):
        for s in range(i * step, i * step + step):
            held[s] = lat[table[s] & 15]
        copy.start()
    for copy in copies:
        copy.wait()


def gather_body(table, arrived_ref, out_ref, total, sems):
    total[...] = jnp.zeros(total.shape, total.dtype)
    for s in range(SLOTS):
        total[table[s]] = total[table[s]] + arrived_ref[s].astype(f32)
    parts = [slice(i * 4, i * 4 + 4) for i in range(4)]
    copies = [pltpu.make_async_copy(total.at[p], out_ref.at[p], sems.at[i]) for i, p in enumerate(parts)]
    for copy in copies:
        copy.start()
    for copy in copies:
        copy.wait()


def take_body(lists, counts, me, arrived_ref, out_ref, table, seen):
    slot_table(lists, me[0], table, seen)
    count = counts[me[0]]
    for j in range(MAXL):
        live = j < count

        @pl.when(live)
        def _():
            out_ref[j * 16 : j * 16 + 16] = arrived_ref[table[j]]

        @pl.when(jnp.logical_not(live))
        def _():
            out_ref[j * 16 : j * 16 + 16] = jnp.zeros((16, WIDE), bf16)


def put_body(lists, counts, me, a_ref, b_ref, c_ref, d_ref, out_ref, table, seen, held, sems):
    slot_table(lists, me[0], table, seen)
    count = counts[me[0]]

    def copy(j):
        return pltpu.make_async_copy(held.at[j * 16 : j * 16 + 16], out_ref.at[table[j]], sems.at[j])

    for j in range(MAXL):
        here = slice(j * 16, j * 16 + 16)
        total = a_ref[here].astype(f32) + b_ref[here].astype(f32)
        total = total + (c_ref[here].astype(f32) + d_ref[here].astype(f32))
        held[here] = total.astype(bf16)

        @pl.when(j < count)
        def _():
            copy(j).start()

    for j in range(MAXL):

        @pl.when(j < count)
        def _():
            copy(j).wait()


def turn_body(q_ref, g_ref, qt_ref, gt_ref):
    rows = qt_ref.shape[1]
    for at in range(0, rows, 256):
        here = slice(at, at + 256)
        part = slice(at // 16, at // 16 + 16)
        q = q_ref[part].reshape(256, WIDE)
        qt_ref[:LAT, here] = q[:, :LAT].T
        rope = jnp.concatenate([q[:, LAT:], q[:, LAT:]], axis=1)
        qt_ref[LAT:, here] = rope.T[: WIDE - LAT]
        gt_ref[:, here] = g_ref[part].reshape(256, LAT).T


def two_body(near_ref, far_ref, out_ref):
    out_ref[...] = (near_ref[...].astype(f32) + far_ref[...].astype(f32)).astype(bf16)


def wrap_body(near_ref, far_ref, out_ref):
    size = out_ref.shape[0]
    out_ref[...] = (near_ref[size:].astype(f32) + far_ref[size:].astype(f32)).astype(bf16)


def next_body(near_ref, far_ref, two_ref, out_ref):
    size = out_ref.shape[0]
    total = near_ref[:size].astype(f32) + far_ref[:size].astype(f32)
    out_ref[...] = (total + two_ref[...].astype(f32)).astype(bf16)


ONCHIP = pl.BlockSpec(memory_space=pltpu.VMEM)
INPLACE = pl.BlockSpec(memory_space=pltpu.HBM)


def call(body, outs, scalars, arrays, scratch=(), direct_in=(), direct=(), alias=None, flops=None, smem_out=()):
    args = [
        pltpu.with_memory_space_constraint(a, pltpu.HBM if i in direct_in else pltpu.VMEM)
        for i, a in enumerate(arrays)
    ]
    scalars = [pltpu.with_memory_space_constraint(a, pltpu.HBM) for a in scalars]
    shapes = [
        (pltpu.HBM if i in direct or i in smem_out else pltpu.VMEM)(o.shape, o.dtype) for i, o in enumerate(outs)
    ]
    small = pl.BlockSpec(memory_space=pltpu.SMEM)
    return pl.pallas_call(
        body,
        in_specs=[small] * len(scalars)
        + [INPLACE if i in direct_in else ONCHIP for i in range(len(arrays))],
        out_specs=tuple(small if i in smem_out else INPLACE if i in direct else ONCHIP for i in range(len(outs))),
        out_shape=tuple(shapes),
        scratch_shapes=list(scratch),
        input_output_aliases=alias or {},
        cost_estimate=flops and pl.CostEstimate(flops=flops, transcendentals=0, bytes_accessed=0),
        compiler_params=pltpu.CompilerParams(vmem_limit_bytes=16 * 1024 * 1024),
    )(*scalars, *args)


def forward_body(nkeys, chunk, off, n, block, *refs):
    refs = list(refs)
    first = chunk == 0
    key_refs, bias, refs = refs[:nkeys], refs[nkeys], refs[nkeys + 1 :]
    if first:
        (q_in, g_in), refs = refs[:2], refs[2:]
        sems, refs = refs[-1], refs[:-1]
    else:
        refs = refs[len(refs) // 2 :]
    e_out, p_out, k_out, st_out, q_ref, g_ref = refs
    steps = q_ref.shape[0] * 16 // block

    def loads(i):
        part = pl.ds(i * (block // 16), block // 16)
        return (
            pltpu.make_async_copy(q_in.at[part], q_ref.at[part], sems.at[2 * i]),
            pltpu.make_async_copy(g_in.at[part], g_ref.at[part], sems.at[2 * i + 1]),
        )

    if first:
        for i in range(steps):
            for copy in loads(i):
                copy.start()
    at = off
    for ref in key_refs:
        k_out[at : at + ref.shape[0]] = ref[...]
        at += ref.shape[0]
    mine = slice(off, off + n)

    def rows(i, carry):
        here = pl.ds(pl.multiple_of(i * block, block), block)
        part = pl.ds(i * (block // 16), block // 16)
        if first:
            for copy in loads(i):
                copy.wait()
        scores = dot(q_ref[part].reshape(block, WIDE), k_out[mine], NT) + bias[...]
        top = jnp.max(scores, axis=1, keepdims=True)
        expo = jnp.exp2((scores - top) * EXPC)
        grads = dot(g_ref[part].reshape(block, LAT), k_out[mine, :LAT], NT)
        e_out[here, mine] = expo.astype(bf16)
        p_out[here, mine] = grads.astype(bf16)
        wide = lambda x: jnp.broadcast_to(x, (block, 128))
        st_out[chunk, here] = wide(top)
        st_out[3 + chunk, here] = wide(jnp.sum(expo, axis=1, keepdims=True))
        st_out[6 + chunk, here] = wide(jnp.sum(expo * grads, axis=1, keepdims=True))
        return carry

    lax.fori_loop(0, steps, rows, 0)


def forward(chunk, off, n, total_keys, key_parts, bias, state):
    first = chunk == 0
    block = 384 if first else 768
    if first:
        rows = state[0].shape[0] * 16
        side = jax.ShapeDtypeStruct((rows, total_keys), bf16)
        outs = [side, side, jax.ShapeDtypeStruct((total_keys, WIDE), bf16), jax.ShapeDtypeStruct((9, rows, 128), f32)]
    else:
        rows, outs = state[0].shape[0], []
    outs += [jax.ShapeDtypeStruct(a.shape, a.dtype) for a in state]
    start = len(key_parts) + 1
    return call(
        functools.partial(forward_body, len(key_parts), chunk, off, n, block),
        outs,
        (),
        [*key_parts, bias, *state],
        direct_in=(start, start + 1) if first else (),
        scratch=[pltpu.SemaphoreType.DMA((2 * rows // block,))] if first else [],
        alias={} if first else {start + i: i for i in range(len(state))},
        flops=2 * rows * n * (WIDE + LAT),
    )


def backward_body(chunk, offs, n, lead, final, early, step, tile, *refs):
    refs = list(refs)
    qt_ref, gt_ref, e_ref, p_ref, row_ref, k_ref = refs[:6]
    parts, refs = refs[6 : 6 + len(offs)], refs[6 + len(offs) :]
    e_out, p_out, row_out, _, s_out = refs[:5]
    held, sems = refs[-2:]
    rows = qt_ref.shape[1]
    if final:
        kept, sem = refs[5], refs[6]
        save = pltpu.make_async_copy(k_ref, kept, sem.at[0])
        save.start()
    if lead:
        for at in range(0, rows, step):
            here = slice(at, at + step)
            col = lambda c: row_ref[c, here]
            top = jnp.maximum(jnp.maximum(col(0), col(1)), col(2))
            fade = [jnp.exp2((col(c) - top) * EXPC) for c in range(3)]
            total = fade[0] * col(3) + fade[1] * col(4) + fade[2] * col(5)
            rdot = fade[0] * col(6) + fade[1] * col(7) + fade[2] * col(8)
            total = 1.0 / total
            for c in range(3):
                row_out[c, here] = fade[c] * total
            row_out[3, here] = rdot * total
    copies = []
    for ref, off in zip(parts, offs):
        for start in range(0, n, tile):
            cols = slice(off + start, off + start + tile)
            spot = len(copies)
            acc = None
            for at in range(0, rows, step):
                here = slice(at, at + step)
                a = jnp.tile(row_out[chunk, here], (1, tile // 128))
                r = jnp.tile(row_out[3, here], (1, tile // 128))
                weights = (e_ref[here, cols].astype(f32) * a).astype(bf16)
                sg = (weights.astype(f32) * (p_ref[here, cols].astype(f32) - r) * SCALE).astype(bf16)
                e_out[here, cols] = weights
                if at < early:
                    p_out[here, cols] = sg
                else:
                    held[spot, at - early : at - early + step] = sg
                key_part = dot(qt_ref[:, here], sg)
                value_part = dot(gt_ref[:, here], weights)
                if acc is None:
                    acc = [key_part[:LAT] + value_part, key_part[LAT:]]
                else:
                    acc = [acc[0] + (key_part[:LAT] + value_part), acc[1] + key_part[LAT:]]
            copies.append(pltpu.make_async_copy(held.at[spot], s_out.at[spot], sems.at[spot]))
            copies[-1].start()
            ref[start : start + tile, :LAT] = acc[0].T.astype(bf16)
            low = jnp.concatenate([acc[1], jnp.zeros_like(acc[1])], axis=0).T[:, : WIDE - LAT]
            ref[start : start + tile, LAT:] = low.astype(bf16)
    for copy in copies:
        copy.wait()
    if final:
        save.wait()


def backward(chunk, offs, n, early, qt, gt, e, p, row, k, lead=False, final=False, tile=256, step=256):
    rows = e.shape[0]
    count = len(offs)
    like = lambda a: jax.ShapeDtypeStruct(a.shape, a.dtype)
    part = jax.ShapeDtypeStruct((n, WIDE), bf16)
    merged = jax.ShapeDtypeStruct((4, rows, 128), f32) if lead else like(row)
    late = (count * n // tile, rows - early, tile)
    outs = [part] * count + [like(e), like(p), merged, like(k), jax.ShapeDtypeStruct(late, bf16)]
    alias = {2: count, 3: count + 1, 5: count + 3}
    scratch = [pltpu.VMEM(late, bf16), pltpu.SemaphoreType.DMA((late[0],))]
    direct = (count + 4,)
    if not lead:
        alias[4] = count + 2
    if final:
        outs.append(like(k))
        direct = (count + 4, count + 5)
        scratch = [pltpu.SemaphoreType.DMA((1,)), *scratch]
    return call(
        functools.partial(backward_body, chunk, offs, n, lead, final, early, step, tile),
        outs,
        (),
        (qt, gt, e, p, row, k),
        scratch=scratch,
        alias=alias,
        direct=direct,
        flops=2 * rows * n * count * (WIDE + LAT),
    )


def leaving(held, out_ref, sems, block):
    def copy(i):
        part = pl.ds(i * (block // 16), block // 16)
        return pltpu.make_async_copy(held.at[part], out_ref.at[part], sems.at[i])

    return copy


def value_body(block, early, w_ref, s_ref, k_ref, out_ref, q_ref, held, held_q, sems, sems_q):
    steps = out_ref.shape[0] * 16 // block
    leave = leaving(held, out_ref, sems, block)
    small = held_q.shape[0] * 16 // sems_q.shape[0]
    leave_q = leaving(held_q, q_ref, sems_q, small)
    for i in range(early // small):
        here = slice(i * small, i * small + small)
        part = slice(i * (small // 16), (i + 1) * (small // 16))
        held_q[part] = dot(s_ref[here], k_ref[...]).astype(bf16).reshape(small // 16, 16, WIDE)
        leave_q(i).start()

    def rows(i, carry):
        here = pl.ds(pl.multiple_of(i * block, block), block)
        part = pl.ds(i * (block // 16), block // 16)
        held[part] = dot(w_ref[here], k_ref[:, :LAT]).astype(bf16).reshape(block // 16, 16, LAT)
        leave(i).start()
        return carry

    lax.fori_loop(0, steps, rows, 0)
    for i in range(early // small):
        leave_q(i).wait()
    for i in range(steps):
        leave(i).wait()


def value_side(w, s, k, early, block=512):
    rows = w.shape[0]
    shape = (rows // 16, 16, LAT)
    dma = lambda n: pltpu.SemaphoreType.DMA((n,))
    return call(
        functools.partial(value_body, block, early),
        (jax.ShapeDtypeStruct(shape, bf16), jax.ShapeDtypeStruct((rows // 16, 16, WIDE), bf16)),
        (),
        (w, s, k),
        scratch=[
            pltpu.VMEM(shape, bf16),
            pltpu.VMEM((early // 16, 16, WIDE), bf16),
            dma(rows // block),
            dma(early // 256),
        ],
        direct=(0, 1),
        flops=2 * k.shape[0] * (rows * LAT + early * WIDE),
    )


def query_body(offs, early, block, *refs):
    s_refs, (k_ref, _, out_ref, s_v, k_v, held, sems_k, sems_s, sems) = refs[: len(offs)], refs[len(offs) :]
    steps = s_v.shape[1] // block
    load_k = pltpu.make_async_copy(k_ref, k_v, sems_k.at[0])
    load_k.start()
    loads = []
    for i in range(steps):
        here = slice(i * block, i * block + block)
        loads.append(
            [
                pltpu.make_async_copy(ref.at[t, here], s_v.at[spot, here], sems_s.at[i * s_v.shape[0] + spot])
                for ref, spots in zip(s_refs, offs)
                for t, spot in enumerate(spots)
            ]
        )
        for copy in loads[-1]:
            copy.start()
    load_k.wait()
    leave = []
    for i in range(steps):
        for copy in loads[i]:
            copy.wait()
        here = slice(i * block, i * block + block)
        part = slice(i * (block // 16), (i + 1) * (block // 16))
        to = slice(early // 16 + part.start, early // 16 + part.stop)
        sg = jnp.concatenate([s_v[t, here] for t in range(s_v.shape[0])], axis=1)
        held[part] = dot(sg, k_v[...]).astype(bf16).reshape(block // 16, 16, WIDE)
        leave.append(pltpu.make_async_copy(held.at[part], out_ref.at[to], sems.at[i]))
        leave[-1].start()
    for copy in leave:
        copy.wait()


def query_side(sgs, offs, early, k, out, block=256):
    tile, rows = sgs[0].shape[2], sgs[0].shape[1]
    dma = lambda n: pltpu.SemaphoreType.DMA((n,))
    steps, tiles = rows // block, k.shape[0] // tile
    return call(
        functools.partial(query_body, [[off // tile for off in o] for o in offs], early, block),
        (jax.ShapeDtypeStruct(out.shape, bf16),),
        (),
        (*sgs, k, out),
        scratch=[
            pltpu.VMEM((tiles, rows, tile), bf16),
            pltpu.VMEM(k.shape, bf16),
            pltpu.VMEM((rows // 16, 16, WIDE), bf16),
            dma(1),
            dma(steps * tiles),
            dma(steps),
        ],
        direct_in=range(len(sgs) + 2),
        direct=(0,),
        alias={len(sgs) + 1: 0},
        flops=2 * rows * k.shape[0] * WIDE,
    )[0]


def per_device(queries, out_grad, latents, list_blocks, list_counts, valid_tokens):
    me = lax.axis_index("req")
    head = lax.axis_index("head")
    chip, core = head // 2, head % 2
    tokens = latents.shape[1]
    pair_a, pair_b, sibling = [[(h, h ^ d) for h in range(8)] for d in (2, 6, 1)]
    send = lambda a, perm: lax.ppermute(a, "head", perm)
    scalars = (list_blocks, list_counts, me.reshape(1).astype(jnp.int32))

    smem = lambda n: pltpu.SMEM((n,), jnp.int32)
    slots = jax.ShapeDtypeStruct((SLOTS, tokens, WIDE), bf16)
    keys = MAXL * tokens
    share_of = lambda n: jax.ShapeDtypeStruct((n, WIDE), bf16)

    dma = lambda n: pltpu.SemaphoreType.DMA((n,))
    outgoing, owned = call(
        pick_body,
        (slots, jax.ShapeDtypeStruct((SLOTS + 1,), jnp.int32)),
        scalars,
        (latents,),
        scratch=[
            pltpu.VMEM(latents.shape, bf16),
            pltpu.VMEM((SLOTS, tokens, WIDE), bf16),
            dma(1),
            dma(4),
        ],
        direct_in=(0,),
        direct=(0,),
        smem_out=(1,),
    )
    arrived = lax.all_to_all(outgoing.reshape(16, CAP, tokens, WIDE), "req", 0, 0, tiled=True)

    my_blocks = lax.dynamic_index_in_dim(list_blocks, me, 0, keepdims=False)
    my_count = lax.dynamic_index_in_dim(list_counts, me, 0, keepdims=False)
    ids = jnp.arange(valid_tokens.shape[0], dtype=jnp.int32)
    filled = jnp.sum(jnp.where(my_blocks[:, None] == ids[None, :], valid_tokens[None, :], 0), axis=1)
    filled = jnp.where(jnp.arange(MAXL, dtype=jnp.int32) < my_count, filled, 0)
    filled = jnp.repeat(filled, tokens)[None, :]
    offset = jnp.tile(jnp.arange(tokens, dtype=jnp.int32), MAXL)[None, :]
    at = lambda d, c: (chip ^ d) * 2 + c
    other = 1 - core
    places = [at(0, core), at(0, other), at(1, core), at(3, core), at(1, other), at(3, other), at(2, core), at(2, other)]
    first_token = jnp.stack(places)[:, None] * tokens
    bias = jnp.where(first_token + offset < filled, 0.0, BIG).astype(f32)
    bias0, bias1, bias2 = [bias[i:j].reshape(1, -1) for i, j in ((0, 2), (2, 6), (6, 8))]

    arrived, bias0, bias1, bias2 = lax.optimization_barrier((arrived, bias0, bias1, bias2))

    (share,) = call(
        take_body,
        (share_of(keys),),
        scalars,
        (arrived.reshape(slots.shape),),
        scratch=[smem(MAXL), smem(16)],
    )

    after = lambda a, *others: lax.optimization_barrier((a, *others))[0]
    every = 8 * keys
    from_b = send(share, pair_b)
    from_a = send(share, pair_a)
    s0 = send(share, sibling)
    state = forward(0, 0, 2 * keys, every, [share, s0], bias0, (queries, out_grad))
    from_b = after(from_b, state[3])
    from_a = after(from_a, state[3])
    r2 = send(from_b, pair_a)
    sa = send(from_a, sibling)
    sb = send(from_b, sibling)
    state = forward(1, 2 * keys, 4 * keys, every, [from_a, from_b, sa, sb], bias1, state)
    r2 = after(r2, state[3])
    s3 = send(r2, sibling)
    flat = lambda a: jax.ShapeDtypeStruct((a.shape[2], a.shape[0] * a.shape[1]), bf16)
    e, p, k, row, q, g = state
    qt, gt = call(turn_body, (flat(queries), flat(out_grad)), (), (q, after(g, r2)))
    e, p, k, row, q, g = forward(2, 6 * keys, 2 * keys, every, [r2, s3], bias2, (e, p, k, after(row, gt), q, g))

    fold = lambda a: a.reshape(-1, tokens, WIDE)
    unfold = lambda a: a.reshape(-1, WIDE)
    early = 256
    back = functools.partial(backward, early=early, qt=qt, gt=gt)
    far2, e, p, row, k, sg2f = back(2, (7 * keys,), keys, e=e, p=p, row=row, k=k, lead=True)
    mate2 = send(far2, sibling)
    near2, e, p, row, k, sg2n = back(2, (6 * keys,), keys, e=e, p=p, row=row, k=k)
    far0, e, p, row, k, sg0f = back(0, (keys,), keys, e=e, p=p, row=row, k=k)
    (two,) = call(two_body, (share_of(keys),), (), (after(near2, far0), mate2))
    got_two = send(two, pair_b)
    far1, e, p, row, k, sg1f, k_saved = back(1, (4 * keys,), 2 * keys, e=e, p=p, row=after(row, two), k=k, final=True)
    mate1 = unfold(send(fold(far1), sibling))
    near1, e, p, row, k, sg1n = back(1, (2 * keys,), 2 * keys, e=e, p=p, row=row, k=k)
    mate0 = send(far0, sibling)
    (to_b,) = call(wrap_body, (share_of(keys),), (), (near1, mate1))
    got_b = send(to_b, pair_b)
    (to_a,) = call(next_body, (share_of(keys),), (), (after(near1, to_b), mate1, got_two))
    got_a = send(to_a, pair_a)
    near0, e, p, row, k, sg0n = back(0, (0,), keys, e=e, p=p, row=after(row, to_a), k=k)
    attended, query_grad = value_side(e, p, after(k, to_a), early)
    near0 = after(near0, attended)
    (slot_grads,) = call(
        put_body,
        (slots,),
        scalars,
        (near0, mate0, got_a, got_b),
        scratch=[smem(MAXL), smem(16), pltpu.VMEM((keys, WIDE), bf16), dma(MAXL)],
        direct=(0,),
    )
    k_saved = after(k_saved, slot_grads)
    query_grad = query_side(
        (sg2f, sg2n, sg0f, sg0n, sg1f, sg1n),
        ((7 * keys,), (6 * keys,), (keys,), (0,), (4 * keys, 5 * keys), (2 * keys, 3 * keys)),
        early,
        k_saved,
        query_grad,
    )
    returned = lax.all_to_all(slot_grads.reshape(16, CAP, tokens, WIDE), "req", 0, 0, tiled=True)
    (latent_grad,) = call(
        gather_body,
        (jax.ShapeDtypeStruct((16, tokens, WIDE), f32),),
        (owned,),
        (returned.reshape(slots.shape),),
        scratch=[pltpu.VMEM((17, tokens, WIDE), f32), dma(4)],
        direct=(0,),
    )
    return (attended, query_grad, latent_grad)


def solution(mesh):
    in_specs = (
        P("req", "head", None),
        P("req", "head", None),
        P("req", "head", None),
        P(),
        P(),
        P(),
    )
    out_specs = (P("req", "head", None), P("req", "head", None), P("req", "head", None))
    return jax.shard_map(per_device, mesh=mesh, in_specs=in_specs, out_specs=out_specs, check_vma=False)
```

```python
import functools
import math

import jax
import jax.numpy as jnp
from jax import lax
from jax.experimental import pallas as pl
from jax.experimental.pallas import tpu as pltpu
from jax.sharding import PartitionSpec as P


LAT = 512
WIDE = 576
MAXL = 16
CAP = 2
BIG = -1e30
SLOTS = 16 * CAP
SCALE = 192.0 ** (-0.5)
EXPC = SCALE * math.log2(math.e)
NT = (((1,), (1,)), ((), ()))
NN = (((1,), (0,)), ((), ()))
f32 = jnp.float32
bf16 = jnp.bfloat16


def dot(a, b, dims=NN):
    return lax.dot_general(a, b, dims, preferred_element_type=f32)


def owner_table(lists, counts, own, table, empty):
    def group(g, carry):
        table[g * CAP] = empty
        table[g * CAP + 1] = empty
        rank = jnp.int32(0)
        for j in range(MAXL):
            block = lists[g, j]
            mine = ((block >> 4) == own) & (j < counts[g])
            table[jnp.where(mine, g * CAP + rank, SLOTS)] = block & 15
            rank = jnp.where(mine, jnp.minimum(rank + 1, CAP - 1), rank)
        return carry

    lax.fori_loop(0, 16, group, 0)


def slot_table(lists, own, table, seen):
    for o in range(16):
        seen[o] = 0
    for j in range(MAXL):
        owner = lists[own, j] >> 4
        rank = seen[owner]
        seen[owner] = jnp.minimum(rank + 1, CAP - 1)
        table[j] = owner * CAP + rank


def pick_body(lists, counts, me, lat_ref, out_ref, table, lat, held, sem, sems):
    load = pltpu.make_async_copy(lat_ref, lat, sem.at[0])
    load.start()
    owner_table(lists, counts, me[0], table, 16)
    load.wait()
    step = SLOTS // 4
    parts = [slice(i * step, i * step + step) for i in range(4)]
    copies = [pltpu.make_async_copy(held.at[p], out_ref.at[p], sems.at[i]) for i, p in enumerate(parts)]
    for i, copy in enumerate(copies):
        for s in range(i * step, i * step + step):
            held[s] = lat[table[s] & 15]
        copy.start()
    for copy in copies:
        copy.wait()


def gather_body(table, arrived_ref, out_ref, total, sems):
    total[...] = jnp.zeros(total.shape, total.dtype)
    for s in range(SLOTS):
        total[table[s]] = total[table[s]] + arrived_ref[s].astype(f32)
    parts = [slice(i * 4, i * 4 + 4) for i in range(4)]
    copies = [pltpu.make_async_copy(total.at[p], out_ref.at[p], sems.at[i]) for i, p in enumerate(parts)]
    for copy in copies:
        copy.start()
    for copy in copies:
        copy.wait()


def take_body(lists, counts, me, arrived_ref, out_ref, table, seen):
    slot_table(lists, me[0], table, seen)
    count = counts[me[0]]
    for j in range(MAXL):
        live = j < count

        @pl.when(live)
        def _():
            out_ref[j * 16 : j * 16 + 16] = arrived_ref[table[j]]

        @pl.when(jnp.logical_not(live))
        def _():
            out_ref[j * 16 : j * 16 + 16] = jnp.zeros((16, WIDE), bf16)


def put_body(lists, counts, me, a_ref, b_ref, c_ref, d_ref, out_ref, table, seen, held, sems):
    slot_table(lists, me[0], table, seen)
    count = counts[me[0]]

    def copy(j):
        return pltpu.make_async_copy(held.at[j * 16 : j * 16 + 16], out_ref.at[table[j]], sems.at[j])

    for j in range(MAXL):
        here = slice(j * 16, j * 16 + 16)
        total = a_ref[here].astype(f32) + b_ref[here].astype(f32)
        total = total + (c_ref[here].astype(f32) + d_ref[here].astype(f32))
        held[here] = total.astype(bf16)

        @pl.when(j < count)
        def _():
            copy(j).start()

    for j in range(MAXL):

        @pl.when(j < count)
        def _():
            copy(j).wait()


def turn_body(q_ref, g_ref, qt_ref, gt_ref):
    rows = qt_ref.shape[1]
    for at in range(0, rows, 256):
        here = slice(at, at + 256)
        part = slice(at // 16, at // 16 + 16)
        q = q_ref[part].reshape(256, WIDE)
        qt_ref[:LAT, here] = q[:, :LAT].T
        rope = jnp.concatenate([q[:, LAT:], q[:, LAT:]], axis=1)
        qt_ref[LAT:, here] = rope.T[: WIDE - LAT]
        gt_ref[:, here] = g_ref[part].reshape(256, LAT).T


def two_body(near_ref, far_ref, low_ref, high_ref):
    half = low_ref.shape[0]
    total = near_ref[...].astype(f32) + far_ref[...].astype(f32)
    low_ref[...] = total[:half].astype(bf16)
    high_ref[...] = total[half:].astype(bf16)


def wrap_body(near_ref, far_ref, low_ref, out_ref):
    size, half = out_ref.shape[0], low_ref.shape[0]
    total = near_ref[size:].astype(f32) + far_ref[size:].astype(f32)
    out_ref[:half] = (total[:half] + low_ref[...].astype(f32)).astype(bf16)
    out_ref[half:] = total[half:].astype(bf16)


def next_body(near_ref, far_ref, high_ref, out_ref):
    size, half = out_ref.shape[0], high_ref.shape[0]
    total = near_ref[:size].astype(f32) + far_ref[:size].astype(f32)
    out_ref[:half] = total[:half].astype(bf16)
    out_ref[half:] = (total[half:] + high_ref[...].astype(f32)).astype(bf16)


ONCHIP = pl.BlockSpec(memory_space=pltpu.VMEM)
INPLACE = pl.BlockSpec(memory_space=pltpu.HBM)


def call(body, outs, scalars, arrays, scratch=(), direct_in=(), direct=(), alias=None, flops=None, smem_out=()):
    args = [
        pltpu.with_memory_space_constraint(a, pltpu.HBM if i in direct_in else pltpu.VMEM)
        for i, a in enumerate(arrays)
    ]
    scalars = [pltpu.with_memory_space_constraint(a, pltpu.HBM) for a in scalars]
    shapes = [
        (pltpu.HBM if i in direct or i in smem_out else pltpu.VMEM)(o.shape, o.dtype) for i, o in enumerate(outs)
    ]
    small = pl.BlockSpec(memory_space=pltpu.SMEM)
    return pl.pallas_call(
        body,
        in_specs=[small] * len(scalars)
        + [INPLACE if i in direct_in else ONCHIP for i in range(len(arrays))],
        out_specs=tuple(small if i in smem_out else INPLACE if i in direct else ONCHIP for i in range(len(outs))),
        out_shape=tuple(shapes),
        scratch_shapes=list(scratch),
        input_output_aliases=alias or {},
        cost_estimate=flops and pl.CostEstimate(flops=flops, transcendentals=0, bytes_accessed=0),
        compiler_params=pltpu.CompilerParams(vmem_limit_bytes=16 * 1024 * 1024),
    )(*scalars, *args)


def forward_body(nkeys, chunk, off, n, block, *refs):
    refs = list(refs)
    first = chunk == 0
    key_refs, bias, refs = refs[:nkeys], refs[nkeys], refs[nkeys + 1 :]
    if first:
        (q_in, g_in), refs = refs[:2], refs[2:]
        sems, refs = refs[-1], refs[:-1]
    else:
        refs = refs[len(refs) // 2 :]
    e_out, p_out, k_out, st_out, q_ref, g_ref = refs
    steps = q_ref.shape[0] * 16 // block

    def loads(i):
        part = pl.ds(i * (block // 16), block // 16)
        return (
            pltpu.make_async_copy(q_in.at[part], q_ref.at[part], sems.at[2 * i]),
            pltpu.make_async_copy(g_in.at[part], g_ref.at[part], sems.at[2 * i + 1]),
        )

    if first:
        for i in range(steps):
            for copy in loads(i):
                copy.start()
    at = off
    for ref in key_refs:
        k_out[at : at + ref.shape[0]] = ref[...]
        at += ref.shape[0]
    mine = slice(off, off + n)

    def rows(i, carry):
        here = pl.ds(pl.multiple_of(i * block, block), block)
        part = pl.ds(i * (block // 16), block // 16)
        if first:
            for copy in loads(i):
                copy.wait()
        scores = dot(q_ref[part].reshape(block, WIDE), k_out[mine], NT) + bias[...]
        top = jnp.max(scores, axis=1, keepdims=True)
        expo = jnp.exp2((scores - top) * EXPC)
        grads = dot(g_ref[part].reshape(block, LAT), k_out[mine, :LAT], NT)
        e_out[here, mine] = expo.astype(bf16)
        p_out[here, mine] = grads.astype(bf16)
        wide = lambda x: jnp.broadcast_to(x, (block, 128))
        st_out[chunk, here] = wide(top)
        st_out[3 + chunk, here] = wide(jnp.sum(expo, axis=1, keepdims=True))
        st_out[6 + chunk, here] = wide(jnp.sum(expo * grads, axis=1, keepdims=True))
        return carry

    lax.fori_loop(0, steps, rows, 0)


def forward(chunk, off, n, total_keys, key_parts, bias, state):
    first = chunk == 0
    block = 384 if first else 768
    if first:
        rows = state[0].shape[0] * 16
        side = jax.ShapeDtypeStruct((rows, total_keys), bf16)
        outs = [side, side, jax.ShapeDtypeStruct((total_keys, WIDE), bf16), jax.ShapeDtypeStruct((9, rows, 128), f32)]
    else:
        rows, outs = state[0].shape[0], []
    outs += [jax.ShapeDtypeStruct(a.shape, a.dtype) for a in state]
    start = len(key_parts) + 1
    return call(
        functools.partial(forward_body, len(key_parts), chunk, off, n, block),
        outs,
        (),
        [*key_parts, bias, *state],
        direct_in=(start, start + 1) if first else (),
        scratch=[pltpu.SemaphoreType.DMA((2 * rows // block,))] if first else [],
        alias={} if first else {start + i: i for i in range(len(state))},
        flops=2 * rows * n * (WIDE + LAT),
    )


def backward_body(chunk, offs, n, lead, final, early, step, tile, *refs):
    refs = list(refs)
    qt_ref, gt_ref, e_ref, p_ref, row_ref, k_ref = refs[:6]
    parts, refs = refs[6 : 6 + len(offs)], refs[6 + len(offs) :]
    e_out, p_out, row_out, _, s_out = refs[:5]
    held, sems = refs[-2:]
    rows = qt_ref.shape[1]
    if final:
        kept, sem = refs[5], refs[6]
        save = pltpu.make_async_copy(k_ref, kept, sem.at[0])
        save.start()
    if lead:
        for at in range(0, rows, step):
            here = slice(at, at + step)
            col = lambda c: row_ref[c, here]
            top = jnp.maximum(jnp.maximum(col(0), col(1)), col(2))
            fade = [jnp.exp2((col(c) - top) * EXPC) for c in range(3)]
            total = fade[0] * col(3) + fade[1] * col(4) + fade[2] * col(5)
            rdot = fade[0] * col(6) + fade[1] * col(7) + fade[2] * col(8)
            total = 1.0 / total
            for c in range(3):
                row_out[c, here] = fade[c] * total
            row_out[3, here] = rdot * total
    copies = []
    for ref, off in zip(parts, offs):
        for start in range(0, n, tile):
            cols = slice(off + start, off + start + tile)
            spot = len(copies)
            acc = None
            for at in range(0, rows, step):
                here = slice(at, at + step)
                a = jnp.tile(row_out[chunk, here], (1, tile // 128))
                r = jnp.tile(row_out[3, here], (1, tile // 128))
                weights = (e_ref[here, cols].astype(f32) * a).astype(bf16)
                sg = (weights.astype(f32) * (p_ref[here, cols].astype(f32) - r) * SCALE).astype(bf16)
                e_out[here, cols] = weights
                if at < early:
                    p_out[here, cols] = sg
                else:
                    held[spot, at - early : at - early + step] = sg
                key_part = dot(qt_ref[:, here], sg)
                value_part = dot(gt_ref[:, here], weights)
                if acc is None:
                    acc = [key_part[:LAT] + value_part, key_part[LAT:]]
                else:
                    acc = [acc[0] + (key_part[:LAT] + value_part), acc[1] + key_part[LAT:]]
            copies.append(pltpu.make_async_copy(held.at[spot], s_out.at[spot], sems.at[spot]))
            copies[-1].start()
            ref[start : start + tile, :LAT] = acc[0].T.astype(bf16)
            low = jnp.concatenate([acc[1], jnp.zeros_like(acc[1])], axis=0).T[:, : WIDE - LAT]
            ref[start : start + tile, LAT:] = low.astype(bf16)
    for copy in copies:
        copy.wait()
    if final:
        save.wait()


def backward(chunk, offs, n, early, qt, gt, e, p, row, k, lead=False, final=False, tile=256, step=256):
    rows = e.shape[0]
    count = len(offs)
    like = lambda a: jax.ShapeDtypeStruct(a.shape, a.dtype)
    part = jax.ShapeDtypeStruct((n, WIDE), bf16)
    merged = jax.ShapeDtypeStruct((4, rows, 128), f32) if lead else like(row)
    late = (count * n // tile, rows - early, tile)
    outs = [part] * count + [like(e), like(p), merged, like(k), jax.ShapeDtypeStruct(late, bf16)]
    alias = {2: count, 3: count + 1, 5: count + 3}
    scratch = [pltpu.VMEM(late, bf16), pltpu.SemaphoreType.DMA((late[0],))]
    direct = (count + 4,)
    if not lead:
        alias[4] = count + 2
    if final:
        outs.append(like(k))
        direct = (count + 4, count + 5)
        scratch = [pltpu.SemaphoreType.DMA((1,)), *scratch]
    return call(
        functools.partial(backward_body, chunk, offs, n, lead, final, early, step, tile),
        outs,
        (),
        (qt, gt, e, p, row, k),
        scratch=scratch,
        alias=alias,
        direct=direct,
        flops=2 * rows * n * count * (WIDE + LAT),
    )


def leaving(held, out_ref, sems, block):
    def copy(i):
        part = pl.ds(i * (block // 16), block // 16)
        return pltpu.make_async_copy(held.at[part], out_ref.at[part], sems.at[i])

    return copy


def value_body(block, early, w_ref, s_ref, k_ref, out_ref, q_ref, held, held_q, sems, sems_q):
    steps = out_ref.shape[0] * 16 // block
    leave = leaving(held, out_ref, sems, block)
    small = held_q.shape[0] * 16 // sems_q.shape[0]
    leave_q = leaving(held_q, q_ref, sems_q, small)
    for i in range(early // small):
        here = slice(i * small, i * small + small)
        part = slice(i * (small // 16), (i + 1) * (small // 16))
        held_q[part] = dot(s_ref[here], k_ref[...]).astype(bf16).reshape(small // 16, 16, WIDE)
        leave_q(i).start()

    def rows(i, carry):
        here = pl.ds(pl.multiple_of(i * block, block), block)
        part = pl.ds(i * (block // 16), block // 16)
        held[part] = dot(w_ref[here], k_ref[:, :LAT]).astype(bf16).reshape(block // 16, 16, LAT)
        leave(i).start()
        return carry

    lax.fori_loop(0, steps, rows, 0)
    for i in range(early // small):
        leave_q(i).wait()
    for i in range(steps):
        leave(i).wait()


def value_side(w, s, k, early, block=512):
    rows = w.shape[0]
    shape = (rows // 16, 16, LAT)
    dma = lambda n: pltpu.SemaphoreType.DMA((n,))
    return call(
        functools.partial(value_body, block, early),
        (jax.ShapeDtypeStruct(shape, bf16), jax.ShapeDtypeStruct((rows // 16, 16, WIDE), bf16)),
        (),
        (w, s, k),
        scratch=[
            pltpu.VMEM(shape, bf16),
            pltpu.VMEM((early // 16, 16, WIDE), bf16),
            dma(rows // block),
            dma(early // 256),
        ],
        direct=(0, 1),
        flops=2 * k.shape[0] * (rows * LAT + early * WIDE),
    )


def query_body(offs, early, block, *refs):
    s_refs, (k_ref, _, out_ref, s_v, k_v, held, sems_k, sems_s, sems) = refs[: len(offs)], refs[len(offs) :]
    steps = s_v.shape[1] // block
    load_k = pltpu.make_async_copy(k_ref, k_v, sems_k.at[0])
    load_k.start()
    loads = []
    for i in range(steps):
        here = slice(i * block, i * block + block)
        loads.append(
            [
                pltpu.make_async_copy(ref.at[t, here], s_v.at[spot, here], sems_s.at[i * s_v.shape[0] + spot])
                for ref, spots in zip(s_refs, offs)
                for t, spot in enumerate(spots)
            ]
        )
        for copy in loads[-1]:
            copy.start()
    load_k.wait()
    leave = []
    for i in range(steps):
        for copy in loads[i]:
            copy.wait()
        here = slice(i * block, i * block + block)
        part = slice(i * (block // 16), (i + 1) * (block // 16))
        to = slice(early // 16 + part.start, early // 16 + part.stop)
        sg = jnp.concatenate([s_v[t, here] for t in range(s_v.shape[0])], axis=1)
        held[part] = dot(sg, k_v[...]).astype(bf16).reshape(block // 16, 16, WIDE)
        leave.append(pltpu.make_async_copy(held.at[part], out_ref.at[to], sems.at[i]))
        leave[-1].start()
    for copy in leave:
        copy.wait()


def query_side(sgs, offs, early, k, out, block=256):
    tile, rows = sgs[0].shape[2], sgs[0].shape[1]
    dma = lambda n: pltpu.SemaphoreType.DMA((n,))
    steps, tiles = rows // block, k.shape[0] // tile
    return call(
        functools.partial(query_body, [[off // tile for off in o] for o in offs], early, block),
        (jax.ShapeDtypeStruct(out.shape, bf16),),
        (),
        (*sgs, k, out),
        scratch=[
            pltpu.VMEM((tiles, rows, tile), bf16),
            pltpu.VMEM(k.shape, bf16),
            pltpu.VMEM((rows // 16, 16, WIDE), bf16),
            dma(1),
            dma(steps * tiles),
            dma(steps),
        ],
        direct_in=range(len(sgs) + 2),
        direct=(0,),
        alias={len(sgs) + 1: 0},
        flops=2 * rows * k.shape[0] * WIDE,
    )[0]


def per_device(queries, out_grad, latents, list_blocks, list_counts, valid_tokens):
    me = lax.axis_index("req")
    head = lax.axis_index("head")
    chip, core = head // 2, head % 2
    tokens = latents.shape[1]
    pair_a, pair_b, sibling = [[(h, h ^ d) for h in range(8)] for d in (2, 6, 1)]
    send = lambda a, perm: lax.ppermute(a, "head", perm)
    scalars = (list_blocks, list_counts, me.reshape(1).astype(jnp.int32))

    smem = lambda n: pltpu.SMEM((n,), jnp.int32)
    slots = jax.ShapeDtypeStruct((SLOTS, tokens, WIDE), bf16)
    keys = MAXL * tokens
    share_of = lambda n: jax.ShapeDtypeStruct((n, WIDE), bf16)

    dma = lambda n: pltpu.SemaphoreType.DMA((n,))
    outgoing, owned = call(
        pick_body,
        (slots, jax.ShapeDtypeStruct((SLOTS + 1,), jnp.int32)),
        scalars,
        (latents,),
        scratch=[
            pltpu.VMEM(latents.shape, bf16),
            pltpu.VMEM((SLOTS, tokens, WIDE), bf16),
            dma(1),
            dma(4),
        ],
        direct_in=(0,),
        direct=(0,),
        smem_out=(1,),
    )
    arrived = lax.all_to_all(outgoing.reshape(16, CAP, tokens, WIDE), "req", 0, 0, tiled=True)

    my_blocks = lax.dynamic_index_in_dim(list_blocks, me, 0, keepdims=False)
    my_count = lax.dynamic_index_in_dim(list_counts, me, 0, keepdims=False)
    ids = jnp.arange(valid_tokens.shape[0], dtype=jnp.int32)
    filled = jnp.sum(jnp.where(my_blocks[:, None] == ids[None, :], valid_tokens[None, :], 0), axis=1)
    filled = jnp.where(jnp.arange(MAXL, dtype=jnp.int32) < my_count, filled, 0)
    filled = jnp.repeat(filled, tokens)[None, :]
    offset = jnp.tile(jnp.arange(tokens, dtype=jnp.int32), MAXL)[None, :]
    at = lambda d, c: (chip ^ d) * 2 + c
    other = 1 - core
    places = [at(0, core), at(0, other), at(1, core), at(3, core), at(1, other), at(3, other), at(2, core), at(2, other)]
    first_token = jnp.stack(places)[:, None] * tokens
    bias = jnp.where(first_token + offset < filled, 0.0, BIG).astype(f32)
    bias0, bias1, bias2 = [bias[i:j].reshape(1, -1) for i, j in ((0, 2), (2, 6), (6, 8))]

    arrived, bias0, bias1, bias2 = lax.optimization_barrier((arrived, bias0, bias1, bias2))

    (share,) = call(
        take_body,
        (share_of(keys),),
        scalars,
        (arrived.reshape(slots.shape),),
        scratch=[smem(MAXL), smem(16)],
    )

    after = lambda a, *others: lax.optimization_barrier((a, *others))[0]
    every = 8 * keys
    from_b = send(share, pair_b)
    from_a = send(share, pair_a)
    s0 = send(share, sibling)
    state = forward(0, 0, 2 * keys, every, [share, s0], bias0, (queries, out_grad))
    from_b = after(from_b, state[3])
    from_a = after(from_a, state[3])
    r2 = send(from_b, pair_a)
    sa = send(from_a, sibling)
    sb = send(from_b, sibling)
    state = forward(1, 2 * keys, 4 * keys, every, [from_a, from_b, sa, sb], bias1, state)
    r2 = after(r2, state[3])
    s3 = send(r2, sibling)
    flat = lambda a: jax.ShapeDtypeStruct((a.shape[2], a.shape[0] * a.shape[1]), bf16)
    e, p, k, row, q, g = state
    qt, gt = call(turn_body, (flat(queries), flat(out_grad)), (), (q, after(g, r2)))
    e, p, k, row, q, g = forward(2, 6 * keys, 2 * keys, every, [r2, s3], bias2, (e, p, k, after(row, gt), q, g))

    fold = lambda a: a.reshape(-1, tokens, WIDE)
    unfold = lambda a: a.reshape(-1, WIDE)
    early = 256
    back = functools.partial(backward, early=early, qt=qt, gt=gt)
    far2, e, p, row, k, sg2f = back(2, (7 * keys,), keys, e=e, p=p, row=row, k=k, lead=True)
    mate2 = send(far2, sibling)
    near2, e, p, row, k, sg2n = back(2, (6 * keys,), keys, e=e, p=p, row=row, k=k)
    far0, e, p, row, k, sg0f = back(0, (keys,), keys, e=e, p=p, row=row, k=k)
    low, high = call(two_body, (share_of(keys // 2),) * 2, (), (after(near2, far0), mate2))
    got_high = send(high, pair_b)
    got_low = send(low, pair_a)
    far1, e, p, row, k, sg1f, k_saved = back(1, (4 * keys,), 2 * keys, e=e, p=p, row=after(row, low), k=k, final=True)
    mate1 = unfold(send(fold(far1), sibling))
    near1, e, p, row, k, sg1n = back(1, (2 * keys,), 2 * keys, e=e, p=p, row=row, k=k)
    mate0 = send(far0, sibling)
    (to_b,) = call(wrap_body, (share_of(keys),), (), (near1, mate1, got_low))
    got_b = send(to_b, pair_b)
    (to_a,) = call(next_body, (share_of(keys),), (), (after(near1, to_b), mate1, got_high))
    got_a = send(to_a, pair_a)
    near0, e, p, row, k, sg0n = back(0, (0,), keys, e=e, p=p, row=after(row, to_a), k=k)
    attended, query_grad = value_side(e, p, after(k, to_a), early)
    near0 = after(near0, attended)
    (slot_grads,) = call(
        put_body,
        (slots,),
        scalars,
        (near0, mate0, got_a, got_b),
        scratch=[smem(MAXL), smem(16), pltpu.VMEM((keys, WIDE), bf16), dma(MAXL)],
        direct=(0,),
    )
    k_saved = after(k_saved, slot_grads)
    query_grad = query_side(
        (sg2f, sg2n, sg0f, sg0n, sg1f, sg1n),
        ((7 * keys,), (6 * keys,), (keys,), (0,), (4 * keys, 5 * keys), (2 * keys, 3 * keys)),
        early,
        k_saved,
        query_grad,
    )
    returned = lax.all_to_all(slot_grads.reshape(16, CAP, tokens, WIDE), "req", 0, 0, tiled=True)
    (latent_grad,) = call(
        gather_body,
        (jax.ShapeDtypeStruct((16, tokens, WIDE), f32),),
        (owned,),
        (returned.reshape(slots.shape),),
        scratch=[pltpu.VMEM((17, tokens, WIDE), f32), dma(4)],
        direct=(0,),
    )
    return (attended, query_grad, latent_grad)


def solution(mesh):
    in_specs = (
        P("req", "head", None),
        P("req", "head", None),
        P("req", "head", None),
        P(),
        P(),
        P(),
    )
    out_specs = (P("req", "head", None), P("req", "head", None), P("req", "head", None))
    return jax.shard_map(per_device, mesh=mesh, in_specs=in_specs, out_specs=out_specs, check_vma=False)
```
